32 devices in a mesh: groups: 2 (over y), seq: 8 (over z, x), head: 2 (over core).
Axes of the slice: x: 2, y: 2, z: 4, core: 2. Of those that a mesh axis runs over, the one named last changes fastest.
Arguments:
- queries: bfloat16 [8192, 2560], P(('groups', 'seq'), 'head'), parts along dimension 0, may hold values from -52 to 52
- keys: bfloat16 [8192, 512], P(('groups', 'seq'), 'head'), parts along dimension 0, may hold values from -4 to 4
- values: bfloat16 [8192, 512], P(('groups', 'seq'), 'head'), parts along dimension 0, may hold values from -4 to 4
- dest_shard: int32 [8192], P(('groups', 'seq')), parts along dimension 0, may hold values from 0 to 7, as said below
- dest_slot: int32 [8192], P(('groups', 'seq')), parts along dimension 0, may hold values from 0 to 511, as said below
- ancestors: int32 [64, 4], P(('groups', 'seq')), parts along dimension 0, may hold values from 0 to 31, as said below
Outputs:
- attended: bfloat16 [8192, 2560], P(('groups', 'seq'), 'head'), parts along dimension 0
The draws below stay inside these ranges and needn't reach their ends.
There are 2 independent parts, one for each index of `groups`. The reference program is written for one: setup_inputs(seed, part) draws one part's arguments, and reference() takes and returns one part's arrays. A program takes and returns all parts, laid end to end along the dimension named above; each array names one. Nothing has to cross between parts.
Inputs may be any that keep to these rules, and one draw needn't show every extreme that they name: `dest_shard`: each shard sends 0, 64 or 128 of its rows to each shard, 128 to some, and every shard receives 512 rows in all. `dest_slot`: with dest_shard, a one-to-one map of the rows of a slab onto the balanced rows. `ancestors`: each entry of block b's list is a block from max(0, b - 4) to b; the first is its parent in its rollout tree, each further one the parent of the one before; b itself marks an unused entry; repeats may occur.
All inputs are finite; a program needn't handle non-finite values.
Results may differ from the reference program's by a relative error of at most 0.0048.
Values may be sent and summed in bfloat16 or wider, within the bound.
No kernel may reach another device: no remote copies, remote signals or barrier semaphores. Data moves between devices by JAX's collectives and lax.ppermute only.
A program may use at most 64 MiB of HBM per device.

```python
import math
import jax
import jax.numpy as jnp
from jax import lax

QUERY_HEADS = 20
KEY_VALUE_HEADS = 4
HEAD_SIZE = 128
BLK = 128
TOK_DEV = 512
SLAB_TOKENS = 4096
BPD = 4
NBLK = 32
ANC = 4
N_SEQ = 8


def routing(key):
    base = jax.random.fold_in(key, 7)
    shards = SLAB_TOKENS // TOK_DEV
    pair = TOK_DEV // shards
    order_ids = jnp.arange(shards, dtype=jnp.int32)
    perm = jax.random.permutation(jax.random.fold_in(base, 1), shards)
    plus = (perm[:, None] == order_ids[None, :]).astype(jnp.int32)
    minus = (jnp.roll(perm, -1)[:, None] == order_ids[None, :]).astype(jnp.int32)
    counts = pair * (1 + plus - minus)

    def expand(count_row, sub_block):
        targets = jnp.repeat(order_ids, count_row, total_repeat_length=TOK_DEV)
        return jax.random.permutation(sub_block, targets)
    subs = jax.random.split(jax.random.fold_in(base, 2), shards)
    shard_of = jax.vmap(expand)(counts, subs).reshape(-1).astype(jnp.int32)
    order = jnp.argsort(shard_of, stable=True)
    sorted_shard = shard_of[order]
    rank_sorted = jnp.arange(SLAB_TOKENS, dtype=jnp.int32) - sorted_shard * TOK_DEV
    slot_subs = jax.random.split(jax.random.fold_in(base, 3), shards)
    slot_perms = jax.vmap(lambda sub_block: jax.random.permutation(sub_block, TOK_DEV))(slot_subs).astype(jnp.int32)
    slot_sorted = slot_perms[sorted_shard, rank_sorted]
    slot_of = jnp.zeros((SLAB_TOKENS,), jnp.int32).at[order].set(slot_sorted)
    return (shard_of, slot_of)


def draw_dest_shard(key, part):
    return routing(key)[0]


def draw_dest_slot(key, part):
    return routing(key)[1]


def draw_ancestors(key, part):
    base = jax.random.fold_in(key, 13)
    blocks = jnp.arange(NBLK, dtype=jnp.int32)
    lowest = jnp.maximum(blocks - BPD, 0)
    span = jnp.maximum(blocks - lowest, 1)
    draws = jax.random.randint(base, (NBLK,), 0, 1 << 20).astype(jnp.int32)
    parent = jnp.where(blocks > 0, lowest + draws % span, 0).astype(jnp.int32)
    entries = []
    current = blocks
    for step in range(ANC):
        current = parent[current]
        entries.append(jnp.where(current >= blocks - BPD, current, blocks))
    return jnp.stack(entries, axis=1).astype(jnp.int32)


def key_field(key):
    sub_block = jax.random.fold_in(key, 21)
    return jnp.clip(jax.random.normal(sub_block, (SLAB_TOKENS, KEY_VALUE_HEADS * HEAD_SIZE), jnp.float32), -4.0, 4.0)


def draw_keys(key, part):
    return key_field(key).astype(jnp.bfloat16)


def draw_queries(key, part):
    base = jax.random.fold_in(key, 23)
    result = jnp.clip(jax.random.normal(base, (SLAB_TOKENS, QUERY_HEADS * HEAD_SIZE), jnp.float32), -4.0, 4.0)
    return result.astype(jnp.bfloat16)


def steps_of(own_key, extent, cuts, smallest, largest):
    def one(position, parts):
        steps = jax.random.uniform(jax.random.fold_in(jax.random.fold_in(own_key, 6), position), (parts,), jnp.float32, smallest / len(cuts), largest / len(cuts))
        return jnp.repeat(jnp.exp(steps), extent[position] // parts).reshape((-1,) + (1,) * (len(extent) - position - 1))

    level = one(*cuts[0])
    for cut in cuts[1:]:
        level = level * one(*cut)
    return level


def normal_values(rng, shape, deviation, limit, cuts=(), kind=jnp.bfloat16):
    values = deviation * jax.random.normal(rng, shape, jnp.float32)
    if cuts:
        values = values * steps_of(rng, shape, cuts, -0.22, 0.18)
    return jnp.clip(values, -limit, limit).astype(kind)


def setup_inputs(seed: int = 0, part: int = 0) -> dict:
    splits = jax.random.split(jax.random.key(seed), 7)
    part_keys = jax.random.split(jax.random.fold_in(splits[6], part), 7)
    queries = draw_queries(jax.random.fold_in(jax.random.fold_in(splits[6], part), 71), part)
    keys = draw_keys(jax.random.fold_in(jax.random.fold_in(splits[6], part), 71), part)
    values = normal_values(part_keys[2], (SLAB_TOKENS, KEY_VALUE_HEADS * HEAD_SIZE), 1.0, 4.0, ((0, 8), (1, 2)))
    dest_shard = draw_dest_shard(jax.random.fold_in(jax.random.fold_in(splits[6], part), 71), part)
    dest_slot = draw_dest_slot(jax.random.fold_in(jax.random.fold_in(splits[6], part), 71), part)
    ancestors = draw_ancestors(jax.random.fold_in(jax.random.fold_in(splits[6], part), 71), part)
    return {"queries": queries, "keys": keys, "values": values, "dest_shard": dest_shard, "dest_slot": dest_slot, "ancestors": ancestors}


def make_visible(anc_rows, shard):
    block_count = anc_rows.shape[0]
    query_blocks = shard * block_count + jnp.arange(block_count, dtype=jnp.int32)
    key_blocks = shard * block_count - block_count + jnp.arange(2 * block_count, dtype=jnp.int32)
    listed = jnp.any(anc_rows[:, :, None] == key_blocks[None, None, :], axis=1)
    earlier = listed & (key_blocks[None, :] < query_blocks[:, None])
    itself = key_blocks[None, :] == query_blocks[:, None]
    earlier_rows = jnp.repeat(jnp.repeat(earlier, BLK, axis=0), BLK, axis=1)
    itself_rows = jnp.repeat(jnp.repeat(itself, BLK, axis=0), BLK, axis=1)
    count = block_count * BLK
    query_pos = jnp.arange(count, dtype=jnp.int32)[:, None]
    key_pos = jnp.arange(2 * count, dtype=jnp.int32)[None, :] - count
    return earlier_rows | itself_rows & (key_pos <= query_pos)

def attend(query_rows, key_rows, value_rows, visible):
    q_heads = query_rows.shape[1] // HEAD_SIZE
    ratio = q_heads // (key_rows.shape[1] // HEAD_SIZE)
    scale = 1.0 / math.sqrt(HEAD_SIZE)

    def one_head(head, result):
        group = head // ratio
        query_part = lax.dynamic_slice_in_dim(query_rows, head * HEAD_SIZE, HEAD_SIZE, 1).astype(jnp.float32)
        key_part = lax.dynamic_slice_in_dim(key_rows, group * HEAD_SIZE, HEAD_SIZE, 1).astype(jnp.float32)
        value_part = lax.dynamic_slice_in_dim(value_rows, group * HEAD_SIZE, HEAD_SIZE, 1).astype(jnp.float32)
        scores = jnp.dot(query_part, key_part.T, precision=lax.Precision.HIGHEST) * scale
        scores = jnp.where(visible, scores, -1e+30)
        peak = lax.optimization_barrier(jnp.max(scores, axis=1, keepdims=True))
        expo = jnp.exp(scores - peak)
        weights = (expo / lax.optimization_barrier(jnp.sum(expo, axis=1, keepdims=True))).astype(jnp.bfloat16)
        output = jnp.dot(weights.astype(jnp.float32), value_part, precision=lax.Precision.HIGHEST).astype(jnp.bfloat16)
        return lax.dynamic_update_slice_in_dim(result, output, head * HEAD_SIZE, 1)
    return lax.fori_loop(0, q_heads, one_head, jnp.zeros(query_rows.shape, jnp.bfloat16))

def reference(queries, keys, values, dest_shard, dest_slot, ancestors):
    target = (dest_shard * TOK_DEV + dest_slot).astype(jnp.int32)
    bal_q = jnp.zeros_like(queries).at[target].set(queries)
    bal_k = jnp.zeros_like(keys).at[target].set(keys)
    bal_v = jnp.zeros_like(values).at[target].set(values)
    pad_k = jnp.concatenate([jnp.zeros((TOK_DEV, bal_k.shape[1]), bal_k.dtype), bal_k], axis=0)
    pad_v = jnp.concatenate([jnp.zeros((TOK_DEV, bal_v.shape[1]), bal_v.dtype), bal_v], axis=0)

    def shard_out(shard):
        start = shard * TOK_DEV
        q_rows = lax.dynamic_slice_in_dim(bal_q, start, TOK_DEV, 0)
        k_rows = lax.dynamic_slice_in_dim(pad_k, start, 2 * TOK_DEV, 0)
        v_rows = lax.dynamic_slice_in_dim(pad_v, start, 2 * TOK_DEV, 0)
        anc_rows = lax.dynamic_slice_in_dim(ancestors, shard * BPD, BPD, 0)
        return attend(q_rows, k_rows, v_rows, make_visible(anc_rows, shard))
    stacked = lax.map(shard_out, jnp.arange(N_SEQ, dtype=jnp.int32))
    return stacked.reshape(SLAB_TOKENS, QUERY_HEADS * HEAD_SIZE)
```

```python
import functools
import math

import jax
import jax.numpy as jnp
from jax import lax
from jax.experimental import pallas as pl
from jax.experimental.pallas import tpu as pltpu
from jax.sharding import PartitionSpec as P

HEAD_SIZE = 128
META = 8
RADIX = 32
NO_DEST = 255.0
NEG = -1e30
VMEM_LIMIT = 56 * 1024 * 1024

VM = pl.BlockSpec(memory_space=pltpu.VMEM)
SM = pl.BlockSpec(memory_space=pltpu.SMEM)
HB = pl.BlockSpec(memory_space=pl.ANY)


def params():
    return pltpu.CompilerParams(vmem_limit_bytes=VMEM_LIMIT)


def iota(shape, axis):
    return lax.broadcasted_iota(jnp.int32, shape, axis)


def matmul(a, b):
    return jnp.dot(a, b, preferred_element_type=jnp.float32)


def matmul_nt(a, b):
    return lax.dot_general(a, b, (((1,), (1,)), ((), ())), preferred_element_type=jnp.float32)


def select_rows(index, start, rows, dtype=jnp.bfloat16):
    return (iota((rows, index.shape[1]), 0) + start == index).astype(dtype)


def pack_kv_kernel(shards, unit, me_ref, dest_ref, slot_ref, k_ref, v_ref, q_ref, *outs):
    blocks, over, index_ref = outs[:shards], outs[shards], outs[shards + 1]
    count = k_ref.shape[0]
    kv = k_ref.shape[1]
    me = me_ref[0]
    dest = dest_ref[...].reshape(1, count)
    code = slot_ref[...].reshape(1, count) + 1
    onehot = (iota((shards, count), 0) == dest).astype(jnp.bfloat16)
    earlier = (iota((count, count), 0) < iota((count, count), 1)).astype(jnp.bfloat16)
    before = matmul(onehot, earlier)
    position = jnp.sum(before * onehot.astype(jnp.float32), axis=0, keepdims=True).astype(jnp.int32)
    base = position < unit
    index = jnp.where(base, (dest ^ me) * unit + position, -1)
    index_ref[...] = index
    over_index = jnp.where(base, -1, position - unit)
    totals = matmul_nt(jnp.ones((META, count), jnp.bfloat16), onehot)
    flags = (totals > unit + 0.5).astype(jnp.float32)
    over_dest = jnp.max(jnp.where(base, -1, dest))
    over_value = jnp.where(over_dest < 0, NO_DEST, over_dest.astype(jnp.float32))

    row = iota((META, count), 0)
    codes = jnp.where(row == 0, code // RADIX, jnp.where(row == 1, code % RADIX, 0))
    codes = codes.astype(jnp.float32).astype(jnp.bfloat16)

    def meta(picked, tail, width):
        sent = matmul_nt(codes, picked)
        sent = jnp.concatenate([sent, tail, jnp.zeros((META, width - unit - tail.shape[1]), jnp.float32)], axis=1)
        return sent

    flag_rows = jnp.where(iota((META, shards), 0) == 2, flags, 0.0)
    for r in range(shards):
        picked = select_rows(index, r * unit, unit)
        blocks[r][0:unit, 0:kv] = matmul(picked, k_ref[...]).astype(jnp.bfloat16)
        blocks[r][0:unit, kv : 2 * kv] = matmul(picked, v_ref[...]).astype(jnp.bfloat16)
        blocks[r][unit : unit + META, :] = meta(picked, flag_rows, 2 * kv).astype(jnp.bfloat16)
    picked = select_rows(over_index, 0, unit)
    width = q_ref.shape[1]
    over[0:unit, 0:width] = matmul(picked, q_ref[...]).astype(jnp.bfloat16)
    over[0:unit, width : width + kv] = matmul(picked, k_ref[...]).astype(jnp.bfloat16)
    over[0:unit, width + kv : width + 2 * kv] = matmul(picked, v_ref[...]).astype(jnp.bfloat16)
    full = width + 2 * kv
    tail = meta(picked, jnp.zeros((META, 0 + unit), jnp.float32), full)
    tail = jnp.where(iota((META, full), 0) == 2, over_value, tail)
    over[unit : unit + META, :] = tail.astype(jnp.bfloat16)


def pack_kv(me, dest, slot, keys, values, queries, shards, unit):
    width = 2 * keys.shape[1]
    full = width + queries.shape[1]
    shapes = [jax.ShapeDtypeStruct((unit + META, width), jnp.bfloat16)] * shards
    shapes += [jax.ShapeDtypeStruct((unit + META, full), jnp.bfloat16)]
    shapes += [jax.ShapeDtypeStruct((1, keys.shape[0]), jnp.int32)]
    outs = pl.pallas_call(
        functools.partial(pack_kv_kernel, shards, unit),
        out_shape=shapes,
        in_specs=[SM, VM, VM, VM, VM, VM],
        out_specs=[VM] * len(shapes),
        compiler_params=params(),
        name="pack_kv",
    )(me, dest, slot, keys, values, queries)
    return outs[:shards], outs[shards], outs[shards + 1]


def pack_q_kernel(shards, unit, index_ref, q_ref, *blocks):
    index = index_ref[...]
    for r in range(shards):
        picked = select_rows(index, r * unit, unit)
        blocks[r][...] = matmul(picked, q_ref[...]).astype(jnp.bfloat16)


def pack_q(index, queries, shards, unit):
    return pl.pallas_call(
        functools.partial(pack_q_kernel, shards, unit),
        out_shape=[jax.ShapeDtypeStruct((unit, queries.shape[1]), jnp.bfloat16)] * shards,
        in_specs=[VM, VM],
        out_specs=[VM] * shards,
        compiler_params=params(),
        name="pack_q",
    )(index, queries)


def pick_over_kernel(unit, me_ref, a_ref, b_ref, c_ref, d_ref, keep_ref, send_ref):
    me = me_ref[0].astype(jnp.float32)
    other = (me_ref[0] ^ 1).astype(jnp.float32)
    keep = jnp.zeros(keep_ref.shape, jnp.float32)
    send = jnp.zeros(keep_ref.shape, jnp.float32)
    for ref in (a_ref, b_ref, c_ref, d_ref):
        block = ref[...].astype(jnp.float32)
        target = block[unit + 2 : unit + 3, :]
        keep = jnp.where(target == me, block, keep)
        send = jnp.where(target == other, block, send)
    keep_ref[...] = keep.astype(jnp.bfloat16)
    send_ref[...] = send.astype(jnp.bfloat16)


def pick_over(me, held, unit):
    return pl.pallas_call(
        functools.partial(pick_over_kernel, unit),
        out_shape=[jax.ShapeDtypeStruct(held[0].shape, jnp.bfloat16)] * 2,
        in_specs=[SM] + [VM] * 4,
        out_specs=[VM, VM],
        compiler_params=params(),
        name="pick_over",
    )(me, *held)


def crowded_kernel(shards, unit, *refs):
    blocks, out_ref = refs[:shards], refs[shards]
    by_dest = jnp.zeros((1, shards), jnp.float32)
    most = jnp.zeros((1, 1), jnp.float32)
    for ref in blocks:
        flags = ref[2:3, unit : unit + shards].astype(jnp.float32)
        by_dest += flags
        most = jnp.maximum(most, jnp.sum(flags, axis=1, keepdims=True))
    most = jnp.maximum(most, jnp.max(by_dest, axis=1, keepdims=True))
    out_ref[...] = jnp.broadcast_to((most > 1.5).astype(jnp.int32), out_ref.shape)


def crowded(blocks, shards, unit):
    width = blocks[0].shape[1]
    spec = pl.BlockSpec((META, width), lambda i: (unit // META, 0))
    return pl.pallas_call(
        functools.partial(crowded_kernel, shards, unit),
        out_shape=jax.ShapeDtypeStruct((8, 128), jnp.int32),
        grid=(1,),
        in_specs=[spec] * shards,
        out_specs=pl.BlockSpec((8, 128), lambda i: (0, 0)),
        compiler_params=params(),
        name="crowded",
    )(*blocks)


def place_kv_kernel(pieces, unit, count, has_extra, *refs):
    it = iter(refs)
    flag_ref = next(it) if has_extra else None
    base = [next(it) for _ in range(pieces)]
    over = [next(it) for _ in range(2)]
    if has_extra:
        extra_ref, extra_code = next(it), next(it)
    placed_ref, codes_ref = next(it), next(it)
    width = placed_ref.shape[1]
    rows, codes = [], []

    def decode(meta):
        return (meta[0:1, 0:unit] * RADIX + meta[1:2, 0:unit]).astype(jnp.int32)

    for ref in base:
        rows.append(ref[0:unit, :])
        codes.append(decode(ref[unit : unit + META, :].astype(jnp.float32)))
    left = over[0].shape[1] - width
    for ref in over:
        rows.append(ref[0:unit, left:])
        codes.append(decode(ref[unit : unit + META, 0:128].astype(jnp.float32)))
    code = jnp.concatenate(codes, axis=1)
    if has_extra:
        is_over = iota(code.shape, 1) >= pieces * unit
        code = jnp.where(is_over & (flag_ref[0] > 0), 0, code)
    codes_ref[...] = code
    onehot = select_rows(code, 1, count)
    placed = matmul(onehot, jnp.concatenate(rows, axis=0))
    placed_ref[...] = placed.astype(jnp.bfloat16)
    if has_extra:

        @pl.when(flag_ref[0] > 0)
        def _():
            more = matmul(select_rows(extra_code[...], 1, count), extra_ref[...])
            placed_ref[...] += more.astype(jnp.bfloat16)


def place_kv(flag, base, over, extra, extra_code, unit, count):
    width = base[0].shape[1]
    raw = (len(base) + 2) * unit
    return pl.pallas_call(
        functools.partial(place_kv_kernel, len(base), unit, count, True),
        out_shape=[
            jax.ShapeDtypeStruct((count, width), jnp.bfloat16),
            jax.ShapeDtypeStruct((1, raw), jnp.int32),
        ],
        in_specs=[SM] + [VM] * (len(base) + 4),
        out_specs=[VM, VM],
        compiler_params=params(),
        name="place_kv",
    )(flag, *base, *over, extra, extra_code)


def attend_core(shard, anc_ref, q_pl, kv_all, out_ref):
    count, width = out_ref.shape
    block_count = anc_ref.shape[0]
    size = count // block_count
    kv_width = kv_all.shape[1] // 2
    groups = kv_width // HEAD_SIZE
    ratio = width // kv_width
    window = (block_count + 1) * size
    scale = math.log2(math.e) / math.sqrt(HEAD_SIZE)
    lane = iota((size, window), 1)
    for b in range(block_count):
        first = (shard - 1) * block_count + b
        key_block = lane // size + first
        seen = lane < 0
        for a in range(anc_ref.shape[1]):
            seen = seen | (key_block == anc_ref[b, a])
        own = lane >= block_count * size
        causal = lane - block_count * size <= iota((size, window), 0)
        seen = (seen & (lane < block_count * size)) | (own & causal)
        bias = jnp.where(seen, 0.0, NEG)
        for g in range(groups):
            columns = [(g * ratio + h) * HEAD_SIZE for h in range(ratio)]
            q = jnp.concatenate(
                [q_pl[b * size : (b + 1) * size, c : c + HEAD_SIZE] for c in columns], axis=0
            )
            k = kv_all[b * size : b * size + window, g * HEAD_SIZE : (g + 1) * HEAD_SIZE]
            v = kv_all[
                b * size : b * size + window,
                kv_width + g * HEAD_SIZE : kv_width + (g + 1) * HEAD_SIZE,
            ]
            scores = (matmul_nt(q, k) * scale).reshape(ratio, size, window) + bias[None]
            scores = scores.reshape(ratio * size, window)
            peak = jnp.max(scores, axis=1, keepdims=True)
            expo = jnp.exp2(scores - peak)
            total = jnp.sum(expo, axis=1, keepdims=True)
            weights = (expo * (1.0 / total)).astype(jnp.bfloat16)
            output = matmul(weights, v).astype(jnp.bfloat16)
            for h, c in enumerate(columns):
                out_ref[b * size : (b + 1) * size, c : c + HEAD_SIZE] = output[h * size : (h + 1) * size]


def attend_kernel(pieces, unit, me_ref, flag_ref, anc_ref, code_ref, *refs):
    it = iter(refs)
    base = [next(it) for _ in range(pieces)]
    over = [next(it) for _ in range(2)]
    own_kv, prior_kv, extra_ref, extra_code = next(it), next(it), next(it), next(it)
    out_ref = next(it)
    raw, q_pl, kv_all, extra_vm, sems, extra_sem = (next(it) for _ in range(6))
    count, width = out_ref.shape
    copies = [
        pltpu.make_async_copy(ref, raw.at[pl.ds(i * unit, unit), :], sems.at[i]) for i, ref in enumerate(base)
    ]
    for j, ref in enumerate(over):
        i = pieces + j
        copies.append(
            pltpu.make_async_copy(
                ref.at[pl.ds(0, unit), pl.ds(0, width)], raw.at[pl.ds(i * unit, unit), :], sems.at[i]
            )
        )
    copies.append(pltpu.make_async_copy(prior_kv, kv_all.at[pl.ds(0, count), :], sems.at[pieces + 2]))
    copies.append(pltpu.make_async_copy(own_kv, kv_all.at[pl.ds(count, count), :], sems.at[pieces + 3]))
    for c in copies:
        c.start()
    onehot = select_rows(code_ref[...], 1, count)
    for c in copies:
        c.wait()
    q_pl[...] = matmul(onehot, raw[...]).astype(jnp.bfloat16)

    @pl.when(flag_ref[0] > 0)
    def _():
        copy = pltpu.make_async_copy(extra_ref, extra_vm, extra_sem)
        copy.start()
        copy.wait()
        q_pl[...] += matmul(select_rows(extra_code[...], 1, count), extra_vm[...]).astype(jnp.bfloat16)

    attend_core(me_ref[0], anc_ref, q_pl, kv_all, out_ref)


def attend(me, flag, ancestors, codes, base, over, own_kv, prior_kv, extra, extra_code, unit):
    count = own_kv.shape[0]
    width = base[0].shape[1]
    pieces = len(base)
    raw = (pieces + 2) * unit
    return pl.pallas_call(
        functools.partial(attend_kernel, pieces, unit),
        out_shape=jax.ShapeDtypeStruct((count, width), jnp.bfloat16),
        in_specs=[SM, SM, SM, VM] + [HB] * (pieces + 5) + [VM],
        out_specs=VM,
        scratch_shapes=[
            pltpu.VMEM((raw, width), jnp.bfloat16),
            pltpu.VMEM((count, width), jnp.bfloat16),
            pltpu.VMEM((2 * count, own_kv.shape[1]), jnp.bfloat16),
            pltpu.VMEM(extra.shape, jnp.bfloat16),
            pltpu.SemaphoreType.DMA((pieces + 4,)),
            pltpu.SemaphoreType.DMA,
        ],
        compiler_params=params(),
        name="attend",
    )(me, flag, ancestors, codes, *base, *over, own_kv, prior_kv, extra, extra_code)


def attend_padded_kernel(me_ref, anc_ref, code_ref, raw_ref, own_kv, prior_kv, out_ref, q_pl, kv_all):
    count = out_ref.shape[0]
    kv_all[0:count, :] = prior_kv[...]
    kv_all[count : 2 * count, :] = own_kv[...]
    q_pl[...] = matmul(select_rows(code_ref[...], 1, count), raw_ref[...]).astype(jnp.bfloat16)
    attend_core(me_ref[0], anc_ref, q_pl, kv_all, out_ref)


def attend_padded(me, ancestors, codes, raw, own_kv, prior_kv):
    count, width = own_kv.shape[0], raw.shape[1]
    return pl.pallas_call(
        attend_padded_kernel,
        out_shape=jax.ShapeDtypeStruct((count, width), jnp.bfloat16),
        in_specs=[SM, SM] + [VM] * 4,
        out_specs=VM,
        scratch_shapes=[
            pltpu.VMEM((count, width), jnp.bfloat16),
            pltpu.VMEM((2 * count, own_kv.shape[1]), jnp.bfloat16),
        ],
        compiler_params=params(),
        name="attend_padded",
    )(me, ancestors, codes, raw, own_kv, prior_kv)


def positions(dest_shard, shards):
    onehot = (dest_shard[:, None] == jnp.arange(shards, dtype=jnp.int32)[None, :]).astype(jnp.int32)
    before = jnp.cumsum(onehot, axis=0) - onehot
    return jnp.sum(before * onehot, axis=1)


def exchange(source, index, total):
    buffer = jnp.zeros((total,) + source.shape[1:], source.dtype).at[index].set(source, mode="drop")
    return lax.all_to_all(buffer, "seq", split_axis=0, concat_axis=0, tiled=True)


def from_behind(block):
    n = lax.axis_size("seq")
    return lax.ppermute(block, "seq", [(i, i + 1) for i in range(n - 1)])


def swap(block, r):
    n = lax.axis_size("seq")
    return lax.ppermute(block, "seq", [(i, i ^ r) for i in range(n)])


def padded_plan(me, queries, keys, values, dest_shard, dest_slot, ancestors):
    count = queries.shape[0]
    shards = lax.axis_size("seq")
    capacity = 2 * count // shards
    total = shards * capacity
    index = dest_shard * capacity + positions(dest_shard, shards)
    kv = exchange(jnp.concatenate([keys, values], axis=1), index, total)
    raw = exchange(queries, index, total)
    code = exchange(dest_slot + 1, index, total)
    slots = jnp.where(code > 0, code - 1, count)
    own_kv = jnp.zeros((count, kv.shape[1]), kv.dtype).at[slots].set(kv, mode="drop")
    prior_kv = from_behind(own_kv)
    return attend_padded(me, ancestors, code.reshape(1, total), raw, own_kv, prior_kv)


def swap_plan(me, queries, keys, values, dest_shard, dest_slot, ancestors):
    count = queries.shape[0]
    shards = lax.axis_size("seq")
    unit = count // shards
    kv_blocks, over, index = pack_kv(me, dest_shard, dest_slot, keys, values, queries, shards, unit)
    first = swap(over, 4)
    got_kv = [kv_blocks[0]] + [swap(kv_blocks[r], r) for r in range(1, shards)]
    q_blocks = pack_q(index, queries, shards, unit)
    got_q = [q_blocks[0]] + [swap(q_blocks[r], r) for r in range(1, shards)]
    second = [swap(over, 2), swap(first, 2)]
    keep, send = pick_over(me, [over, first, *second], unit)
    over_rows = [keep, swap(send, 1)]
    flag = crowded(got_kv, shards, unit)[0, :1]
    width = queries.shape[1]

    def more():
        place = positions(dest_shard, shards) - unit
        at = jnp.where(place >= 0, dest_shard * unit + place, count)
        rows = exchange(jnp.concatenate([queries, keys, values], axis=1), at, count)
        return rows[:, :width], rows[:, width:], exchange(dest_slot + 1, at, count).reshape(1, count)

    def nothing():
        return (
            jnp.zeros(queries.shape, jnp.bfloat16),
            jnp.zeros((count, 2 * keys.shape[1]), jnp.bfloat16),
            jnp.zeros((1, count), jnp.int32),
        )

    extra_q, extra_kv, extra_code = lax.cond(flag[0] > 0, more, nothing)
    own_kv, codes = place_kv(flag, got_kv, over_rows, extra_kv, extra_code, unit, count)
    prior_kv = from_behind(own_kv)
    return attend(me, flag, ancestors, codes, got_q, over_rows, own_kv, prior_kv, extra_q, extra_code, unit)


def local(queries, keys, values, dest_shard, dest_slot, ancestors):
    shards = lax.axis_size("seq")
    me = lax.axis_index("seq").astype(jnp.int32).reshape(1)
    plan = swap_plan if shards == 8 and queries.shape[0] % (16 * shards) == 0 else padded_plan
    return plan(me, queries, keys, values, dest_shard, dest_slot, ancestors)


def solution(mesh):
    rows = P(("groups", "seq"))
    heads = P(("groups", "seq"), "head")
    return jax.shard_map(
        local,
        mesh=mesh,
        in_specs=(heads, heads, heads, rows, rows, P(("groups", "seq"), None)),
        out_specs=heads,
        check_vma=False,
    )
```

```python
import functools
import math

import jax
import jax.numpy as jnp
from jax import lax
from jax.experimental import pallas as pl
from jax.experimental.pallas import tpu as pltpu
from jax.sharding import PartitionSpec as P

HEAD_SIZE = 128
META = 8
RADIX = 32
NO_DEST = 255.0
NEG = -1e30

VM = pl.BlockSpec(memory_space=pltpu.VMEM)
SM = pl.BlockSpec(memory_space=pltpu.SMEM)
HB = pl.BlockSpec(memory_space=pl.ANY)


def light():
    return pl.CostEstimate(flops=0, bytes_accessed=0, transcendentals=0)


def params(mebibytes=56):
    return pltpu.CompilerParams(vmem_limit_bytes=mebibytes * 1024 * 1024)


def iota(shape, axis):
    return lax.broadcasted_iota(jnp.int32, shape, axis)


def matmul(a, b):
    return jnp.dot(a, b, preferred_element_type=jnp.float32)


def matmul_nt(a, b):
    return lax.dot_general(a, b, (((1,), (1,)), ((), ())), preferred_element_type=jnp.float32)


def select_rows(index, start, rows, dtype=jnp.bfloat16):
    return (iota((rows, index.shape[1]), 0) + start == index).astype(dtype)


def pack_kv_kernel(shards, unit, me_ref, dest_ref, slot_ref, k_ref, v_ref, q_ref, *outs):
    blocks, over, index_ref = outs[:shards], outs[shards], outs[shards + 1]
    count = k_ref.shape[0]
    kv = k_ref.shape[1]
    me = me_ref[0]
    dest = dest_ref[...].reshape(1, count)
    code = slot_ref[...].reshape(1, count) + 1
    onehot = (iota((shards, count), 0) == dest).astype(jnp.bfloat16)
    earlier = (iota((count, count), 0) < iota((count, count), 1)).astype(jnp.bfloat16)
    before = matmul(onehot, earlier)
    position = jnp.sum(before * onehot.astype(jnp.float32), axis=0, keepdims=True).astype(jnp.int32)
    base = position < unit
    index = jnp.where(base, (dest ^ me) * unit + position, -1)
    index_ref[...] = jnp.where(base, dest * unit + position, -1)
    over_index = jnp.where(base, -1, position - unit)
    totals = matmul_nt(jnp.ones((META, count), jnp.bfloat16), onehot)
    flags = (totals > unit + 0.5).astype(jnp.float32)
    over_dest = jnp.max(jnp.where(base, -1, dest))
    over_value = jnp.where(over_dest < 0, NO_DEST, over_dest.astype(jnp.float32))

    row = iota((META, count), 0)
    codes = jnp.where(row == 0, code // RADIX, jnp.where(row == 1, code % RADIX, 0))
    codes = codes.astype(jnp.float32).astype(jnp.bfloat16)

    def meta(picked, tail, width):
        sent = matmul_nt(codes, picked)
        sent = jnp.concatenate([sent, tail, jnp.zeros((META, width - unit - tail.shape[1]), jnp.float32)], axis=1)
        return sent

    flag_rows = jnp.where(iota((META, shards), 0) == 2, flags, 0.0)
    for r in range(shards):
        picked = select_rows(index, r * unit, unit)
        blocks[r][0:unit, 0:kv] = matmul(picked, k_ref[...]).astype(jnp.bfloat16)
        blocks[r][0:unit, kv : 2 * kv] = matmul(picked, v_ref[...]).astype(jnp.bfloat16)
        blocks[r][unit : unit + META, :] = meta(picked, flag_rows, 2 * kv).astype(jnp.bfloat16)
    picked = select_rows(over_index, 0, unit)
    width = q_ref.shape[1]
    over[0:unit, 0:width] = matmul(picked, q_ref[...]).astype(jnp.bfloat16)
    over[0:unit, width : width + kv] = matmul(picked, k_ref[...]).astype(jnp.bfloat16)
    over[0:unit, width + kv : width + 2 * kv] = matmul(picked, v_ref[...]).astype(jnp.bfloat16)
    full = width + 2 * kv
    tail = meta(picked, jnp.zeros((META, 0 + unit), jnp.float32), full)
    tail = jnp.where(iota((META, full), 0) == 2, over_value, tail)
    over[unit : unit + META, :] = tail.astype(jnp.bfloat16)


def pack_kv(me, dest, slot, keys, values, queries, shards, unit):
    width = 2 * keys.shape[1]
    full = width + queries.shape[1]
    shapes = [jax.ShapeDtypeStruct((unit + META, width), jnp.bfloat16)] * shards
    shapes += [jax.ShapeDtypeStruct((unit + META, full), jnp.bfloat16)]
    shapes += [jax.ShapeDtypeStruct((1, keys.shape[0]), jnp.int32)]
    outs = pl.pallas_call(
        functools.partial(pack_kv_kernel, shards, unit),
        out_shape=shapes,
        in_specs=[SM, VM, VM, VM, VM, VM],
        out_specs=[VM] * len(shapes),
        compiler_params=params(16),
        cost_estimate=light(),
        name="pack_kv",
    )(me, dest, slot, keys, values, queries)
    return outs[:shards], outs[shards], outs[shards + 1]


def pack_q_kernel(index_ref, q_ref, out_ref):
    picked = select_rows(index_ref[...], 0, out_ref.shape[0])
    out_ref[...] = matmul(picked, q_ref[...]).astype(jnp.bfloat16)


def pack_q(index, queries):
    return pl.pallas_call(
        pack_q_kernel,
        out_shape=jax.ShapeDtypeStruct(queries.shape, jnp.bfloat16),
        in_specs=[VM, VM],
        out_specs=VM,
        compiler_params=params(12),
        cost_estimate=light(),
        name="pack_q",
    )(index, queries)


def pick_over_kernel(unit, me_ref, a_ref, b_ref, c_ref, d_ref, keep_ref, send_ref):
    me = me_ref[0].astype(jnp.float32)
    other = (me_ref[0] ^ 1).astype(jnp.float32)
    keep = jnp.zeros(keep_ref.shape, jnp.float32)
    send = jnp.zeros(keep_ref.shape, jnp.float32)
    for ref in (a_ref, b_ref, c_ref, d_ref):
        block = ref[...].astype(jnp.float32)
        target = block[unit + 2 : unit + 3, :]
        keep = jnp.where(target == me, block, keep)
        send = jnp.where(target == other, block, send)
    keep_ref[...] = keep.astype(jnp.bfloat16)
    send_ref[...] = send.astype(jnp.bfloat16)


def pick_over(me, held, unit):
    return pl.pallas_call(
        functools.partial(pick_over_kernel, unit),
        out_shape=[jax.ShapeDtypeStruct(held[0].shape, jnp.bfloat16)] * 2,
        in_specs=[SM] + [VM] * 4,
        out_specs=[VM, VM],
        compiler_params=params(8),
        cost_estimate=light(),
        name="pick_over",
    )(me, *held)


def crowded_kernel(shards, unit, *refs):
    blocks, out_ref = refs[:shards], refs[shards]
    by_dest = jnp.zeros((1, shards), jnp.float32)
    most = jnp.zeros((1, 1), jnp.float32)
    for ref in blocks:
        flags = ref[2:3, unit : unit + shards].astype(jnp.float32)
        by_dest += flags
        most = jnp.maximum(most, jnp.sum(flags, axis=1, keepdims=True))
    most = jnp.maximum(most, jnp.max(by_dest, axis=1, keepdims=True))
    out_ref[...] = jnp.broadcast_to((most > 1.5).astype(jnp.int32), out_ref.shape)


def crowded(blocks, shards, unit):
    width = blocks[0].shape[1]
    spec = pl.BlockSpec((META, width), lambda i: (unit // META, 0))
    return pl.pallas_call(
        functools.partial(crowded_kernel, shards, unit),
        out_shape=jax.ShapeDtypeStruct((8, 128), jnp.int32),
        grid=(1,),
        in_specs=[spec] * shards,
        out_specs=pl.BlockSpec((8, 128), lambda i: (0, 0)),
        compiler_params=params(4),
        cost_estimate=light(),
        name="crowded",
    )(*blocks)


def place_kv_kernel(pieces, unit, count, *refs):
    base, over = refs[:pieces], refs[pieces : pieces + 2]
    placed_ref, codes_ref = refs[pieces + 2 :]
    width = placed_ref.shape[1]
    rows, codes = [], []

    def decode(meta):
        return (meta[0:1, 0:unit] * RADIX + meta[1:2, 0:unit]).astype(jnp.int32)

    for ref in base:
        rows.append(ref[0:unit, :])
        codes.append(decode(ref[unit : unit + META, :].astype(jnp.float32)))
    left = over[0].shape[1] - width
    for ref in over:
        rows.append(ref[0:unit, left:])
        codes.append(decode(ref[unit : unit + META, 0:128].astype(jnp.float32)))
    code = jnp.concatenate(codes, axis=1)
    codes_ref[...] = code
    placed = matmul(select_rows(code, 1, count), jnp.concatenate(rows, axis=0))
    placed_ref[...] = placed.astype(jnp.bfloat16)


def place_kv(base, over, unit, count):
    width = base[0].shape[1]
    raw = (len(base) + 2) * unit
    return pl.pallas_call(
        functools.partial(place_kv_kernel, len(base), unit, count),
        out_shape=[
            jax.ShapeDtypeStruct((count, width), jnp.bfloat16),
            jax.ShapeDtypeStruct((1, raw), jnp.int32),
        ],
        in_specs=[VM] * (len(base) + 2),
        out_specs=[VM, VM],
        compiler_params=params(10),
        cost_estimate=light(),
        name="place_kv",
    )(*base, *over)


def attend_core(shard, anc_ref, q_pl, kv_all, out_ref):
    count, width = out_ref.shape
    block_count = anc_ref.shape[0]
    size = count // block_count
    kv_width = kv_all.shape[1] // 2
    groups = kv_width // HEAD_SIZE
    ratio = width // kv_width
    window = (block_count + 1) * size
    scale = math.log2(math.e) / math.sqrt(HEAD_SIZE)
    lane = iota((size, window), 1)
    for b in range(block_count):
        first = (shard - 1) * block_count + b
        key_block = lane // size + first
        seen = lane < 0
        for a in range(anc_ref.shape[1]):
            seen = seen | (key_block == anc_ref[b, a])
        own = lane >= block_count * size
        causal = lane - block_count * size <= iota((size, window), 0)
        seen = (seen & (lane < block_count * size)) | (own & causal)
        bias = jnp.where(seen, 0.0, NEG)
        for g in range(groups):
            columns = [(g * ratio + h) * HEAD_SIZE for h in range(ratio)]
            q = jnp.concatenate(
                [q_pl[b * size : (b + 1) * size, c : c + HEAD_SIZE] for c in columns], axis=0
            )
            k = kv_all[b * size : b * size + window, g * HEAD_SIZE : (g + 1) * HEAD_SIZE]
            v = kv_all[
                b * size : b * size + window,
                kv_width + g * HEAD_SIZE : kv_width + (g + 1) * HEAD_SIZE,
            ]
            scores = (matmul_nt(q, k) * scale).reshape(ratio, size, window) + bias[None]
            scores = scores.reshape(ratio * size, window)
            peak = jnp.max(scores, axis=1, keepdims=True)
            expo = jnp.exp2(scores - peak)
            total = jnp.sum(expo, axis=1, keepdims=True)
            weights = (expo * (1.0 / total)).astype(jnp.bfloat16)
            output = matmul(weights, v).astype(jnp.bfloat16)
            for h, c in enumerate(columns):
                out_ref[b * size : (b + 1) * size, c : c + HEAD_SIZE] = output[h * size : (h + 1) * size]


def attend_kernel(pieces, unit, me_ref, anc_ref, code_ref, *refs):
    base, over = refs[0], refs[1:3]
    own_kv, prior_kv, out_ref, raw, q_pl, kv_all, sems = refs[3:]
    count, width = out_ref.shape
    copies = []
    for r in range(pieces):
        start = pl.multiple_of((me_ref[0] ^ r) * unit, unit)
        copies.append(
            pltpu.make_async_copy(
                base.at[pl.ds(start, unit), :], raw.at[pl.ds(r * unit, unit), :], sems.at[r]
            )
        )
    for j, ref in enumerate(over):
        i = pieces + j
        copies.append(
            pltpu.make_async_copy(
                ref.at[pl.ds(0, unit), pl.ds(0, width)], raw.at[pl.ds(i * unit, unit), :], sems.at[i]
            )
        )
    copies.append(pltpu.make_async_copy(prior_kv, kv_all.at[pl.ds(0, count), :], sems.at[pieces + 2]))
    copies.append(pltpu.make_async_copy(own_kv, kv_all.at[pl.ds(count, count), :], sems.at[pieces + 3]))
    for c in copies:
        c.start()
    onehot = select_rows(code_ref[...], 1, count)
    for c in copies:
        c.wait()
    q_pl[...] = matmul(onehot, raw[...]).astype(jnp.bfloat16)
    attend_core(me_ref[0], anc_ref, q_pl, kv_all, out_ref)


def attend(me, ancestors, codes, base, over, own_kv, prior_kv, unit):
    count, width = base.shape
    pieces = count // unit
    raw = (pieces + 2) * unit
    return pl.pallas_call(
        functools.partial(attend_kernel, pieces, unit),
        out_shape=jax.ShapeDtypeStruct((count, width), jnp.bfloat16),
        in_specs=[SM, SM, VM] + [HB] * 5,
        out_specs=VM,
        scratch_shapes=[
            pltpu.VMEM((raw, width), jnp.bfloat16),
            pltpu.VMEM((count, width), jnp.bfloat16),
            pltpu.VMEM((2 * count, own_kv.shape[1]), jnp.bfloat16),
            pltpu.SemaphoreType.DMA((pieces + 4,)),
        ],
        compiler_params=params(28),
        cost_estimate=light(),
        name="attend",
    )(me, ancestors, codes, base, *over, own_kv, prior_kv)


def attend_padded_kernel(me_ref, anc_ref, code_ref, raw_ref, own_kv, prior_kv, out_ref, q_pl, kv_all):
    count = out_ref.shape[0]
    kv_all[0:count, :] = prior_kv[...]
    kv_all[count : 2 * count, :] = own_kv[...]
    q_pl[...] = matmul(select_rows(code_ref[...], 1, count), raw_ref[...]).astype(jnp.bfloat16)
    attend_core(me_ref[0], anc_ref, q_pl, kv_all, out_ref)


def attend_padded(me, ancestors, codes, raw, own_kv, prior_kv):
    count, width = own_kv.shape[0], raw.shape[1]
    return pl.pallas_call(
        attend_padded_kernel,
        out_shape=jax.ShapeDtypeStruct((count, width), jnp.bfloat16),
        in_specs=[SM, SM] + [VM] * 4,
        out_specs=VM,
        scratch_shapes=[
            pltpu.VMEM((count, width), jnp.bfloat16),
            pltpu.VMEM((2 * count, own_kv.shape[1]), jnp.bfloat16),
        ],
        compiler_params=params(),
        name="attend_padded",
    )(me, ancestors, codes, raw, own_kv, prior_kv)


def positions(dest_shard, shards):
    onehot = (dest_shard[:, None] == jnp.arange(shards, dtype=jnp.int32)[None, :]).astype(jnp.int32)
    before = jnp.cumsum(onehot, axis=0) - onehot
    return jnp.sum(before * onehot, axis=1)


def exchange(source, index, total):
    buffer = jnp.zeros((total,) + source.shape[1:], source.dtype).at[index].set(source, mode="drop")
    return lax.all_to_all(buffer, "seq", split_axis=0, concat_axis=0, tiled=True)


def from_behind(block):
    n = lax.axis_size("seq")
    return lax.ppermute(block, "seq", [(i, i + 1) for i in range(n - 1)])


def swap(block, r):
    n = lax.axis_size("seq")
    return lax.ppermute(block, "seq", [(i, i ^ r) for i in range(n)])


def padded_plan(me, queries, keys, values, dest_shard, dest_slot, ancestors):
    count = queries.shape[0]
    shards = lax.axis_size("seq")
    capacity = 2 * count // shards
    total = shards * capacity
    index = dest_shard * capacity + positions(dest_shard, shards)
    kv = exchange(jnp.concatenate([keys, values], axis=1), index, total)
    raw = exchange(queries, index, total)
    code = exchange(dest_slot + 1, index, total)
    slots = jnp.where(code > 0, code - 1, count)
    own_kv = jnp.zeros((count, kv.shape[1]), kv.dtype).at[slots].set(kv, mode="drop")
    prior_kv = from_behind(own_kv)
    return attend_padded(me, ancestors, code.reshape(1, total), raw, own_kv, prior_kv)


def swap_plan(me, queries, keys, values, dest_shard, dest_slot, ancestors):
    count = queries.shape[0]
    shards = lax.axis_size("seq")
    unit = count // shards
    kv_blocks, over, index = pack_kv(me, dest_shard, dest_slot, keys, values, queries, shards, unit)
    got_q = lax.all_to_all(pack_q(index, queries), "seq", split_axis=0, concat_axis=0, tiled=True)
    first = swap(over, 4)
    got_kv = [kv_blocks[0]] + [swap(kv_blocks[r], r) for r in range(1, shards)]
    second = [swap(over, 2), swap(first, 2)]
    keep, send = pick_over(me, [over, first, *second], unit)
    over_rows = [keep, swap(send, 1)]
    own_kv, codes = place_kv(got_kv, over_rows, unit, count)
    prior_kv = from_behind(own_kv)
    result = attend(me, ancestors, codes, got_q, over_rows, own_kv, prior_kv, unit)
    flag = crowded(got_kv, shards, unit)[0, 0]
    args = (queries, keys, values, dest_shard, dest_slot, ancestors)
    return lax.cond(flag > 0, lambda: padded_plan(me, *args), lambda: result)


def local(queries, keys, values, dest_shard, dest_slot, ancestors):
    shards = lax.axis_size("seq")
    me = lax.axis_index("seq").astype(jnp.int32).reshape(1)
    plan = swap_plan if shards == 8 and queries.shape[0] % (16 * shards) == 0 else padded_plan
    return plan(me, queries, keys, values, dest_shard, dest_slot, ancestors)


def solution(mesh):
    rows = P(("groups", "seq"))
    heads = P(("groups", "seq"), "head")
    return jax.shard_map(
        local,
        mesh=mesh,
        in_specs=(heads, heads, heads, rows, rows, P(("groups", "seq"), None)),
        out_specs=heads,
        check_vma=False,
    )
```

```python
import functools
import math

import jax
import jax.numpy as jnp
from jax import lax
from jax.experimental import pallas as pl
from jax.experimental.pallas import tpu as pltpu
from jax.sharding import PartitionSpec as P

HEAD_SIZE = 128
META = 8
RADIX = 32
NO_DEST = 255.0
NEG = -1e30

VM = pl.BlockSpec(memory_space=pltpu.VMEM)
SM = pl.BlockSpec(memory_space=pltpu.SMEM)
HB = pl.BlockSpec(memory_space=pl.ANY)


def light():
    return pl.CostEstimate(flops=0, bytes_accessed=0, transcendentals=0)


def params(mebibytes=56):
    return pltpu.CompilerParams(vmem_limit_bytes=mebibytes * 1024 * 1024)


def iota(shape, axis):
    return lax.broadcasted_iota(jnp.int32, shape, axis)


def matmul(a, b):
    return jnp.dot(a, b, preferred_element_type=jnp.float32)


def matmul_nt(a, b):
    return lax.dot_general(a, b, (((1,), (1,)), ((), ())), preferred_element_type=jnp.float32)


def select_rows(index, start, rows, dtype=jnp.bfloat16):
    return (iota((rows, index.shape[1]), 0) + start == index).astype(dtype)


def pack_kv_kernel(shards, unit, me_ref, dest_ref, slot_ref, k_ref, v_ref, q_ref, *outs):
    blocks, over, index_ref = outs[:shards], outs[shards], outs[shards + 1]
    count = k_ref.shape[0]
    kv = k_ref.shape[1]
    me = me_ref[0]
    dest = dest_ref[...].reshape(1, count)
    code = slot_ref[...].reshape(1, count) + 1
    onehot = (iota((shards, count), 0) == dest).astype(jnp.bfloat16)
    earlier = (iota((count, count), 0) < iota((count, count), 1)).astype(jnp.bfloat16)
    before = matmul(onehot, earlier)
    position = jnp.sum(before * onehot.astype(jnp.float32), axis=0, keepdims=True).astype(jnp.int32)
    base = position < unit
    index = jnp.where(base, (dest ^ me) * unit + position, -1)
    index_ref[...] = index
    over_index = jnp.where(base, -1, position - unit)
    totals = matmul_nt(jnp.ones((META, count), jnp.bfloat16), onehot)
    flags = (totals > unit + 0.5).astype(jnp.float32)
    over_dest = jnp.max(jnp.where(base, -1, dest))
    over_value = jnp.where(over_dest < 0, NO_DEST, over_dest.astype(jnp.float32))

    row = iota((META, count), 0)
    codes = jnp.where(row == 0, code // RADIX, jnp.where(row == 1, code % RADIX, 0))
    codes = codes.astype(jnp.float32).astype(jnp.bfloat16)

    def meta(picked, tail, width):
        sent = matmul_nt(codes, picked)
        sent = jnp.concatenate([sent, tail, jnp.zeros((META, width - unit - tail.shape[1]), jnp.float32)], axis=1)
        return sent

    flag_rows = jnp.where(iota((META, shards), 0) == 2, flags, 0.0)
    for r in range(shards):
        picked = select_rows(index, r * unit, unit)
        blocks[r][0:unit, 0:kv] = matmul(picked, k_ref[...]).astype(jnp.bfloat16)
        blocks[r][0:unit, kv : 2 * kv] = matmul(picked, v_ref[...]).astype(jnp.bfloat16)
        blocks[r][unit : unit + META, :] = meta(picked, flag_rows, 2 * kv).astype(jnp.bfloat16)
    picked = select_rows(over_index, 0, unit)
    width = q_ref.shape[1]
    over[0:unit, 0:width] = matmul(picked, q_ref[...]).astype(jnp.bfloat16)
    over[0:unit, width : width + kv] = matmul(picked, k_ref[...]).astype(jnp.bfloat16)
    over[0:unit, width + kv : width + 2 * kv] = matmul(picked, v_ref[...]).astype(jnp.bfloat16)
    full = width + 2 * kv
    tail = meta(picked, jnp.zeros((META, 0 + unit), jnp.float32), full)
    tail = jnp.where(iota((META, full), 0) == 2, over_value, tail)
    over[unit : unit + META, :] = tail.astype(jnp.bfloat16)


def pack_kv(me, dest, slot, keys, values, queries, shards, unit):
    width = 2 * keys.shape[1]
    full = width + queries.shape[1]
    shapes = [jax.ShapeDtypeStruct((unit + META, width), jnp.bfloat16)] * shards
    shapes += [jax.ShapeDtypeStruct((unit + META, full), jnp.bfloat16)]
    shapes += [jax.ShapeDtypeStruct((1, keys.shape[0]), jnp.int32)]
    outs = pl.pallas_call(
        functools.partial(pack_kv_kernel, shards, unit),
        out_shape=shapes,
        in_specs=[SM, VM, VM, VM, VM, VM],
        out_specs=[VM] * len(shapes),
        compiler_params=params(16),
        cost_estimate=light(),
        name="pack_kv",
    )(me, dest, slot, keys, values, queries)
    return outs[:shards], outs[shards], outs[shards + 1]


def pack_q_kernel(unit, cuts, index_ref, q_ref, *outs):
    index = index_ref[...]
    outs = iter(outs)
    for r, parts in enumerate(cuts):
        picked = select_rows(index, r * unit, unit)
        width = q_ref.shape[1] // parts
        for i in range(parts):
            rows = matmul(picked, q_ref[:, i * width : (i + 1) * width])
            next(outs)[...] = rows.astype(jnp.bfloat16)


def pack_q(index, queries, unit, cuts):
    width = queries.shape[1]
    shapes = [jax.ShapeDtypeStruct((unit, width // n), jnp.bfloat16) for n in cuts for _ in range(n)]
    outs = iter(
        pl.pallas_call(
            functools.partial(pack_q_kernel, unit, cuts),
            out_shape=shapes,
            in_specs=[VM, VM],
            out_specs=[VM] * len(shapes),
            compiler_params=params(12),
            cost_estimate=light(),
            name="pack_q",
        )(index, queries)
    )
    return [[next(outs) for _ in range(n)] for n in cuts]


def pick_over_kernel(unit, me_ref, a_ref, b_ref, c_ref, d_ref, keep_ref, send_ref):
    me = me_ref[0].astype(jnp.float32)
    other = (me_ref[0] ^ 1).astype(jnp.float32)
    keep = jnp.zeros(keep_ref.shape, jnp.float32)
    send = jnp.zeros(keep_ref.shape, jnp.float32)
    for ref in (a_ref, b_ref, c_ref, d_ref):
        block = ref[...].astype(jnp.float32)
        target = block[unit + 2 : unit + 3, :]
        keep = jnp.where(target == me, block, keep)
        send = jnp.where(target == other, block, send)
    keep_ref[...] = keep.astype(jnp.bfloat16)
    send_ref[...] = send.astype(jnp.bfloat16)


def pick_over(me, held, unit):
    return pl.pallas_call(
        functools.partial(pick_over_kernel, unit),
        out_shape=[jax.ShapeDtypeStruct(held[0].shape, jnp.bfloat16)] * 2,
        in_specs=[SM] + [VM] * 4,
        out_specs=[VM, VM],
        compiler_params=params(8),
        cost_estimate=light(),
        name="pick_over",
    )(me, *held)


def crowded_kernel(shards, unit, *refs):
    blocks, out_ref = refs[:shards], refs[shards]
    by_dest = jnp.zeros((1, shards), jnp.float32)
    most = jnp.zeros((1, 1), jnp.float32)
    for ref in blocks:
        flags = ref[2:3, unit : unit + shards].astype(jnp.float32)
        by_dest += flags
        most = jnp.maximum(most, jnp.sum(flags, axis=1, keepdims=True))
    most = jnp.maximum(most, jnp.max(by_dest, axis=1, keepdims=True))
    out_ref[...] = jnp.broadcast_to((most > 1.5).astype(jnp.int32), out_ref.shape)


def crowded(blocks, shards, unit):
    width = blocks[0].shape[1]
    spec = pl.BlockSpec((META, width), lambda i: (unit // META, 0))
    return pl.pallas_call(
        functools.partial(crowded_kernel, shards, unit),
        out_shape=jax.ShapeDtypeStruct((8, 128), jnp.int32),
        grid=(1,),
        in_specs=[spec] * shards,
        out_specs=pl.BlockSpec((8, 128), lambda i: (0, 0)),
        compiler_params=params(4),
        cost_estimate=light(),
        name="crowded",
    )(*blocks)


def decode(meta, unit):
    meta = meta.astype(jnp.float32)
    return (meta[0:1, 0:unit] * RADIX + meta[1:2, 0:unit]).astype(jnp.int32)


def place_kv_kernel(pieces, unit, count, *refs):
    base, (placed_ref, codes_ref) = refs[:pieces], refs[pieces:]
    code = jnp.concatenate([decode(ref[unit : unit + META, :], unit) for ref in base], axis=1)
    codes_ref[...] = code
    rows = jnp.concatenate([ref[0:unit, :] for ref in base], axis=0)
    placed_ref[...] = matmul(select_rows(code, 1, count), rows).astype(jnp.bfloat16)


def place_kv(base, unit, count):
    width = base[0].shape[1]
    raw = len(base) * unit
    return pl.pallas_call(
        functools.partial(place_kv_kernel, len(base), unit, count),
        out_shape=[
            jax.ShapeDtypeStruct((count, width), jnp.bfloat16),
            jax.ShapeDtypeStruct((1, raw), jnp.int32),
        ],
        in_specs=[VM] * len(base),
        out_specs=[VM, VM],
        compiler_params=params(10),
        cost_estimate=light(),
        name="place_kv",
    )(*base)


def merge_over_kernel(a_ref, b_ref, q_ref, kv_ref):
    rows, width = q_ref.shape
    q_ref[...] = a_ref[0:rows, 0:width] + b_ref[0:rows, 0:width]
    kv_ref[...] = a_ref[:, width:] + b_ref[:, width:]
    kv_ref[rows:, 0:HEAD_SIZE] = a_ref[rows:, 0:HEAD_SIZE] + b_ref[rows:, 0:HEAD_SIZE]


def merge_over(kept, got, unit, kv_width):
    width = kept.shape[1] - kv_width
    return pl.pallas_call(
        merge_over_kernel,
        out_shape=[
            jax.ShapeDtypeStruct((unit, width), jnp.bfloat16),
            jax.ShapeDtypeStruct((unit + META, kv_width), jnp.bfloat16),
        ],
        in_specs=[VM, VM],
        out_specs=[VM, VM],
        compiler_params=params(4),
        cost_estimate=light(),
        name="merge_over",
    )(kept, got)


def attend_core(shard, anc_ref, q_pl, kv_all, out_ref, groups):
    count, width = out_ref.shape
    block_count = anc_ref.shape[0]
    size = count // block_count
    ratio = width // groups // HEAD_SIZE
    window = (block_count + 1) * size
    scale = math.log2(math.e) / math.sqrt(HEAD_SIZE)
    lane = iota((size, window), 1)
    for b in range(block_count):
        first = (shard - 1) * block_count + b
        key_block = lane // size + first
        seen = lane < 0
        for a in range(anc_ref.shape[1]):
            seen = seen | (key_block == anc_ref[b, a])
        own = lane >= block_count * size
        causal = lane - block_count * size <= iota((size, window), 0)
        seen = (seen & (lane < block_count * size)) | (own & causal)
        bias = jnp.where(seen, 0.0, NEG)
        for g in range(groups):
            columns = [(g * ratio + h) * HEAD_SIZE for h in range(ratio)]
            q = jnp.concatenate(
                [q_pl[b * size : (b + 1) * size, c : c + HEAD_SIZE] for c in columns], axis=0
            )
            k = kv_all[b * size : b * size + window, g * HEAD_SIZE : (g + 1) * HEAD_SIZE]
            v = kv_all[
                b * size : b * size + window,
                (groups + g) * HEAD_SIZE : (groups + g + 1) * HEAD_SIZE,
            ]
            scores = (matmul_nt(q, k) * scale).reshape(ratio, size, window) + bias[None]
            scores = scores.reshape(ratio * size, window)
            peak = jnp.max(scores, axis=1, keepdims=True)
            expo = jnp.exp2(scores - peak)
            total = jnp.sum(expo, axis=1, keepdims=True)
            weights = (expo * (1.0 / total)).astype(jnp.bfloat16)
            output = matmul(weights, v).astype(jnp.bfloat16)
            for h, c in enumerate(columns):
                out_ref[b * size : (b + 1) * size, c : c + HEAD_SIZE] = output[h * size : (h + 1) * size]


def attend_kernel(pieces, unit, group, me_ref, anc_ref, code_ref, over_ref, behind_ref, *refs):
    base, over_q, own_kv, prior_kv = refs[:pieces], *refs[pieces : pieces + 3]
    out_ref, raw, q_pl, kv_all, sems = refs[-5:]
    count, width = q_pl.shape
    kv_width = own_kv.shape[1] // 2
    copies = []

    def fetch(source, target):
        copies.append(pltpu.make_async_copy(source, target, sems.at[len(copies)]))

    for r, ref in enumerate(base):
        start = group * width if ref.shape[1] > width else 0
        fetch(ref.at[:, pl.ds(start, width)], raw.at[pl.ds(r * unit, unit), :])
    fetch(over_q.at[:, pl.ds(group * width, width)], raw.at[pl.ds(pieces * unit, unit), :])
    for j, ref in enumerate((prior_kv, own_kv)):
        for h in range(2):
            fetch(
                ref.at[:, pl.ds(h * kv_width + group * HEAD_SIZE, HEAD_SIZE)],
                kv_all.at[pl.ds(j * count, count), pl.ds(h * HEAD_SIZE, HEAD_SIZE)],
            )
    for c in copies:
        c.start()
    own_over = decode(over_ref[unit : unit + META, :], unit)
    behind_over = decode(behind_ref[unit : unit + META, :], unit)
    onehot = select_rows(jnp.concatenate([code_ref[...], own_over], axis=1), 1, count)
    for c in copies:
        c.wait()
    q_pl[...] = matmul(onehot, raw[...]).astype(jnp.bfloat16)
    for j, (code, ref) in enumerate(((behind_over, behind_ref), (own_over, over_ref))):
        picked = select_rows(code, 1, count)
        for h in range(2):
            c = h * kv_width + group * HEAD_SIZE
            rows = matmul(picked, ref[0:unit, c : c + HEAD_SIZE]).astype(jnp.bfloat16)
            kv_all[j * count : (j + 1) * count, h * HEAD_SIZE : (h + 1) * HEAD_SIZE] += rows
    attend_core(me_ref[0], anc_ref, q_pl, kv_all, out_ref, 1)


def attend(me, ancestors, codes, over_kv, behind_kv, base, over_q, own_kv, prior_kv, unit, group, groups, sofar):
    count = own_kv.shape[0]
    width = over_q.shape[1] // groups
    pieces = len(base)
    args = [me, ancestors, codes, over_kv, behind_kv, *base, over_q, own_kv, prior_kv]
    aliases = {}
    if sofar is not None:
        aliases = {len(args): 0}
        args.append(sofar)

    def whole(x):
        return pl.BlockSpec(x.shape, lambda i: (0, 0))

    return pl.pallas_call(
        functools.partial(attend_kernel, pieces, unit, group),
        out_shape=jax.ShapeDtypeStruct((count, width * groups), jnp.bfloat16),
        grid=(1,),
        in_specs=[SM, SM, whole(codes), whole(over_kv), whole(behind_kv)] + [HB] * (len(args) - 5),
        out_specs=pl.BlockSpec((count, width), lambda i: (0, group)),
        scratch_shapes=[
            pltpu.VMEM(((pieces + 1) * unit, width), jnp.bfloat16),
            pltpu.VMEM((count, width), jnp.bfloat16),
            pltpu.VMEM((2 * count, 2 * HEAD_SIZE), jnp.bfloat16),
            pltpu.SemaphoreType.DMA((pieces + 5,)),
        ],
        input_output_aliases=aliases,
        compiler_params=params(24),
        cost_estimate=light(),
        name="attend",
    )(*args)


def attend_padded_kernel(me_ref, anc_ref, code_ref, raw_ref, own_kv, prior_kv, out_ref, q_pl, kv_all):
    count = out_ref.shape[0]
    kv_all[0:count, :] = prior_kv[...]
    kv_all[count : 2 * count, :] = own_kv[...]
    q_pl[...] = matmul(select_rows(code_ref[...], 1, count), raw_ref[...]).astype(jnp.bfloat16)
    attend_core(me_ref[0], anc_ref, q_pl, kv_all, out_ref, kv_all.shape[1] // (2 * HEAD_SIZE))


def attend_padded(me, ancestors, codes, raw, own_kv, prior_kv):
    count, width = own_kv.shape[0], raw.shape[1]
    return pl.pallas_call(
        attend_padded_kernel,
        out_shape=jax.ShapeDtypeStruct((count, width), jnp.bfloat16),
        in_specs=[SM, SM] + [VM] * 4,
        out_specs=VM,
        scratch_shapes=[
            pltpu.VMEM((count, width), jnp.bfloat16),
            pltpu.VMEM((2 * count, own_kv.shape[1]), jnp.bfloat16),
        ],
        compiler_params=params(),
        name="attend_padded",
    )(me, ancestors, codes, raw, own_kv, prior_kv)


def positions(dest_shard, shards):
    onehot = (dest_shard[:, None] == jnp.arange(shards, dtype=jnp.int32)[None, :]).astype(jnp.int32)
    before = jnp.cumsum(onehot, axis=0) - onehot
    return jnp.sum(before * onehot, axis=1)


def exchange(source, index, total):
    buffer = jnp.zeros((total,) + source.shape[1:], source.dtype).at[index].set(source, mode="drop")
    return lax.all_to_all(buffer, "seq", split_axis=0, concat_axis=0, tiled=True)


def from_behind(block):
    n = lax.axis_size("seq")
    return lax.ppermute(block, "seq", [(i, i + 1) for i in range(n - 1)])


def swap(block, r):
    n = lax.axis_size("seq")
    return lax.ppermute(block, "seq", [(i, i ^ r) for i in range(n)])


def padded_plan(me, queries, keys, values, dest_shard, dest_slot, ancestors):
    count = queries.shape[0]
    shards = lax.axis_size("seq")
    capacity = 2 * count // shards
    total = shards * capacity
    index = dest_shard * capacity + positions(dest_shard, shards)
    kv = exchange(jnp.concatenate([keys, values], axis=1), index, total)
    raw = exchange(queries, index, total)
    code = exchange(dest_slot + 1, index, total)
    slots = jnp.where(code > 0, code - 1, count)
    own_kv = jnp.zeros((count, kv.shape[1]), kv.dtype).at[slots].set(kv, mode="drop")
    prior_kv = from_behind(own_kv)
    return attend_padded(me, ancestors, code.reshape(1, total), raw, own_kv, prior_kv)


def after(block, *done):
    return lax.optimization_barrier((block, *done))[0]


class Line:
    def __init__(self, depth):
        self.depth, self.done = depth, []

    def send(self, move, block, *also):
        wait = self.done[-self.depth : len(self.done) - self.depth + 1]
        self.done.append(move(after(block, *wait, *also)))
        return self.done[-1]

    def swap(self, block, r, *also):
        return self.send(lambda x: swap(x, r), block, *also)


def swap_plan(me, queries, keys, values, dest_shard, dest_slot, ancestors):
    count = queries.shape[0]
    shards = lax.axis_size("seq")
    unit = count // shards
    groups = keys.shape[1] // HEAD_SIZE
    kv_blocks, over, index = pack_kv(me, dest_shard, dest_slot, keys, values, queries, shards, unit)
    cuts = [1] * 4 + [groups] * 4
    q_blocks = pack_q(index, queries, unit, cuts)
    line = Line(5)
    got_kv = [kv_blocks[0]] + [None] * 7
    got_q = [q_blocks[0] * groups] + [[None] * groups for _ in range(7)]

    def kv(r, *also):
        got_kv[r] = line.swap(kv_blocks[r], r, *also)

    def q(r, g=None):
        if g is None:
            got_q[r] = [line.swap(q_blocks[r][0], r)] * groups
        else:
            got_q[r][g] = line.swap(q_blocks[r][g], r)

    first = line.swap(over, 4)
    for r in (4, 5, 6, 7):
        kv(r)
    kv(1, q_blocks[0][0])
    kv(2)
    q(4, 0)
    kv(3)
    q(5, 0)
    second = [line.swap(over, 2), line.swap(first, 2)]
    q(6, 0)
    own_kv, codes = place_kv(got_kv, unit, count)
    prior_kv = line.send(from_behind, own_kv)
    q(7, 0)
    keep, send = pick_over(me, [over, first, *second], unit)
    last = line.swap(send, 1)
    over_q, over_kv = merge_over(keep, last, unit, own_kv.shape[1])
    for r in (1, 2, 3):
        q(r)
    q(4, 1)
    behind_kv = line.send(from_behind, over_kv)
    q(5, 1)
    q(6, 1)
    q(7, 1)
    result = None
    for g in range(groups):
        result = attend(
            me,
            ancestors,
            codes,
            over_kv,
            behind_kv,
            [pieces[g] for pieces in got_q],
            over_q,
            own_kv,
            prior_kv,
            unit,
            g,
            groups,
            result,
        )
    flag = crowded(got_kv, shards, unit)[0, 0]
    args = (queries, keys, values, dest_shard, dest_slot, ancestors)
    return lax.cond(flag > 0, lambda: padded_plan(me, *args), lambda: result)


def local(queries, keys, values, dest_shard, dest_slot, ancestors):
    shards = lax.axis_size("seq")
    me = lax.axis_index("seq").astype(jnp.int32).reshape(1)
    plan = swap_plan if shards == 8 and queries.shape[0] % (16 * shards) == 0 else padded_plan
    return plan(me, queries, keys, values, dest_shard, dest_slot, ancestors)


def solution(mesh):
    rows = P(("groups", "seq"))
    heads = P(("groups", "seq"), "head")
    return jax.shard_map(
        local,
        mesh=mesh,
        in_specs=(heads, heads, heads, rows, rows, P(("groups", "seq"), None)),
        out_specs=heads,
        check_vma=False,
    )
```

```python
import functools
import math

import jax
import jax.numpy as jnp
from jax import lax
from jax.experimental import pallas as pl
from jax.experimental.pallas import tpu as pltpu
from jax.sharding import PartitionSpec as P

HEAD_SIZE = 128
META = 8
RADIX = 32
NO_DEST = 255.0
NEG = -1e30

VM = pl.BlockSpec(memory_space=pltpu.VMEM)
SM = pl.BlockSpec(memory_space=pltpu.SMEM)
HB = pl.BlockSpec(memory_space=pl.ANY)


def light():
    return pl.CostEstimate(flops=0, bytes_accessed=0, transcendentals=0)


def params(mebibytes=56):
    return pltpu.CompilerParams(vmem_limit_bytes=mebibytes * 1024 * 1024)


def iota(shape, axis):
    return lax.broadcasted_iota(jnp.int32, shape, axis)


def matmul(a, b):
    return jnp.dot(a, b, preferred_element_type=jnp.float32)


def matmul_nt(a, b):
    return lax.dot_general(a, b, (((1,), (1,)), ((), ())), preferred_element_type=jnp.float32)


def select_rows(index, start, rows, dtype=jnp.bfloat16):
    return (iota((rows, index.shape[1]), 0) + start == index).astype(dtype)


def pack_kv_kernel(shards, unit, dest_ref, slot_ref, k_ref, v_ref, q_ref, blocks, over, index_ref):
    count, kv = k_ref.shape
    dest = dest_ref[...].reshape(1, count)
    code = slot_ref[...].reshape(1, count) + 1
    onehot = (iota((shards, count), 0) == dest).astype(jnp.bfloat16)
    earlier = (iota((count, count), 0) < iota((count, count), 1)).astype(jnp.bfloat16)
    before = matmul(onehot, earlier)
    position = jnp.sum(before * onehot.astype(jnp.float32), axis=0, keepdims=True).astype(jnp.int32)
    base = position < unit
    index = jnp.where(base, dest * unit + position, -1)
    index_ref[...] = index
    over_index = jnp.where(base, -1, position - unit)
    totals = matmul_nt(jnp.ones((META, count), jnp.bfloat16), onehot)
    flags = jnp.where(iota((META, shards), 0) == 2, (totals > unit + 0.5).astype(jnp.float32), 0.0)
    over_dest = jnp.max(jnp.where(base, -1, dest))
    over_value = jnp.where(over_dest < 0, NO_DEST, over_dest.astype(jnp.float32))

    row = iota((META, count), 0)
    codes = jnp.where(row == 0, code // RADIX, jnp.where(row == 1, code % RADIX, 0))
    codes = codes.astype(jnp.float32).astype(jnp.bfloat16)

    picked = select_rows(index, 0, count)
    k_rows = matmul(picked, k_ref[...]).astype(jnp.bfloat16)
    v_rows = matmul(picked, v_ref[...]).astype(jnp.bfloat16)
    sent = matmul_nt(codes, picked)
    step = unit + META
    for d in range(shards):
        rows = slice(d * unit, (d + 1) * unit)
        blocks[d * step : d * step + unit, 0:kv] = k_rows[rows]
        blocks[d * step : d * step + unit, kv : 2 * kv] = v_rows[rows]
        meta = jnp.concatenate(
            [sent[:, rows], flags, jnp.zeros((META, 2 * kv - unit - shards), jnp.float32)], axis=1
        )
        blocks[d * step + unit : (d + 1) * step, :] = meta.astype(jnp.bfloat16)
    picked = select_rows(over_index, 0, unit)
    width = q_ref.shape[1]
    over[0:unit, 0:width] = matmul(picked, q_ref[...]).astype(jnp.bfloat16)
    over[0:unit, width : width + kv] = matmul(picked, k_ref[...]).astype(jnp.bfloat16)
    over[0:unit, width + kv : width + 2 * kv] = matmul(picked, v_ref[...]).astype(jnp.bfloat16)
    full = width + 2 * kv
    sent = matmul_nt(codes, picked)
    meta = jnp.concatenate([sent, jnp.zeros((META, full - unit), jnp.float32)], axis=1)
    meta = jnp.where(iota((META, full), 0) == 2, over_value, meta)
    over[unit : unit + META, :] = meta.astype(jnp.bfloat16)


def pack_kv(dest, slot, keys, values, queries, shards, unit):
    width = 2 * keys.shape[1]
    full = width + queries.shape[1]
    shapes = [
        jax.ShapeDtypeStruct((shards * (unit + META), width), jnp.bfloat16),
        jax.ShapeDtypeStruct((unit + META, full), jnp.bfloat16),
        jax.ShapeDtypeStruct((1, keys.shape[0]), jnp.int32),
    ]
    return pl.pallas_call(
        functools.partial(pack_kv_kernel, shards, unit),
        out_shape=shapes,
        in_specs=[VM] * 5,
        out_specs=[VM] * 3,
        compiler_params=params(16),
        cost_estimate=light(),
        name="pack_kv",
    )(dest, slot, keys, values, queries)


def pack_q_kernel(index_ref, q_ref, out_ref):
    picked = select_rows(index_ref[...], 0, q_ref.shape[0])
    out_ref[...] = matmul(picked, q_ref[...]).astype(jnp.bfloat16)


def pack_q(index, queries):
    return pl.pallas_call(
        pack_q_kernel,
        out_shape=jax.ShapeDtypeStruct(queries.shape, jnp.bfloat16),
        in_specs=[VM, VM],
        out_specs=VM,
        compiler_params=params(12),
        cost_estimate=light(),
        name="pack_q",
    )(index, queries)


def pick_over_kernel(unit, me_ref, a_ref, b_ref, c_ref, d_ref, keep_ref, send_ref):
    me = me_ref[0].astype(jnp.float32)
    other = (me_ref[0] ^ 1).astype(jnp.float32)
    keep = jnp.zeros(keep_ref.shape, jnp.float32)
    send = jnp.zeros(keep_ref.shape, jnp.float32)
    for ref in (a_ref, b_ref, c_ref, d_ref):
        block = ref[...].astype(jnp.float32)
        target = block[unit + 2 : unit + 3, :]
        keep = jnp.where(target == me, block, keep)
        send = jnp.where(target == other, block, send)
    keep_ref[...] = keep.astype(jnp.bfloat16)
    send_ref[...] = send.astype(jnp.bfloat16)


def pick_over(me, held, unit):
    return pl.pallas_call(
        functools.partial(pick_over_kernel, unit),
        out_shape=[jax.ShapeDtypeStruct(held[0].shape, jnp.bfloat16)] * 2,
        in_specs=[SM] + [VM] * 4,
        out_specs=[VM, VM],
        compiler_params=params(8),
        cost_estimate=light(),
        name="pick_over",
    )(me, *held)


def decode(meta, unit):
    meta = meta.astype(jnp.float32)
    return (meta[0:1, 0:unit] * RADIX + meta[1:2, 0:unit]).astype(jnp.int32)


def place_kv_kernel(shards, unit, got_ref, placed_ref, codes_ref, crowd_ref):
    step = unit + META
    count = placed_ref.shape[0]
    metas = [got_ref[s * step + unit : (s + 1) * step, 0:HEAD_SIZE] for s in range(shards)]
    code = jnp.concatenate([decode(meta, unit) for meta in metas], axis=1)
    codes_ref[...] = code
    rows = jnp.concatenate([got_ref[s * step : s * step + unit, :] for s in range(shards)], axis=0)
    placed_ref[...] = matmul(select_rows(code, 1, count), rows).astype(jnp.bfloat16)
    by_dest = jnp.zeros((1, shards), jnp.float32)
    most = jnp.zeros((1, 1), jnp.float32)
    for meta in metas:
        flags = meta[2:3, unit : unit + shards].astype(jnp.float32)
        by_dest += flags
        most = jnp.maximum(most, jnp.sum(flags, axis=1, keepdims=True))
    most = jnp.maximum(most, jnp.max(by_dest, axis=1, keepdims=True))
    crowd_ref[...] = jnp.broadcast_to((most > 1.5).astype(jnp.int32), crowd_ref.shape)


def place_kv(got, shards, unit):
    count = shards * unit
    return pl.pallas_call(
        functools.partial(place_kv_kernel, shards, unit),
        out_shape=[
            jax.ShapeDtypeStruct((count, got.shape[1]), jnp.bfloat16),
            jax.ShapeDtypeStruct((1, count), jnp.int32),
            jax.ShapeDtypeStruct((8, 128), jnp.int32),
        ],
        in_specs=[VM],
        out_specs=[VM, VM, VM],
        compiler_params=params(10),
        cost_estimate=light(),
        name="place_kv",
    )(got)


def merge_over_kernel(a_ref, b_ref, q_ref, kv_ref):
    rows, width = q_ref.shape
    q_ref[...] = a_ref[0:rows, 0:width] + b_ref[0:rows, 0:width]
    kv_ref[...] = a_ref[:, width:] + b_ref[:, width:]
    kv_ref[rows:, 0:HEAD_SIZE] = a_ref[rows:, 0:HEAD_SIZE] + b_ref[rows:, 0:HEAD_SIZE]


def merge_over(kept, got, unit, kv_width):
    width = kept.shape[1] - kv_width
    return pl.pallas_call(
        merge_over_kernel,
        out_shape=[
            jax.ShapeDtypeStruct((unit, width), jnp.bfloat16),
            jax.ShapeDtypeStruct((unit + META, kv_width), jnp.bfloat16),
        ],
        in_specs=[VM, VM],
        out_specs=[VM, VM],
        compiler_params=params(4),
        cost_estimate=light(),
        name="merge_over",
    )(kept, got)


def attend_core(shard, anc_ref, q_pl, kv_all, out_ref, groups):
    count, width = out_ref.shape
    block_count = anc_ref.shape[0]
    size = count // block_count
    ratio = width // groups // HEAD_SIZE
    window = (block_count + 1) * size
    scale = math.log2(math.e) / math.sqrt(HEAD_SIZE)
    lane = iota((size, window), 1)
    for b in range(block_count):
        first = (shard - 1) * block_count + b
        key_block = lane // size + first
        seen = lane < 0
        for a in range(anc_ref.shape[1]):
            seen = seen | (key_block == anc_ref[b, a])
        own = lane >= block_count * size
        causal = lane - block_count * size <= iota((size, window), 0)
        seen = (seen & (lane < block_count * size)) | (own & causal)
        bias = jnp.where(seen, 0.0, NEG)
        for g in range(groups):
            columns = [(g * ratio + h) * HEAD_SIZE for h in range(ratio)]
            q = jnp.concatenate(
                [q_pl[b * size : (b + 1) * size, c : c + HEAD_SIZE] for c in columns], axis=0
            )
            k = kv_all[b * size : b * size + window, g * HEAD_SIZE : (g + 1) * HEAD_SIZE]
            v = kv_all[
                b * size : b * size + window,
                (groups + g) * HEAD_SIZE : (groups + g + 1) * HEAD_SIZE,
            ]
            scores = (matmul_nt(q, k) * scale).reshape(ratio, size, window) + bias[None]
            scores = scores.reshape(ratio * size, window)
            peak = jnp.max(scores, axis=1, keepdims=True)
            expo = jnp.exp2(scores - peak)
            total = jnp.sum(expo, axis=1, keepdims=True)
            weights = (expo * (1.0 / total)).astype(jnp.bfloat16)
            output = matmul(weights, v).astype(jnp.bfloat16)
            for h, c in enumerate(columns):
                out_ref[b * size : (b + 1) * size, c : c + HEAD_SIZE] = output[h * size : (h + 1) * size]


def attend_kernel(unit, groups, me_ref, anc_ref, code_ref, over_ref, behind_ref, *refs):
    base, over_q, own_kv, prior_kv, out_ref, raw, q_pl, kv_all, sems = refs
    count, width = out_ref.shape
    copies = [
        pltpu.make_async_copy(base, raw.at[pl.ds(0, count), :], sems.at[0]),
        pltpu.make_async_copy(over_q, raw.at[pl.ds(count, unit), :], sems.at[1]),
        pltpu.make_async_copy(prior_kv, kv_all.at[pl.ds(0, count), :], sems.at[2]),
        pltpu.make_async_copy(own_kv, kv_all.at[pl.ds(count, count), :], sems.at[3]),
    ]
    for c in copies:
        c.start()
    own_over = decode(over_ref[unit : unit + META, :], unit)
    behind_over = decode(behind_ref[unit : unit + META, :], unit)
    onehot = select_rows(jnp.concatenate([code_ref[...], own_over], axis=1), 1, count)
    for c in copies:
        c.wait()
    q_pl[...] = matmul(onehot, raw[...]).astype(jnp.bfloat16)
    for j, (code, ref) in enumerate(((behind_over, behind_ref), (own_over, over_ref))):
        rows = matmul(select_rows(code, 1, count), ref[0:unit, :]).astype(jnp.bfloat16)
        kv_all[j * count : (j + 1) * count, :] += rows
    attend_core(me_ref[0], anc_ref, q_pl, kv_all, out_ref, groups)


def attend(me, ancestors, codes, over_kv, behind_kv, base, over_q, own_kv, prior_kv, unit):
    count, width = base.shape
    groups = own_kv.shape[1] // (2 * HEAD_SIZE)
    return pl.pallas_call(
        functools.partial(attend_kernel, unit, groups),
        out_shape=jax.ShapeDtypeStruct((count, width), jnp.bfloat16),
        in_specs=[SM, SM, VM, VM, VM] + [HB] * 4,
        out_specs=VM,
        scratch_shapes=[
            pltpu.VMEM((count + unit, width), jnp.bfloat16),
            pltpu.VMEM((count, width), jnp.bfloat16),
            pltpu.VMEM((2 * count, own_kv.shape[1]), jnp.bfloat16),
            pltpu.SemaphoreType.DMA((4,)),
        ],
        compiler_params=params(28),
        cost_estimate=light(),
        name="attend",
    )(me, ancestors, codes, over_kv, behind_kv, base, over_q, own_kv, prior_kv)


def attend_padded_kernel(me_ref, anc_ref, code_ref, raw_ref, own_kv, prior_kv, out_ref, q_pl, kv_all):
    count = out_ref.shape[0]
    kv_all[0:count, :] = prior_kv[...]
    kv_all[count : 2 * count, :] = own_kv[...]
    q_pl[...] = matmul(select_rows(code_ref[...], 1, count), raw_ref[...]).astype(jnp.bfloat16)
    attend_core(me_ref[0], anc_ref, q_pl, kv_all, out_ref, kv_all.shape[1] // (2 * HEAD_SIZE))


def attend_padded(me, ancestors, codes, raw, own_kv, prior_kv):
    count, width = own_kv.shape[0], raw.shape[1]
    return pl.pallas_call(
        attend_padded_kernel,
        out_shape=jax.ShapeDtypeStruct((count, width), jnp.bfloat16),
        in_specs=[SM, SM] + [VM] * 4,
        out_specs=VM,
        scratch_shapes=[
            pltpu.VMEM((count, width), jnp.bfloat16),
            pltpu.VMEM((2 * count, own_kv.shape[1]), jnp.bfloat16),
        ],
        compiler_params=params(),
        name="attend_padded",
    )(me, ancestors, codes, raw, own_kv, prior_kv)


def positions(dest_shard, shards):
    onehot = (dest_shard[:, None] == jnp.arange(shards, dtype=jnp.int32)[None, :]).astype(jnp.int32)
    before = jnp.cumsum(onehot, axis=0) - onehot
    return jnp.sum(before * onehot, axis=1)


def exchange(source, index, total):
    buffer = jnp.zeros((total,) + source.shape[1:], source.dtype).at[index].set(source, mode="drop")
    return lax.all_to_all(buffer, "seq", split_axis=0, concat_axis=0, tiled=True)


def from_behind(block):
    n = lax.axis_size("seq")
    return lax.ppermute(block, "seq", [(i, i + 1) for i in range(n - 1)])


def swap(block, r):
    n = lax.axis_size("seq")
    return lax.ppermute(block, "seq", [(i, i ^ r) for i in range(n)])


def padded_plan(me, queries, keys, values, dest_shard, dest_slot, ancestors):
    count = queries.shape[0]
    shards = lax.axis_size("seq")
    capacity = 2 * count // shards
    total = shards * capacity
    index = dest_shard * capacity + positions(dest_shard, shards)
    kv = exchange(jnp.concatenate([keys, values], axis=1), index, total)
    raw = exchange(queries, index, total)
    code = exchange(dest_slot + 1, index, total)
    slots = jnp.where(code > 0, code - 1, count)
    own_kv = jnp.zeros((count, kv.shape[1]), kv.dtype).at[slots].set(kv, mode="drop")
    prior_kv = from_behind(own_kv)
    return attend_padded(me, ancestors, code.reshape(1, total), raw, own_kv, prior_kv)


def after(block, *done):
    return lax.optimization_barrier((block, *done))[0]


def all_to_all(blocks):
    return lax.all_to_all(blocks, "seq", split_axis=0, concat_axis=0, tiled=True)


def swap_plan(me, queries, keys, values, dest_shard, dest_slot, ancestors):
    count = queries.shape[0]
    shards = lax.axis_size("seq")
    unit = count // shards
    kv_blocks, over, index = pack_kv(dest_shard, dest_slot, keys, values, queries, shards, unit)
    got_kv = all_to_all(kv_blocks)
    first = swap(over, 4)
    own_kv, codes, crowd = place_kv(got_kv, shards, unit)
    prior_kv = from_behind(own_kv)
    got_q = all_to_all(after(pack_q(index, queries), own_kv, first))
    second = [swap(over, 2), swap(first, 2)]
    keep, send = pick_over(me, [over, first, *second], unit)
    over_q, over_kv = merge_over(keep, swap(send, 1), unit, own_kv.shape[1])
    behind_kv = from_behind(over_kv)
    result = attend(me, ancestors, codes, over_kv, behind_kv, got_q, over_q, own_kv, prior_kv, unit)
    args = (queries, keys, values, dest_shard, dest_slot, ancestors)
    return lax.cond(crowd[0, 0] > 0, lambda: padded_plan(me, *args), lambda: result)


def local(queries, keys, values, dest_shard, dest_slot, ancestors):
    shards = lax.axis_size("seq")
    me = lax.axis_index("seq").astype(jnp.int32).reshape(1)
    plan = swap_plan if shards == 8 and queries.shape[0] % (16 * shards) == 0 else padded_plan
    return plan(me, queries, keys, values, dest_shard, dest_slot, ancestors)


def solution(mesh):
    rows = P(("groups", "seq"))
    heads = P(("groups", "seq"), "head")
    return jax.shard_map(
        local,
        mesh=mesh,
        in_specs=(heads, heads, heads, rows, rows, P(("groups", "seq"), None)),
        out_specs=heads,
        check_vma=False,
    )
```

```python
import functools
import math

import jax
import jax.numpy as jnp
from jax import lax
from jax.experimental import pallas as pl
from jax.experimental.pallas import tpu as pltpu
from jax.sharding import PartitionSpec as P

HEAD_SIZE = 128
PIECE = 8
RADIX = 32
NO_DEST = 255.0
NEG = -1e30

VM = pl.BlockSpec(memory_space=pltpu.VMEM)
SM = pl.BlockSpec(memory_space=pltpu.SMEM)
HB = pl.BlockSpec(memory_space=pl.ANY)


def light():
    return pl.CostEstimate(flops=0, bytes_accessed=0, transcendentals=0)


def params(mebibytes=56):
    return pltpu.CompilerParams(vmem_limit_bytes=mebibytes * 1024 * 1024)


def iota(shape, axis):
    return lax.broadcasted_iota(jnp.int32, shape, axis)


def matmul(a, b):
    return jnp.dot(a, b, preferred_element_type=jnp.float32)


def matmul_nt(a, b):
    return lax.dot_general(a, b, (((1,), (1,)), ((), ())), preferred_element_type=jnp.float32)


def select_rows(index, start, rows, dtype=jnp.bfloat16):
    return (iota((rows, index.shape[1]), 0) + start == index).astype(dtype)


def strips(width, kv_width):
    return [(c, min(c + kv_width, width)) for c in range(0, width, kv_width)]


def pack_kv_kernel(shards, unit, me_ref, dest_ref, slot_ref, k_ref, v_ref, q_ref, *outs):
    blocks, index_ref = outs[:shards], outs[shards]
    count, kv = k_ref.shape
    dest = dest_ref[...].reshape(1, count)
    code = slot_ref[...].reshape(1, count) + 1
    onehot = (iota((shards, count), 0) == dest).astype(jnp.bfloat16)
    earlier = (iota((count, count), 0) < iota((count, count), 1)).astype(jnp.bfloat16)
    before = matmul(onehot, earlier)
    position = jnp.sum(before * onehot.astype(jnp.float32), axis=0, keepdims=True).astype(jnp.int32)
    base = position < unit
    index = jnp.where(base, ((dest - me_ref[0]) & (shards - 1)) * unit + position, -1)
    index_ref[...] = index
    over_index = jnp.where(base, -1, position - unit)
    totals = matmul_nt(jnp.ones((PIECE, count), jnp.bfloat16), onehot)
    flags = jnp.where(iota((PIECE, shards), 0) == 2, (totals > unit + 0.5).astype(jnp.float32), 0.0)
    flags = jnp.concatenate([flags, jnp.zeros((PIECE, unit - shards), jnp.float32)], axis=1)
    over_dest = jnp.max(jnp.where(base, -1, dest))
    over_value = jnp.where(over_dest < 0, NO_DEST, over_dest.astype(jnp.float32))

    row = iota((PIECE, count), 0)
    codes = jnp.where(row == 0, code // RADIX, jnp.where(row == 1, code % RADIX, 0))
    codes = codes.astype(jnp.float32).astype(jnp.bfloat16)

    picked = select_rows(index, 0, count)
    k_rows = matmul(picked, k_ref[...]).astype(jnp.bfloat16)
    v_rows = matmul(picked, v_ref[...]).astype(jnp.bfloat16)
    sent = matmul_nt(codes, picked)
    picked = select_rows(over_index, 0, unit)
    over_k = matmul(picked, k_ref[...])
    over_v = matmul(picked, v_ref[...])
    over_q = matmul(picked, q_ref[...])
    over_sent = matmul_nt(codes, picked)
    over_sent = jnp.where(iota((PIECE, unit), 0) == 2, over_value, over_sent)
    empty = jnp.zeros((PIECE, unit), jnp.float32)
    for r in range(shards):
        rows = slice(r * unit, (r + 1) * unit)
        blocks[r][0:unit, 0:kv] = k_rows[rows]
        blocks[r][0:unit, kv : 2 * kv] = v_rows[rows]
        piece = slice(r * PIECE, (r + 1) * PIECE)
        meta = jnp.concatenate([sent[:, rows], flags, over_sent, empty], axis=1)
        tail = [jnp.concatenate([over_k[piece], over_v[piece]], axis=1)]
        for start, stop in strips(over_q.shape[1], 2 * kv):
            tail.append(over_q[piece, start:stop])
        tail[-1] = jnp.concatenate([tail[-1], meta], axis=1)
        blocks[r][unit:, :] = jnp.concatenate(tail, axis=0).astype(jnp.bfloat16)


def pack_kv(me, dest, slot, keys, values, queries, shards, unit):
    kv_width = 2 * keys.shape[1]
    rows = unit + PIECE * (1 + len(strips(queries.shape[1], kv_width)))
    shapes = [jax.ShapeDtypeStruct((rows, kv_width), jnp.bfloat16)] * shards
    shapes += [jax.ShapeDtypeStruct((1, keys.shape[0]), jnp.int32)]
    outs = pl.pallas_call(
        functools.partial(pack_kv_kernel, shards, unit),
        out_shape=shapes,
        in_specs=[SM] + [VM] * 5,
        out_specs=[VM] * len(shapes),
        compiler_params=params(16),
        cost_estimate=light(),
        name="pack_kv",
    )(me, dest, slot, keys, values, queries)
    return outs[:shards], outs[shards]


def pack_q_kernel(unit, index_ref, q_ref, *blocks):
    for r, block in enumerate(blocks):
        picked = select_rows(index_ref[...], r * unit, unit)
        block[0:unit, :] = matmul(picked, q_ref[...]).astype(jnp.bfloat16)


def pack_q(index, queries, shards, unit):
    return pl.pallas_call(
        functools.partial(pack_q_kernel, unit),
        out_shape=[jax.ShapeDtypeStruct((unit + 2 * PIECE, queries.shape[1]), jnp.bfloat16)] * shards,
        in_specs=[VM, VM],
        out_specs=[VM] * shards,
        compiler_params=params(12),
        cost_estimate=light(),
        name="pack_q",
    )(index, queries)


def by_lane(parts, row):
    lane = iota((1, parts[0].shape[1]), 1) // PIECE
    total = jnp.zeros(lane.shape, jnp.float32)
    for r, part in enumerate(parts):
        total += jnp.where(lane == r, part[row : row + 1, :], 0.0)
    return total


def decode(high, low):
    return (high * RADIX + low).astype(jnp.int32)


def relay_kernel(shards, unit, me_ref, *refs):
    got = refs[:shards]
    placed_ref, codes_ref, crowd_ref = refs[2 * shards : 2 * shards + 3]
    blocks = refs[2 * shards + 3 : 3 * shards + 3]
    tails, sems = refs[3 * shards + 3 :]
    count, kv_width = placed_ref.shape
    width = tails.shape[2]
    cuts = strips(width, kv_width)
    meta_at = cuts[-1][1] - cuts[-1][0]
    ends = [ref[unit:, :].astype(jnp.float32) for ref in got]
    metas = [end[-PIECE:, meta_at:] for end in ends]

    over = [meta[:, 2 * unit : 3 * unit] for meta in metas]
    dest = by_lane(over, 2).astype(jnp.int32)
    part = iota(dest.shape, 1) % PIECE
    to = jnp.where(dest < shards, ((dest - me_ref[0]) & (shards - 1)) * PIECE + part, -1)
    behind = jnp.where(dest < shards - 1, ((dest + 1 - me_ref[0]) & (shards - 1)) * PIECE + part, -1)
    to, behind = select_rows(to, 0, shards * PIECE), select_rows(behind, 0, shards * PIECE)
    over_kv = jnp.concatenate([end[0:PIECE] for end in ends], axis=0).astype(jnp.bfloat16)
    row = iota((PIECE, unit), 0)
    codes = jnp.where(row == 0, by_lane(over, 0), jnp.where(row == 1, by_lane(over, 1), 0.0)).astype(jnp.bfloat16)
    meta = jnp.concatenate([matmul_nt(codes, to), matmul_nt(codes, behind)], axis=1)
    meta = jnp.concatenate([meta, jnp.zeros((PIECE, width - 2 * kv_width - 2 * unit), jnp.float32)], axis=1)
    to_kv, behind_kv = matmul(to, over_kv), matmul(behind, over_kv)
    to_q = []
    for i, (start, stop) in enumerate(cuts):
        strip = [end[(i + 1) * PIECE : (i + 2) * PIECE, 0 : stop - start] for end in ends]
        to_q.append(matmul(to, jnp.concatenate(strip, axis=0).astype(jnp.bfloat16)))
    to_q = jnp.concatenate(to_q, axis=1)
    copies = []
    for r in range(shards):
        piece = slice(r * PIECE, (r + 1) * PIECE)
        lower = jnp.concatenate([to_kv[piece], behind_kv[piece], meta], axis=1)
        tails[r] = jnp.concatenate([to_q[piece], lower], axis=0).astype(jnp.bfloat16)
        copies.append(pltpu.make_async_copy(tails.at[r], blocks[r].at[pl.ds(unit, 2 * PIECE), :], sems.at[r]))
        copies[-1].start()

    code = jnp.concatenate([decode(meta[0:1, 0:unit], meta[1:2, 0:unit]) for meta in metas], axis=1)
    codes_ref[...] = code
    rows = jnp.concatenate([ref[0:unit, :] for ref in got], axis=0)
    placed_ref[...] = matmul(select_rows(code, 1, count), rows).astype(jnp.bfloat16)
    by_dest = jnp.zeros((1, unit), jnp.float32)
    most = jnp.zeros((1, 1), jnp.float32)
    for meta in metas:
        flags = meta[2:3, unit : 2 * unit]
        by_dest += flags
        most = jnp.maximum(most, jnp.sum(flags, axis=1, keepdims=True))
    most = jnp.maximum(most, jnp.max(by_dest, axis=1, keepdims=True))
    crowd_ref[...] = jnp.broadcast_to((most > 1.5).astype(jnp.int32), crowd_ref.shape)
    for c in copies:
        c.wait()


def relay(me, got, q_blocks, unit):
    shards = len(got)
    count = shards * unit
    shape = q_blocks[0].shape
    outs = pl.pallas_call(
        functools.partial(relay_kernel, shards, unit),
        out_shape=[
            jax.ShapeDtypeStruct((count, got[0].shape[1]), jnp.bfloat16),
            jax.ShapeDtypeStruct((1, count), jnp.int32),
            jax.ShapeDtypeStruct((8, 128), jnp.int32),
        ]
        + [jax.ShapeDtypeStruct(shape, jnp.bfloat16)] * shards,
        in_specs=[SM] + [VM] * shards + [HB] * shards,
        out_specs=[VM] * 3 + [HB] * shards,
        scratch_shapes=[
            pltpu.VMEM((shards, 2 * PIECE, shape[1]), jnp.bfloat16),
            pltpu.SemaphoreType.DMA((shards,)),
        ],
        input_output_aliases={1 + shards + r: 3 + r for r in range(shards)},
        compiler_params=params(10),
        cost_estimate=light(),
        name="relay",
    )(me, *got, *q_blocks)
    return outs[0], outs[1], outs[2], outs[3:]


def attend_core(shard, anc_ref, q_pl, kv_all, out_ref, groups):
    count, width = out_ref.shape
    block_count = anc_ref.shape[0]
    size = count // block_count
    ratio = width // groups // HEAD_SIZE
    window = (block_count + 1) * size
    scale = math.log2(math.e) / math.sqrt(HEAD_SIZE)
    lane = iota((size, window), 1)
    for b in range(block_count):
        first = (shard - 1) * block_count + b
        key_block = lane // size + first
        seen = lane < 0
        for a in range(anc_ref.shape[1]):
            seen = seen | (key_block == anc_ref[b, a])
        own = lane >= block_count * size
        causal = lane - block_count * size <= iota((size, window), 0)
        seen = (seen & (lane < block_count * size)) | (own & causal)
        bias = jnp.where(seen, 0.0, NEG)
        for g in range(groups):
            columns = [(g * ratio + h) * HEAD_SIZE for h in range(ratio)]
            q = jnp.concatenate(
                [q_pl[b * size : (b + 1) * size, c : c + HEAD_SIZE] for c in columns], axis=0
            )
            k = kv_all[b * size : b * size + window, g * HEAD_SIZE : (g + 1) * HEAD_SIZE]
            v = kv_all[
                b * size : b * size + window,
                (groups + g) * HEAD_SIZE : (groups + g + 1) * HEAD_SIZE,
            ]
            scores = (matmul_nt(q, k) * scale).reshape(ratio, size, window) + bias[None]
            scores = scores.reshape(ratio * size, window)
            peak = jnp.max(scores, axis=1, keepdims=True)
            expo = jnp.exp2(scores - peak)
            total = jnp.sum(expo, axis=1, keepdims=True)
            weights = (expo * (1.0 / total)).astype(jnp.bfloat16)
            output = matmul(weights, v).astype(jnp.bfloat16)
            for h, c in enumerate(columns):
                out_ref[b * size : (b + 1) * size, c : c + HEAD_SIZE] = output[h * size : (h + 1) * size]


def attend_kernel(shards, unit, groups, me_ref, anc_ref, code_ref, *refs):
    got, own_kv, prior_kv = refs[:shards], *refs[shards : shards + 2]
    out_ref, raw, tails, q_pl, kv_all, sems = refs[shards + 2 :]
    count, width = out_ref.shape
    kv_width = own_kv.shape[1]
    copies = []

    def fetch(source, target):
        copies.append(pltpu.make_async_copy(source, target, sems.at[len(copies)]))
        copies[-1].start()

    for r, ref in enumerate(got):
        fetch(ref.at[pl.ds(unit, 2 * PIECE), :], tails.at[r])
        fetch(ref.at[pl.ds(0, unit), :], raw.at[pl.ds(r * unit, unit), :])
    fetch(prior_kv, kv_all.at[pl.ds(0, count), :])
    fetch(own_kv, kv_all.at[pl.ds(count, count), :])
    for c in copies:
        c.wait()
    ends = [tails[r].astype(jnp.float32) for r in range(shards)]
    metas = [end[PIECE:, 2 * kv_width :] for end in ends]
    own = [meta[:, 0:unit] for meta in metas]
    behind = [meta[:, unit : 2 * unit] for meta in metas]
    own = decode(by_lane(own, 0), by_lane(own, 1))
    behind = decode(by_lane(behind, 0), by_lane(behind, 1))
    raw[count:, :] = jnp.concatenate([end[0:PIECE] for end in ends], axis=0).astype(jnp.bfloat16)
    onehot = select_rows(jnp.concatenate([code_ref[...], own], axis=1), 1, count)
    q_pl[...] = matmul(onehot, raw[...]).astype(jnp.bfloat16)
    for j, (code, start) in enumerate(((behind, kv_width), (own, 0))):
        rows = jnp.concatenate([end[PIECE:, start : start + kv_width] for end in ends], axis=0)
        rows = matmul(select_rows(code, 1, count), rows.astype(jnp.bfloat16))
        kv_all[j * count : (j + 1) * count, :] += rows.astype(jnp.bfloat16)
    attend_core(me_ref[0], anc_ref, q_pl, kv_all, out_ref, groups)


def attend(me, ancestors, codes, got, own_kv, prior_kv, unit):
    shards = len(got)
    count, width = shards * unit, got[0].shape[1]
    groups = own_kv.shape[1] // (2 * HEAD_SIZE)
    return pl.pallas_call(
        functools.partial(attend_kernel, shards, unit, groups),
        out_shape=jax.ShapeDtypeStruct((count, width), jnp.bfloat16),
        in_specs=[SM, SM, VM] + [HB] * (shards + 2),
        out_specs=VM,
        scratch_shapes=[
            pltpu.VMEM((count + shards * PIECE, width), jnp.bfloat16),
            pltpu.VMEM((shards, 2 * PIECE, width), jnp.bfloat16),
            pltpu.VMEM((count, width), jnp.bfloat16),
            pltpu.VMEM((2 * count, own_kv.shape[1]), jnp.bfloat16),
            pltpu.SemaphoreType.DMA((2 * shards + 2,)),
        ],
        compiler_params=params(28),
        cost_estimate=light(),
        name="attend",
    )(me, ancestors, codes, *got, own_kv, prior_kv)


def attend_padded_kernel(me_ref, anc_ref, code_ref, raw_ref, own_kv, prior_kv, out_ref, q_pl, kv_all):
    count = out_ref.shape[0]
    kv_all[0:count, :] = prior_kv[...]
    kv_all[count : 2 * count, :] = own_kv[...]
    q_pl[...] = matmul(select_rows(code_ref[...], 1, count), raw_ref[...]).astype(jnp.bfloat16)
    attend_core(me_ref[0], anc_ref, q_pl, kv_all, out_ref, kv_all.shape[1] // (2 * HEAD_SIZE))


def attend_padded(me, ancestors, codes, raw, own_kv, prior_kv):
    count, width = own_kv.shape[0], raw.shape[1]
    return pl.pallas_call(
        attend_padded_kernel,
        out_shape=jax.ShapeDtypeStruct((count, width), jnp.bfloat16),
        in_specs=[SM, SM] + [VM] * 4,
        out_specs=VM,
        scratch_shapes=[
            pltpu.VMEM((count, width), jnp.bfloat16),
            pltpu.VMEM((2 * count, own_kv.shape[1]), jnp.bfloat16),
        ],
        compiler_params=params(),
        name="attend_padded",
    )(me, ancestors, codes, raw, own_kv, prior_kv)


def positions(dest_shard, shards):
    onehot = (dest_shard[:, None] == jnp.arange(shards, dtype=jnp.int32)[None, :]).astype(jnp.int32)
    before = jnp.cumsum(onehot, axis=0) - onehot
    return jnp.sum(before * onehot, axis=1)


def exchange(source, index, total):
    buffer = jnp.zeros((total,) + source.shape[1:], source.dtype).at[index].set(source, mode="drop")
    return lax.all_to_all(buffer, "seq", split_axis=0, concat_axis=0, tiled=True)


def from_behind(block):
    n = lax.axis_size("seq")
    return lax.ppermute(block, "seq", [(i, i + 1) for i in range(n - 1)])


def rotate(block, r):
    n = lax.axis_size("seq")
    return lax.ppermute(block, "seq", [(i, (i + r) % n) for i in range(n)])


def padded_plan(me, queries, keys, values, dest_shard, dest_slot, ancestors):
    count = queries.shape[0]
    shards = lax.axis_size("seq")
    capacity = 2 * count // shards
    total = shards * capacity
    index = dest_shard * capacity + positions(dest_shard, shards)
    kv = exchange(jnp.concatenate([keys, values], axis=1), index, total)
    raw = exchange(queries, index, total)
    code = exchange(dest_slot + 1, index, total)
    slots = jnp.where(code > 0, code - 1, count)
    own_kv = jnp.zeros((count, kv.shape[1]), kv.dtype).at[slots].set(kv, mode="drop")
    prior_kv = from_behind(own_kv)
    return attend_padded(me, ancestors, code.reshape(1, total), raw, own_kv, prior_kv)


def after(block, *done):
    return lax.optimization_barrier((block, *done))[0]


def relay_plan(me, queries, keys, values, dest_shard, dest_slot, ancestors):
    count = queries.shape[0]
    shards = lax.axis_size("seq")
    unit = count // shards
    kv_blocks, index = pack_kv(me, dest_shard, dest_slot, keys, values, queries, shards, unit)
    got_kv = [kv_blocks[0]] + [rotate(kv_blocks[r], r) for r in range(1, shards)]
    q_blocks = pack_q(after(index, got_kv[1]), queries, shards, unit)
    own_kv, codes, crowd, q_blocks = relay(me, got_kv, q_blocks, unit)
    prior_kv = from_behind(own_kv)
    got_q = [q_blocks[0]] + [rotate(q_blocks[r], r) for r in range(1, shards)]
    result = attend(me, ancestors, codes, got_q, own_kv, prior_kv, unit)
    args = (queries, keys, values, dest_shard, dest_slot, ancestors)
    return lax.cond(crowd[0, 0] > 0, lambda: padded_plan(me, *args), lambda: result)


def local(queries, keys, values, dest_shard, dest_slot, ancestors):
    shards = lax.axis_size("seq")
    me = lax.axis_index("seq").astype(jnp.int32).reshape(1)
    plan = relay_plan if queries.shape[0] == 8 * PIECE * shards and shards == 8 else padded_plan
    return plan(me, queries, keys, values, dest_shard, dest_slot, ancestors)


def solution(mesh):
    rows = P(("groups", "seq"))
    heads = P(("groups", "seq"), "head")
    return jax.shard_map(
        local,
        mesh=mesh,
        in_specs=(heads, heads, heads, rows, rows, P(("groups", "seq"), None)),
        out_specs=heads,
        check_vma=False,
    )
```

```python
import functools
import math

import jax
import jax.numpy as jnp
from jax import lax
from jax.experimental import pallas as pl
from jax.experimental.pallas import tpu as pltpu
from jax.sharding import PartitionSpec as P

HEAD_SIZE = 128
PIECE = 8
RADIX = 32
NO_DEST = 255.0
NEG = -1e30

VM = pl.BlockSpec(memory_space=pltpu.VMEM)
SM = pl.BlockSpec(memory_space=pltpu.SMEM)
HB = pl.BlockSpec(memory_space=pl.ANY)


def light():
    return pl.CostEstimate(flops=0, bytes_accessed=0, transcendentals=0)


def params(mebibytes=56):
    return pltpu.CompilerParams(vmem_limit_bytes=mebibytes * 1024 * 1024)


def iota(shape, axis):
    return lax.broadcasted_iota(jnp.int32, shape, axis)


def matmul(a, b):
    return jnp.dot(a, b, preferred_element_type=jnp.float32)


def matmul_nt(a, b):
    return lax.dot_general(a, b, (((1,), (1,)), ((), ())), preferred_element_type=jnp.float32)


def select_rows(index, start, rows, dtype=jnp.bfloat16):
    return (iota((rows, index.shape[1]), 0) + start == index).astype(dtype)


def strips(width, kv_width):
    return [(c, min(c + kv_width, width)) for c in range(0, width, kv_width)]


def pack_kv_kernel(shards, unit, me_ref, dest_ref, slot_ref, k_ref, v_ref, q_ref, *outs):
    blocks, index_ref = outs[:shards], outs[shards]
    count, kv = k_ref.shape
    dest = dest_ref[...].reshape(1, count)
    code = slot_ref[...].reshape(1, count) + 1
    onehot = (iota((shards, count), 0) == dest).astype(jnp.bfloat16)
    earlier = (iota((count, count), 0) < iota((count, count), 1)).astype(jnp.bfloat16)
    before = matmul(onehot, earlier)
    position = jnp.sum(before * onehot.astype(jnp.float32), axis=0, keepdims=True).astype(jnp.int32)
    base = position < unit
    index = jnp.where(base, ((dest - me_ref[0]) & (shards - 1)) * unit + position, -1)
    index_ref[...] = index
    v_index = jnp.where(base, (((dest ^ 1) - me_ref[0]) & (shards - 1)) * unit + position, -1)
    over_index = jnp.where(base, -1, position - unit)
    totals = matmul_nt(jnp.ones((PIECE, count), jnp.bfloat16), onehot)
    flags = jnp.where(iota((PIECE, shards), 0) == 2, (totals > unit + 0.5).astype(jnp.float32), 0.0)
    flags = jnp.concatenate([flags, jnp.zeros((PIECE, unit - shards), jnp.float32)], axis=1)
    over_dest = jnp.max(jnp.where(base, -1, dest))
    over_value = jnp.where(over_dest < 0, NO_DEST, over_dest.astype(jnp.float32))

    row = iota((PIECE, count), 0)
    codes = jnp.where(row == 0, code // RADIX, jnp.where(row == 1, code % RADIX, 0))
    codes = codes.astype(jnp.float32).astype(jnp.bfloat16)

    picked = select_rows(index, 0, count)
    k_rows = matmul(picked, k_ref[...]).astype(jnp.bfloat16)
    sent = matmul_nt(codes, picked)
    picked = select_rows(v_index, 0, count)
    v_rows = matmul(picked, v_ref[...]).astype(jnp.bfloat16)
    v_sent = matmul_nt(codes, picked)
    picked = select_rows(over_index, 0, unit)
    over_k = matmul(picked, k_ref[...])
    over_v = matmul(picked, v_ref[...])
    over_q = matmul(picked, q_ref[...])
    over_sent = matmul_nt(codes, picked)
    over_sent = jnp.where(iota((PIECE, unit), 0) == 2, over_value, over_sent)
    empty = jnp.zeros((PIECE, unit), jnp.float32)
    for r in range(shards):
        rows = slice(r * unit, (r + 1) * unit)
        blocks[r][0:unit, 0:kv] = k_rows[rows]
        blocks[r][0:unit, kv : 2 * kv] = v_rows[rows]
        piece = slice(r * PIECE, (r + 1) * PIECE)
        meta = jnp.concatenate([sent[:, rows], flags + v_sent[:, rows], over_sent, empty], axis=1)
        tail = [jnp.concatenate([over_k[piece], over_v[piece]], axis=1)]
        for start, stop in strips(over_q.shape[1], 2 * kv):
            tail.append(over_q[piece, start:stop])
        tail[-1] = jnp.concatenate([tail[-1], meta], axis=1)
        blocks[r][unit:, :] = jnp.concatenate(tail, axis=0).astype(jnp.bfloat16)


def pack_kv(me, dest, slot, keys, values, queries, shards, unit):
    kv_width = 2 * keys.shape[1]
    rows = unit + PIECE * (1 + len(strips(queries.shape[1], kv_width)))
    shapes = [jax.ShapeDtypeStruct((rows, kv_width), jnp.bfloat16)] * shards
    shapes += [jax.ShapeDtypeStruct((1, keys.shape[0]), jnp.int32)]
    outs = pl.pallas_call(
        functools.partial(pack_kv_kernel, shards, unit),
        out_shape=shapes,
        in_specs=[SM] + [VM] * 5,
        out_specs=[VM] * len(shapes),
        compiler_params=params(16),
        cost_estimate=light(),
        name="pack_kv",
    )(me, dest, slot, keys, values, queries)
    return outs[:shards], outs[shards]


def pack_q_kernel(unit, index_ref, q_ref, *blocks):
    for r, block in enumerate(blocks):
        picked = select_rows(index_ref[...], r * unit, unit)
        block[0:unit, :] = matmul(picked, q_ref[...]).astype(jnp.bfloat16)


def pack_q(index, queries, shards, unit):
    return pl.pallas_call(
        functools.partial(pack_q_kernel, unit),
        out_shape=[jax.ShapeDtypeStruct((unit + 2 * PIECE, queries.shape[1]), jnp.bfloat16)] * shards,
        in_specs=[VM, VM],
        out_specs=[VM] * shards,
        compiler_params=params(12),
        cost_estimate=light(),
        name="pack_q",
    )(index, queries)


def by_lane(parts, row):
    lane = iota((1, parts[0].shape[1]), 1) // PIECE
    total = jnp.zeros(lane.shape, jnp.float32)
    for r, part in enumerate(parts):
        total += jnp.where(lane == r, part[row : row + 1, :], 0.0)
    return total


def decode(high, low):
    return (high * RADIX + low).astype(jnp.int32)


def relay_kernel(shards, unit, me_ref, *refs):
    got = refs[:shards]
    k_out, v_out, codes_ref, crowd_ref = refs[2 * shards : 2 * shards + 4]
    blocks = refs[2 * shards + 4 : 3 * shards + 4]
    tails, sems = refs[3 * shards + 4 :]
    count, half = k_out.shape
    kv_width = 2 * half
    width = tails.shape[2]
    cuts = strips(width, kv_width)
    meta_at = cuts[-1][1] - cuts[-1][0]
    ends = [ref[unit:, :].astype(jnp.float32) for ref in got]
    metas = [end[-PIECE:, meta_at:] for end in ends]

    over = [meta[:, 2 * unit : 3 * unit] for meta in metas]
    dest = by_lane(over, 2).astype(jnp.int32)
    part = iota(dest.shape, 1) % PIECE
    to = jnp.where(dest < shards, ((dest - me_ref[0]) & (shards - 1)) * PIECE + part, -1)
    behind = jnp.where(dest < shards - 1, ((dest + 1 - me_ref[0]) & (shards - 1)) * PIECE + part, -1)
    to, behind = select_rows(to, 0, shards * PIECE), select_rows(behind, 0, shards * PIECE)
    over_kv = jnp.concatenate([end[0:PIECE] for end in ends], axis=0).astype(jnp.bfloat16)
    row = iota((PIECE, unit), 0)
    codes = jnp.where(row == 0, by_lane(over, 0), jnp.where(row == 1, by_lane(over, 1), 0.0)).astype(jnp.bfloat16)
    meta = jnp.concatenate([matmul_nt(codes, to), matmul_nt(codes, behind)], axis=1)
    meta = jnp.concatenate([meta, jnp.zeros((PIECE, width - 2 * kv_width - 2 * unit), jnp.float32)], axis=1)
    to_kv, behind_kv = matmul(to, over_kv), matmul(behind, over_kv)
    to_q = []
    for i, (start, stop) in enumerate(cuts):
        strip = [end[(i + 1) * PIECE : (i + 2) * PIECE, 0 : stop - start] for end in ends]
        to_q.append(matmul(to, jnp.concatenate(strip, axis=0).astype(jnp.bfloat16)))
    to_q = jnp.concatenate(to_q, axis=1)
    copies = []
    for r in range(shards):
        piece = slice(r * PIECE, (r + 1) * PIECE)
        lower = jnp.concatenate([to_kv[piece], behind_kv[piece], meta], axis=1)
        tails[r] = jnp.concatenate([to_q[piece], lower], axis=0).astype(jnp.bfloat16)
        copies.append(pltpu.make_async_copy(tails.at[r], blocks[r].at[pl.ds(unit, 2 * PIECE), :], sems.at[r]))
        copies[-1].start()

    code = jnp.concatenate([decode(meta[0:1, 0:unit], meta[1:2, 0:unit]) for meta in metas], axis=1)
    codes_ref[...] = code
    rows = jnp.concatenate([ref[0:unit, 0:half] for ref in got], axis=0)
    k_out[...] = matmul(select_rows(code, 1, count), rows).astype(jnp.bfloat16)
    code = [decode(meta[0:1, unit : 2 * unit], meta[1:2, unit : 2 * unit]) for meta in metas]
    rows = jnp.concatenate([ref[0:unit, half:] for ref in got], axis=0)
    v_out[...] = matmul(select_rows(jnp.concatenate(code, axis=1), 1, count), rows).astype(jnp.bfloat16)
    by_dest = jnp.zeros((1, unit), jnp.float32)
    most = jnp.zeros((1, 1), jnp.float32)
    for meta in metas:
        flags = meta[2:3, unit : 2 * unit]
        by_dest += flags
        most = jnp.maximum(most, jnp.sum(flags, axis=1, keepdims=True))
    most = jnp.maximum(most, jnp.max(by_dest, axis=1, keepdims=True))
    crowd_ref[...] = jnp.broadcast_to((most > 1.5).astype(jnp.int32), crowd_ref.shape)
    for c in copies:
        c.wait()


def relay(me, got, q_blocks, unit):
    shards = len(got)
    count = shards * unit
    shape = q_blocks[0].shape
    outs = pl.pallas_call(
        functools.partial(relay_kernel, shards, unit),
        out_shape=[
            jax.ShapeDtypeStruct((count, got[0].shape[1] // 2), jnp.bfloat16),
            jax.ShapeDtypeStruct((count, got[0].shape[1] // 2), jnp.bfloat16),
            jax.ShapeDtypeStruct((1, count), jnp.int32),
            jax.ShapeDtypeStruct((8, 128), jnp.int32),
        ]
        + [jax.ShapeDtypeStruct(shape, jnp.bfloat16)] * shards,
        in_specs=[SM] + [VM] * shards + [HB] * shards,
        out_specs=[VM] * 4 + [HB] * shards,
        scratch_shapes=[
            pltpu.VMEM((shards, 2 * PIECE, shape[1]), jnp.bfloat16),
            pltpu.SemaphoreType.DMA((shards,)),
        ],
        input_output_aliases={1 + shards + r: 4 + r for r in range(shards)},
        compiler_params=params(10),
        cost_estimate=light(),
        name="relay",
    )(me, *got, *q_blocks)
    return *outs[:4], outs[4:]


def attend_core(shard, anc_ref, q_pl, kv_all, out_ref, groups):
    count, width = out_ref.shape
    block_count = anc_ref.shape[0]
    size = count // block_count
    ratio = width // groups // HEAD_SIZE
    window = (block_count + 1) * size
    scale = math.log2(math.e) / math.sqrt(HEAD_SIZE)
    lane = iota((size, window), 1)
    for b in range(block_count):
        first = (shard - 1) * block_count + b
        key_block = lane // size + first
        seen = lane < 0
        for a in range(anc_ref.shape[1]):
            seen = seen | (key_block == anc_ref[b, a])
        own = lane >= block_count * size
        causal = lane - block_count * size <= iota((size, window), 0)
        seen = (seen & (lane < block_count * size)) | (own & causal)
        bias = jnp.where(seen, 0.0, NEG)
        for g in range(groups):
            columns = [(g * ratio + h) * HEAD_SIZE for h in range(ratio)]
            q = jnp.concatenate(
                [q_pl[b * size : (b + 1) * size, c : c + HEAD_SIZE] for c in columns], axis=0
            )
            k = kv_all[b * size : b * size + window, g * HEAD_SIZE : (g + 1) * HEAD_SIZE]
            v = kv_all[
                b * size : b * size + window,
                (groups + g) * HEAD_SIZE : (groups + g + 1) * HEAD_SIZE,
            ]
            scores = (matmul_nt(q, k) * scale).reshape(ratio, size, window) + bias[None]
            scores = scores.reshape(ratio * size, window)
            peak = jnp.max(scores, axis=1, keepdims=True)
            expo = jnp.exp2(scores - peak)
            total = jnp.sum(expo, axis=1, keepdims=True)
            weights = (expo * (1.0 / total)).astype(jnp.bfloat16)
            output = matmul(weights, v).astype(jnp.bfloat16)
            for h, c in enumerate(columns):
                out_ref[b * size : (b + 1) * size, c : c + HEAD_SIZE] = output[h * size : (h + 1) * size]


def attend_kernel(shards, unit, groups, me_ref, anc_ref, code_ref, *refs):
    got, (own_k, own_v, prior_k, beside_v, prior_v) = refs[:shards], refs[shards : shards + 5]
    out_ref, raw, tails, q_pl, kv_all, sems = refs[shards + 5 :]
    count, width = out_ref.shape
    half = own_k.shape[1]
    kv_width = 2 * half
    copies = []

    def fetch(source, target):
        copies.append(pltpu.make_async_copy(source, target, sems.at[len(copies)]))
        copies[-1].start()

    for r, ref in enumerate(got):
        fetch(ref.at[pl.ds(unit, 2 * PIECE), :], tails.at[r])
        fetch(ref.at[pl.ds(0, unit), :], raw.at[pl.ds(r * unit, unit), :])
    fetch(prior_k, kv_all.at[pl.ds(0, count), pl.ds(0, half)])
    fetch(own_k, kv_all.at[pl.ds(count, count), pl.ds(0, half)])
    fetch(own_v, kv_all.at[pl.ds(count, count), pl.ds(half, half)])
    odd = me_ref[0] & 1

    @pl.when(odd == 1)
    def _():
        kv_all[0:count, half:] = beside_v[...]

    @pl.when(odd == 0)
    def _():
        kv_all[0:count, half:] = prior_v[...]

    for c in copies:
        c.wait()
    ends = [tails[r].astype(jnp.float32) for r in range(shards)]
    metas = [end[PIECE:, 2 * kv_width :] for end in ends]
    own = [meta[:, 0:unit] for meta in metas]
    behind = [meta[:, unit : 2 * unit] for meta in metas]
    own = decode(by_lane(own, 0), by_lane(own, 1))
    behind = decode(by_lane(behind, 0), by_lane(behind, 1))
    raw[count:, :] = jnp.concatenate([end[0:PIECE] for end in ends], axis=0).astype(jnp.bfloat16)
    onehot = select_rows(jnp.concatenate([code_ref[...], own], axis=1), 1, count)
    q_pl[...] = matmul(onehot, raw[...]).astype(jnp.bfloat16)
    for j, (code, start) in enumerate(((behind, kv_width), (own, 0))):
        rows = jnp.concatenate([end[PIECE:, start : start + kv_width] for end in ends], axis=0)
        rows = matmul(select_rows(code, 1, count), rows.astype(jnp.bfloat16))
        kv_all[j * count : (j + 1) * count, :] += rows.astype(jnp.bfloat16)
    attend_core(me_ref[0], anc_ref, q_pl, kv_all, out_ref, groups)


def attend(me, ancestors, codes, got, own_k, own_v, prior_k, beside_v, prior_v, unit):
    shards = len(got)
    count, width = shards * unit, got[0].shape[1]
    groups = own_k.shape[1] // HEAD_SIZE
    return pl.pallas_call(
        functools.partial(attend_kernel, shards, unit, groups),
        out_shape=jax.ShapeDtypeStruct((count, width), jnp.bfloat16),
        in_specs=[SM, SM, VM] + [HB] * (shards + 3) + [VM, VM],
        out_specs=VM,
        scratch_shapes=[
            pltpu.VMEM((count + shards * PIECE, width), jnp.bfloat16),
            pltpu.VMEM((shards, 2 * PIECE, width), jnp.bfloat16),
            pltpu.VMEM((count, width), jnp.bfloat16),
            pltpu.VMEM((2 * count, 2 * own_k.shape[1]), jnp.bfloat16),
            pltpu.SemaphoreType.DMA((2 * shards + 3,)),
        ],
        compiler_params=params(28),
        cost_estimate=light(),
        name="attend",
    )(me, ancestors, codes, *got, own_k, own_v, prior_k, beside_v, prior_v)


def attend_padded_kernel(me_ref, anc_ref, code_ref, raw_ref, own_kv, prior_kv, out_ref, q_pl, kv_all):
    count = out_ref.shape[0]
    kv_all[0:count, :] = prior_kv[...]
    kv_all[count : 2 * count, :] = own_kv[...]
    q_pl[...] = matmul(select_rows(code_ref[...], 1, count), raw_ref[...]).astype(jnp.bfloat16)
    attend_core(me_ref[0], anc_ref, q_pl, kv_all, out_ref, kv_all.shape[1] // (2 * HEAD_SIZE))


def attend_padded(me, ancestors, codes, raw, own_kv, prior_kv):
    count, width = own_kv.shape[0], raw.shape[1]
    return pl.pallas_call(
        attend_padded_kernel,
        out_shape=jax.ShapeDtypeStruct((count, width), jnp.bfloat16),
        in_specs=[SM, SM] + [VM] * 4,
        out_specs=VM,
        scratch_shapes=[
            pltpu.VMEM((count, width), jnp.bfloat16),
            pltpu.VMEM((2 * count, own_kv.shape[1]), jnp.bfloat16),
        ],
        compiler_params=params(),
        name="attend_padded",
    )(me, ancestors, codes, raw, own_kv, prior_kv)


def positions(dest_shard, shards):
    onehot = (dest_shard[:, None] == jnp.arange(shards, dtype=jnp.int32)[None, :]).astype(jnp.int32)
    before = jnp.cumsum(onehot, axis=0) - onehot
    return jnp.sum(before * onehot, axis=1)


def exchange(source, index, total):
    buffer = jnp.zeros((total,) + source.shape[1:], source.dtype).at[index].set(source, mode="drop")
    return lax.all_to_all(buffer, "seq", split_axis=0, concat_axis=0, tiled=True)


def from_behind(block):
    n = lax.axis_size("seq")
    return lax.ppermute(block, "seq", [(i, i + 1) for i in range(n - 1)])


def rotate(block, r):
    n = lax.axis_size("seq")
    return lax.ppermute(block, "seq", [(i, (i + r) % n) for i in range(n)])


def padded_plan(me, queries, keys, values, dest_shard, dest_slot, ancestors):
    count = queries.shape[0]
    shards = lax.axis_size("seq")
    capacity = 2 * count // shards
    total = shards * capacity
    index = dest_shard * capacity + positions(dest_shard, shards)
    kv = exchange(jnp.concatenate([keys, values], axis=1), index, total)
    raw = exchange(queries, index, total)
    code = exchange(dest_slot + 1, index, total)
    slots = jnp.where(code > 0, code - 1, count)
    own_kv = jnp.zeros((count, kv.shape[1]), kv.dtype).at[slots].set(kv, mode="drop")
    prior_kv = from_behind(own_kv)
    return attend_padded(me, ancestors, code.reshape(1, total), raw, own_kv, prior_kv)


def after(block, *done):
    return lax.optimization_barrier((block, *done))[0]


def relay_plan(me, queries, keys, values, dest_shard, dest_slot, ancestors):
    count = queries.shape[0]
    shards = lax.axis_size("seq")
    unit = count // shards
    kv_blocks, index = pack_kv(me, dest_shard, dest_slot, keys, values, queries, shards, unit)
    got_kv = [kv_blocks[0]] + [rotate(kv_blocks[r], r) for r in range(1, shards)]
    q_blocks = pack_q(after(index, got_kv[1]), queries, shards, unit)
    own_k, beside_v, codes, crowd, q_blocks = relay(me, got_kv, q_blocks, unit)
    prior_k = from_behind(own_k)
    prior_v = lax.ppermute(beside_v, "seq", [(i, i + 2) for i in range(0, shards - 2, 2)])
    own_v = lax.ppermute(beside_v, "seq", [(i, i ^ 1) for i in range(shards)])
    got_q = [q_blocks[0]] + [rotate(q_blocks[r], r) for r in range(1, shards)]
    result = attend(me, ancestors, codes, got_q, own_k, own_v, prior_k, beside_v, prior_v, unit)
    args = (queries, keys, values, dest_shard, dest_slot, ancestors)
    return lax.cond(crowd[0, 0] > 0, lambda: padded_plan(me, *args), lambda: result)


def local(queries, keys, values, dest_shard, dest_slot, ancestors):
    shards = lax.axis_size("seq")
    me = lax.axis_index("seq").astype(jnp.int32).reshape(1)
    plan = relay_plan if queries.shape[0] == 8 * PIECE * shards and shards == 8 else padded_plan
    return plan(me, queries, keys, values, dest_shard, dest_slot, ancestors)


def solution(mesh):
    rows = P(("groups", "seq"))
    heads = P(("groups", "seq"), "head")
    return jax.shard_map(
        local,
        mesh=mesh,
        in_specs=(heads, heads, heads, rows, rows, P(("groups", "seq"), None)),
        out_specs=heads,
        check_vma=False,
    )
```

```python
import functools
import math

import jax
import jax.numpy as jnp
from jax import lax
from jax.experimental import pallas as pl
from jax.experimental.pallas import tpu as pltpu
from jax.sharding import PartitionSpec as P

HEAD_SIZE = 128
PIECE = 8
RADIX = 32
NO_DEST = 255.0
NEG = -1e30

VM = pl.BlockSpec(memory_space=pltpu.VMEM)
SM = pl.BlockSpec(memory_space=pltpu.SMEM)
HB = pl.BlockSpec(memory_space=pl.ANY)


def light():
    return pl.CostEstimate(flops=0, bytes_accessed=0, transcendentals=0)


def params(mebibytes=56):
    return pltpu.CompilerParams(vmem_limit_bytes=mebibytes * 1024 * 1024)


def iota(shape, axis):
    return lax.broadcasted_iota(jnp.int32, shape, axis)


def matmul(a, b):
    return jnp.dot(a, b, preferred_element_type=jnp.float32)


def matmul_nt(a, b):
    return lax.dot_general(a, b, (((1,), (1,)), ((), ())), preferred_element_type=jnp.float32)


def select_rows(index, start, rows, dtype=jnp.bfloat16):
    return (iota((rows, index.shape[1]), 0) + start == index).astype(dtype)


def strips(width, kv_width):
    return [(c, min(c + kv_width, width)) for c in range(0, width, kv_width)]


def pack_kv_kernel(shards, unit, me_ref, dest_ref, slot_ref, k_ref, v_ref, q_ref, *outs):
    blocks, index_ref = outs[:shards], outs[shards]
    count, kv = k_ref.shape
    dest = dest_ref[...].reshape(1, count)
    code = slot_ref[...].reshape(1, count) + 1
    onehot = (iota((shards, count), 0) == dest).astype(jnp.bfloat16)
    earlier = (iota((count, count), 0) < iota((count, count), 1)).astype(jnp.bfloat16)
    before = matmul(onehot, earlier)
    position = jnp.sum(before * onehot.astype(jnp.float32), axis=0, keepdims=True).astype(jnp.int32)
    base = position < unit
    index = jnp.where(base, ((dest - me_ref[0]) & (shards - 1)) * unit + position, -1)
    index_ref[...] = index
    v_index = jnp.where(base, (((dest ^ 1) - me_ref[0]) & (shards - 1)) * unit + position, -1)
    over_index = jnp.where(base, -1, position - unit)
    totals = matmul_nt(jnp.ones((PIECE, count), jnp.bfloat16), onehot)
    flags = jnp.where(iota((PIECE, shards), 0) == 2, (totals > unit + 0.5).astype(jnp.float32), 0.0)
    flags = jnp.concatenate([flags, jnp.zeros((PIECE, unit - shards), jnp.float32)], axis=1)
    over_dest = jnp.max(jnp.where(base, -1, dest))
    over_value = jnp.where(over_dest < 0, NO_DEST, over_dest.astype(jnp.float32))

    row = iota((PIECE, count), 0)
    codes = jnp.where(row == 0, code // RADIX, jnp.where(row == 1, code % RADIX, 0))
    codes = codes.astype(jnp.float32).astype(jnp.bfloat16)

    picked = select_rows(index, 0, count)
    k_rows = matmul(picked, k_ref[...]).astype(jnp.bfloat16)
    sent = matmul_nt(codes, picked)
    picked = select_rows(v_index, 0, count)
    v_rows = matmul(picked, v_ref[...]).astype(jnp.bfloat16)
    v_sent = matmul_nt(codes, picked)
    picked = select_rows(over_index, 0, unit)
    over_k = matmul(picked, k_ref[...])
    over_v = matmul(picked, v_ref[...])
    over_q = matmul(picked, q_ref[...])
    over_sent = matmul_nt(codes, picked)
    over_sent = jnp.where(iota((PIECE, unit), 0) == 2, over_value, over_sent)
    empty = jnp.zeros((PIECE, unit), jnp.float32)
    for r in range(shards):
        rows = slice(r * unit, (r + 1) * unit)
        blocks[r][0:unit, 0:kv] = k_rows[rows]
        blocks[r][0:unit, kv : 2 * kv] = v_rows[rows]
        piece = slice(r * PIECE, (r + 1) * PIECE)
        meta = jnp.concatenate([sent[:, rows], flags + v_sent[:, rows], over_sent, empty], axis=1)
        tail = [jnp.concatenate([over_k[piece], over_v[piece]], axis=1)]
        for start, stop in strips(over_q.shape[1], 2 * kv):
            tail.append(over_q[piece, start:stop])
        tail[-1] = jnp.concatenate([tail[-1], meta], axis=1)
        blocks[r][unit:, :] = jnp.concatenate(tail, axis=0).astype(jnp.bfloat16)


def pack_kv(me, dest, slot, keys, values, queries, shards, unit):
    kv_width = 2 * keys.shape[1]
    rows = unit + PIECE * (1 + len(strips(queries.shape[1], kv_width)))
    shapes = [jax.ShapeDtypeStruct((rows, kv_width), jnp.bfloat16)] * shards
    shapes += [jax.ShapeDtypeStruct((1, keys.shape[0]), jnp.int32)]
    outs = pl.pallas_call(
        functools.partial(pack_kv_kernel, shards, unit),
        out_shape=shapes,
        in_specs=[SM] + [VM] * 5,
        out_specs=[VM] * len(shapes),
        compiler_params=params(16),
        cost_estimate=light(),
        name="pack_kv",
    )(me, dest, slot, keys, values, queries)
    return outs[:shards], outs[shards]


def pack_q_kernel(unit, index_ref, q_ref, *blocks):
    for r, block in enumerate(blocks):
        picked = select_rows(index_ref[...], r * unit, unit)
        block[0:unit, :] = matmul(picked, q_ref[...]).astype(jnp.bfloat16)


def pack_q(index, queries, shards, unit):
    return pl.pallas_call(
        functools.partial(pack_q_kernel, unit),
        out_shape=[jax.ShapeDtypeStruct((unit + 2 * PIECE, queries.shape[1]), jnp.bfloat16)] * shards,
        in_specs=[VM, VM],
        out_specs=[VM] * shards,
        compiler_params=params(12),
        cost_estimate=light(),
        name="pack_q",
    )(index, queries)


def by_lane(parts, row):
    lane = iota((1, parts[0].shape[1]), 1) // PIECE
    total = jnp.zeros(lane.shape, jnp.float32)
    for r, part in enumerate(parts):
        total += jnp.where(lane == r, part[row : row + 1, :], 0.0)
    return total


def decode(high, low):
    return (high * RADIX + low).astype(jnp.int32)


def relay_kernel(shards, unit, me_ref, *refs):
    got = refs[:shards]
    k_out, v_out, codes_ref, crowd_ref = refs[2 * shards : 2 * shards + 4]
    blocks = refs[2 * shards + 4 : 3 * shards + 4]
    tails, sems = refs[3 * shards + 4 :]
    count, half = k_out.shape
    kv_width = 2 * half
    width = tails.shape[2]
    cuts = strips(width, kv_width)
    meta_at = cuts[-1][1] - cuts[-1][0]
    ends = [ref[unit:, :].astype(jnp.float32) for ref in got]
    metas = [end[-PIECE:, meta_at:] for end in ends]

    over = [meta[:, 2 * unit : 3 * unit] for meta in metas]
    dest = by_lane(over, 2).astype(jnp.int32)
    part = iota(dest.shape, 1) % PIECE
    to = jnp.where(dest < shards, ((dest - me_ref[0]) & (shards - 1)) * PIECE + part, -1)
    behind = jnp.where(dest < shards - 1, ((dest + 1 - me_ref[0]) & (shards - 1)) * PIECE + part, -1)
    to, behind = select_rows(to, 0, shards * PIECE), select_rows(behind, 0, shards * PIECE)
    over_kv = jnp.concatenate([end[0:PIECE] for end in ends], axis=0).astype(jnp.bfloat16)
    row = iota((PIECE, unit), 0)
    codes = jnp.where(row == 0, by_lane(over, 0), jnp.where(row == 1, by_lane(over, 1), 0.0)).astype(jnp.bfloat16)
    meta = jnp.concatenate([matmul_nt(codes, to), matmul_nt(codes, behind)], axis=1)
    meta = jnp.concatenate([meta, jnp.zeros((PIECE, width - 2 * kv_width - 2 * unit), jnp.float32)], axis=1)
    to_kv, behind_kv = matmul(to, over_kv), matmul(behind, over_kv)
    to_q = []
    for i, (start, stop) in enumerate(cuts):
        strip = [end[(i + 1) * PIECE : (i + 2) * PIECE, 0 : stop - start] for end in ends]
        to_q.append(matmul(to, jnp.concatenate(strip, axis=0).astype(jnp.bfloat16)))
    to_q = jnp.concatenate(to_q, axis=1)
    copies = []
    for r in range(shards):
        piece = slice(r * PIECE, (r + 1) * PIECE)
        lower = jnp.concatenate([to_kv[piece], behind_kv[piece], meta], axis=1)
        tails[r] = jnp.concatenate([to_q[piece], lower], axis=0).astype(jnp.bfloat16)
        copies.append(pltpu.make_async_copy(tails.at[r], blocks[r].at[pl.ds(unit, 2 * PIECE), :], sems.at[r]))
        copies[-1].start()

    code = jnp.concatenate([decode(meta[0:1, 0:unit], meta[1:2, 0:unit]) for meta in metas], axis=1)
    codes_ref[...] = code
    rows = jnp.concatenate([ref[0:unit, 0:half] for ref in got], axis=0)
    k_out[...] = matmul(select_rows(code, 1, count), rows).astype(jnp.bfloat16)
    code = [decode(meta[0:1, unit : 2 * unit], meta[1:2, unit : 2 * unit]) for meta in metas]
    rows = jnp.concatenate([ref[0:unit, half:] for ref in got], axis=0)
    v_out[...] = matmul(select_rows(jnp.concatenate(code, axis=1), 1, count), rows).astype(jnp.bfloat16)
    by_dest = jnp.zeros((1, unit), jnp.float32)
    most = jnp.zeros((1, 1), jnp.float32)
    for meta in metas:
        flags = meta[2:3, unit : 2 * unit]
        by_dest += flags
        most = jnp.maximum(most, jnp.sum(flags, axis=1, keepdims=True))
    most = jnp.maximum(most, jnp.max(by_dest, axis=1, keepdims=True))
    crowd_ref[...] = jnp.broadcast_to((most > 1.5).astype(jnp.int32), crowd_ref.shape)
    for c in copies:
        c.wait()


def relay(me, got, q_blocks, unit):
    shards = len(got)
    count = shards * unit
    shape = q_blocks[0].shape
    outs = pl.pallas_call(
        functools.partial(relay_kernel, shards, unit),
        out_shape=[
            jax.ShapeDtypeStruct((count, got[0].shape[1] // 2), jnp.bfloat16),
            jax.ShapeDtypeStruct((count, got[0].shape[1] // 2), jnp.bfloat16),
            jax.ShapeDtypeStruct((1, count), jnp.int32),
            jax.ShapeDtypeStruct((8, 128), jnp.int32),
        ]
        + [jax.ShapeDtypeStruct(shape, jnp.bfloat16)] * shards,
        in_specs=[SM] + [VM] * shards + [HB] * shards,
        out_specs=[VM] * 4 + [HB] * shards,
        scratch_shapes=[
            pltpu.VMEM((shards, 2 * PIECE, shape[1]), jnp.bfloat16),
            pltpu.SemaphoreType.DMA((shards,)),
        ],
        input_output_aliases={1 + shards + r: 4 + r for r in range(shards)},
        compiler_params=params(10),
        cost_estimate=light(),
        name="relay",
    )(me, *got, *q_blocks)
    return *outs[:4], outs[4:]


def attend_core(shard, anc_ref, q_pl, kv_all, out_ref, groups):
    count, width = out_ref.shape
    block_count = anc_ref.shape[0]
    size = count // block_count
    ratio = width // groups // HEAD_SIZE
    window = (block_count + 1) * size
    scale = math.log2(math.e) / math.sqrt(HEAD_SIZE)
    lane = iota((size, window), 1)
    for b in range(block_count):
        first = (shard - 1) * block_count + b
        key_block = lane // size + first
        seen = lane < 0
        for a in range(anc_ref.shape[1]):
            seen = seen | (key_block == anc_ref[b, a])
        own = lane >= block_count * size
        causal = lane - block_count * size <= iota((size, window), 0)
        seen = (seen & (lane < block_count * size)) | (own & causal)
        bias = jnp.where(seen, 0.0, NEG)
        for g in range(groups):
            columns = [(g * ratio + h) * HEAD_SIZE for h in range(ratio)]
            q = jnp.concatenate(
                [q_pl[b * size : (b + 1) * size, c : c + HEAD_SIZE] for c in columns], axis=0
            )
            k = kv_all[b * size : b * size + window, g * HEAD_SIZE : (g + 1) * HEAD_SIZE]
            v = kv_all[
                b * size : b * size + window,
                (groups + g) * HEAD_SIZE : (groups + g + 1) * HEAD_SIZE,
            ]
            scores = (matmul_nt(q, k) * scale).reshape(ratio, size, window) + bias[None]
            scores = scores.reshape(ratio * size, window)
            peak = jnp.max(scores, axis=1, keepdims=True)
            expo = jnp.exp2(scores - peak)
            total = jnp.sum(expo, axis=1, keepdims=True)
            output = (matmul(expo.astype(jnp.bfloat16), v) * (1.0 / total)).astype(jnp.bfloat16)
            for h, c in enumerate(columns):
                out_ref[b * size : (b + 1) * size, c : c + HEAD_SIZE] = output[h * size : (h + 1) * size]


def attend_kernel(shards, unit, groups, me_ref, anc_ref, code_ref, *refs):
    got, (own_k, own_v, prior_k, beside_v, prior_v) = refs[:shards], refs[shards : shards + 5]
    out_ref, raw, tails, q_pl, kv_all, sems = refs[shards + 5 :]
    count, width = out_ref.shape
    half = own_k.shape[1]
    kv_width = 2 * half
    copies = []

    def fetch(source, target):
        copies.append(pltpu.make_async_copy(source, target, sems.at[len(copies)]))
        copies[-1].start()

    for r, ref in enumerate(got):
        fetch(ref.at[pl.ds(unit, 2 * PIECE), :], tails.at[r])
        fetch(ref.at[pl.ds(0, unit), :], raw.at[pl.ds(r * unit, unit), :])
    fetch(prior_k, kv_all.at[pl.ds(0, count), pl.ds(0, half)])
    fetch(own_k, kv_all.at[pl.ds(count, count), pl.ds(0, half)])
    fetch(own_v, kv_all.at[pl.ds(count, count), pl.ds(half, half)])
    odd = me_ref[0] & 1

    @pl.when(odd == 1)
    def _():
        kv_all[0:count, half:] = beside_v[...]

    @pl.when(odd == 0)
    def _():
        kv_all[0:count, half:] = prior_v[...]

    for c in copies:
        c.wait()
    ends = [tails[r].astype(jnp.float32) for r in range(shards)]
    metas = [end[PIECE:, 2 * kv_width :] for end in ends]
    own = [meta[:, 0:unit] for meta in metas]
    behind = [meta[:, unit : 2 * unit] for meta in metas]
    own = decode(by_lane(own, 0), by_lane(own, 1))
    behind = decode(by_lane(behind, 0), by_lane(behind, 1))
    raw[count:, :] = jnp.concatenate([end[0:PIECE] for end in ends], axis=0).astype(jnp.bfloat16)
    onehot = select_rows(jnp.concatenate([code_ref[...], own], axis=1), 1, count)
    q_pl[...] = matmul(onehot, raw[...]).astype(jnp.bfloat16)
    for j, (code, start) in enumerate(((behind, kv_width), (own, 0))):
        rows = jnp.concatenate([end[PIECE:, start : start + kv_width] for end in ends], axis=0)
        rows = matmul(select_rows(code, 1, count), rows.astype(jnp.bfloat16))
        kv_all[j * count : (j + 1) * count, :] += rows.astype(jnp.bfloat16)
    attend_core(me_ref[0], anc_ref, q_pl, kv_all, out_ref, groups)


def attend(me, ancestors, codes, got, own_k, own_v, prior_k, beside_v, prior_v, unit):
    shards = len(got)
    count, width = shards * unit, got[0].shape[1]
    groups = own_k.shape[1] // HEAD_SIZE
    return pl.pallas_call(
        functools.partial(attend_kernel, shards, unit, groups),
        out_shape=jax.ShapeDtypeStruct((count, width), jnp.bfloat16),
        in_specs=[SM, SM, VM] + [HB] * (shards + 3) + [VM, VM],
        out_specs=VM,
        scratch_shapes=[
            pltpu.VMEM((count + shards * PIECE, width), jnp.bfloat16),
            pltpu.VMEM((shards, 2 * PIECE, width), jnp.bfloat16),
            pltpu.VMEM((count, width), jnp.bfloat16),
            pltpu.VMEM((2 * count, 2 * own_k.shape[1]), jnp.bfloat16),
            pltpu.SemaphoreType.DMA((2 * shards + 3,)),
        ],
        compiler_params=params(28),
        cost_estimate=light(),
        name="attend",
    )(me, ancestors, codes, *got, own_k, own_v, prior_k, beside_v, prior_v)


def attend_padded_kernel(me_ref, anc_ref, code_ref, raw_ref, own_kv, prior_kv, out_ref, q_pl, kv_all):
    count = out_ref.shape[0]
    kv_all[0:count, :] = prior_kv[...]
    kv_all[count : 2 * count, :] = own_kv[...]
    q_pl[...] = matmul(select_rows(code_ref[...], 1, count), raw_ref[...]).astype(jnp.bfloat16)
    attend_core(me_ref[0], anc_ref, q_pl, kv_all, out_ref, kv_all.shape[1] // (2 * HEAD_SIZE))


def attend_padded(me, ancestors, codes, raw, own_kv, prior_kv):
    count, width = own_kv.shape[0], raw.shape[1]
    return pl.pallas_call(
        attend_padded_kernel,
        out_shape=jax.ShapeDtypeStruct((count, width), jnp.bfloat16),
        in_specs=[SM, SM] + [VM] * 4,
        out_specs=VM,
        scratch_shapes=[
            pltpu.VMEM((count, width), jnp.bfloat16),
            pltpu.VMEM((2 * count, own_kv.shape[1]), jnp.bfloat16),
        ],
        compiler_params=params(),
        name="attend_padded",
    )(me, ancestors, codes, raw, own_kv, prior_kv)


def positions(dest_shard, shards):
    onehot = (dest_shard[:, None] == jnp.arange(shards, dtype=jnp.int32)[None, :]).astype(jnp.int32)
    before = jnp.cumsum(onehot, axis=0) - onehot
    return jnp.sum(before * onehot, axis=1)


def exchange(source, index, total):
    buffer = jnp.zeros((total,) + source.shape[1:], source.dtype).at[index].set(source, mode="drop")
    return lax.all_to_all(buffer, "seq", split_axis=0, concat_axis=0, tiled=True)


def from_behind(block):
    n = lax.axis_size("seq")
    return lax.ppermute(block, "seq", [(i, i + 1) for i in range(n - 1)])


def rotate(block, r):
    n = lax.axis_size("seq")
    return lax.ppermute(block, "seq", [(i, (i + r) % n) for i in range(n)])


def padded_plan(me, queries, keys, values, dest_shard, dest_slot, ancestors):
    count = queries.shape[0]
    shards = lax.axis_size("seq")
    capacity = 2 * count // shards
    total = shards * capacity
    index = dest_shard * capacity + positions(dest_shard, shards)
    kv = exchange(jnp.concatenate([keys, values], axis=1), index, total)
    raw = exchange(queries, index, total)
    code = exchange(dest_slot + 1, index, total)
    slots = jnp.where(code > 0, code - 1, count)
    own_kv = jnp.zeros((count, kv.shape[1]), kv.dtype).at[slots].set(kv, mode="drop")
    prior_kv = from_behind(own_kv)
    return attend_padded(me, ancestors, code.reshape(1, total), raw, own_kv, prior_kv)


def after(block, *done):
    return lax.optimization_barrier((block, *done))[0]


def relay_plan(me, queries, keys, values, dest_shard, dest_slot, ancestors):
    count = queries.shape[0]
    shards = lax.axis_size("seq")
    unit = count // shards
    kv_blocks, index = pack_kv(me, dest_shard, dest_slot, keys, values, queries, shards, unit)
    got_kv = [kv_blocks[0]] + [rotate(kv_blocks[r], r) for r in range(1, shards)]
    q_blocks = pack_q(after(index, got_kv[1]), queries, shards, unit)
    own_k, beside_v, codes, crowd, q_blocks = relay(me, got_kv, q_blocks, unit)
    got_q = [q_blocks[0]] + [rotate(q_blocks[r], r) for r in range(1, shards)]
    prior_k = from_behind(after(own_k, got_q[1]))
    to_v = after(beside_v, got_q[2])
    prior_v = lax.ppermute(to_v, "seq", [(i, i + 2) for i in range(0, shards - 2, 2)])
    own_v = lax.ppermute(after(beside_v, got_q[3]), "seq", [(i, i ^ 1) for i in range(shards)])
    result = attend(me, ancestors, codes, got_q, own_k, own_v, prior_k, beside_v, prior_v, unit)
    args = (queries, keys, values, dest_shard, dest_slot, ancestors)
    return lax.cond(crowd[0, 0] > 0, lambda: padded_plan(me, *args), lambda: result)


def local(queries, keys, values, dest_shard, dest_slot, ancestors):
    shards = lax.axis_size("seq")
    me = lax.axis_index("seq").astype(jnp.int32).reshape(1)
    plan = relay_plan if queries.shape[0] == 8 * PIECE * shards and shards == 8 else padded_plan
    return plan(me, queries, keys, values, dest_shard, dest_slot, ancestors)


def solution(mesh):
    rows = P(("groups", "seq"))
    heads = P(("groups", "seq"), "head")
    return jax.shard_map(
        local,
        mesh=mesh,
        in_specs=(heads, heads, heads, rows, rows, P(("groups", "seq"), None)),
        out_specs=heads,
        check_vma=False,
    )
```

```python
import functools
import math

import jax
import jax.numpy as jnp
from jax import lax
from jax.experimental import pallas as pl
from jax.experimental.pallas import tpu as pltpu
from jax.sharding import PartitionSpec as P

HEAD_SIZE = 128
PIECE = 8
RADIX = 32
NO_DEST = 255.0
NEG = -1e30

VM = pl.BlockSpec(memory_space=pltpu.VMEM)
SM = pl.BlockSpec(memory_space=pltpu.SMEM)
HB = pl.BlockSpec(memory_space=pl.ANY)


def light():
    return pl.CostEstimate(flops=0, bytes_accessed=0, transcendentals=0)


def params(mebibytes=56):
    return pltpu.CompilerParams(vmem_limit_bytes=mebibytes * 1024 * 1024)


def iota(shape, axis):
    return lax.broadcasted_iota(jnp.int32, shape, axis)


def matmul(a, b):
    return jnp.dot(a, b, preferred_element_type=jnp.float32)


def matmul_nt(a, b):
    return lax.dot_general(a, b, (((1,), (1,)), ((), ())), preferred_element_type=jnp.float32)


def select_rows(index, start, rows, dtype=jnp.bfloat16):
    return (iota((rows, index.shape[1]), 0) + start == index).astype(dtype)


def strips(width, kv_width):
    return [(c, min(c + kv_width, width)) for c in range(0, width, kv_width)]


def pack_kv_kernel(shards, unit, me_ref, dest_ref, slot_ref, k_ref, v_ref, q_ref, *outs):
    blocks, index_ref = outs[:shards], outs[shards]
    count, kv = k_ref.shape
    dest = dest_ref[...].reshape(1, count)
    code = slot_ref[...].reshape(1, count) + 1
    onehot = (iota((shards, count), 0) == dest).astype(jnp.bfloat16)
    earlier = (iota((count, count), 0) < iota((count, count), 1)).astype(jnp.bfloat16)
    before = matmul(onehot, earlier)
    position = jnp.sum(before * onehot.astype(jnp.float32), axis=0, keepdims=True).astype(jnp.int32)
    base = position < unit
    index = jnp.where(base, ((dest - me_ref[0]) & (shards - 1)) * unit + position, -1)
    index_ref[...] = index
    v_index = jnp.where(base, (((dest ^ 1) - me_ref[0]) & (shards - 1)) * unit + position, -1)
    over_index = jnp.where(base, -1, position - unit)
    totals = matmul_nt(jnp.ones((PIECE, count), jnp.bfloat16), onehot)
    flags = jnp.where(iota((PIECE, shards), 0) == 2, (totals > unit + 0.5).astype(jnp.float32), 0.0)
    flags = jnp.concatenate([flags, jnp.zeros((PIECE, unit - shards), jnp.float32)], axis=1)
    over_dest = jnp.max(jnp.where(base, -1, dest))
    over_value = jnp.where(over_dest < 0, NO_DEST, over_dest.astype(jnp.float32))

    row = iota((PIECE, count), 0)
    codes = jnp.where(row == 0, code // RADIX, jnp.where(row == 1, code % RADIX, 0))
    codes = codes.astype(jnp.float32).astype(jnp.bfloat16)

    picked = select_rows(index, 0, count)
    k_rows = matmul(picked, k_ref[...]).astype(jnp.bfloat16)
    sent = matmul_nt(codes, picked)
    picked = select_rows(v_index, 0, count)
    v_rows = matmul(picked, v_ref[...]).astype(jnp.bfloat16)
    v_sent = matmul_nt(codes, picked)
    picked = select_rows(over_index, 0, unit)
    over_k = matmul(picked, k_ref[...])
    over_v = matmul(picked, v_ref[...])
    over_q = matmul(picked, q_ref[...])
    over_sent = matmul_nt(codes, picked)
    over_sent = jnp.where(iota((PIECE, unit), 0) == 2, over_value, over_sent)
    empty = jnp.zeros((PIECE, unit), jnp.float32)
    for r in range(shards):
        rows = slice(r * unit, (r + 1) * unit)
        blocks[r][0:unit, 0:kv] = k_rows[rows]
        blocks[r][0:unit, kv : 2 * kv] = v_rows[rows]
        piece = slice(r * PIECE, (r + 1) * PIECE)
        meta = jnp.concatenate([sent[:, rows], flags + v_sent[:, rows], over_sent, empty], axis=1)
        tail = [jnp.concatenate([over_k[piece], over_v[piece]], axis=1)]
        for start, stop in strips(over_q.shape[1], 2 * kv):
            tail.append(over_q[piece, start:stop])
        tail[-1] = jnp.concatenate([tail[-1], meta], axis=1)
        blocks[r][unit:, :] = jnp.concatenate(tail, axis=0).astype(jnp.bfloat16)


def pack_kv(me, dest, slot, keys, values, queries, shards, unit):
    kv_width = 2 * keys.shape[1]
    rows = unit + PIECE * (1 + len(strips(queries.shape[1], kv_width)))
    shapes = [jax.ShapeDtypeStruct((rows, kv_width), jnp.bfloat16)] * shards
    shapes += [jax.ShapeDtypeStruct((1, keys.shape[0]), jnp.int32)]
    outs = pl.pallas_call(
        functools.partial(pack_kv_kernel, shards, unit),
        out_shape=shapes,
        in_specs=[SM] + [VM] * 5,
        out_specs=[VM] * len(shapes),
        compiler_params=params(16),
        cost_estimate=light(),
        name="pack_kv",
    )(me, dest, slot, keys, values, queries)
    return outs[:shards], outs[shards]


def pack_q_kernel(unit, index_ref, q_ref, *blocks):
    for r, block in enumerate(blocks):
        picked = select_rows(index_ref[...], r * unit, unit)
        block[0:unit, :] = matmul(picked, q_ref[...]).astype(jnp.bfloat16)


def pack_q(index, queries, shards, unit):
    return pl.pallas_call(
        functools.partial(pack_q_kernel, unit),
        out_shape=[jax.ShapeDtypeStruct((unit + 2 * PIECE, queries.shape[1]), jnp.bfloat16)] * shards,
        in_specs=[VM, VM],
        out_specs=[VM] * shards,
        compiler_params=params(12),
        cost_estimate=light(),
        name="pack_q",
    )(index, queries)


def by_lane(parts, row):
    lane = iota((1, parts[0].shape[1]), 1) // PIECE
    total = jnp.zeros(lane.shape, jnp.float32)
    for r, part in enumerate(parts):
        total += jnp.where(lane == r, part[row : row + 1, :], 0.0)
    return total


def decode(high, low):
    return (high * RADIX + low).astype(jnp.int32)


def relay_kernel(shards, unit, me_ref, *refs):
    got = refs[:shards]
    k_out, v_out, codes_ref, crowd_ref = refs[2 * shards : 2 * shards + 4]
    blocks = refs[2 * shards + 4 : 3 * shards + 4]
    tails, sems = refs[3 * shards + 4 :]
    count, half = k_out.shape
    kv_width = 2 * half
    width = tails.shape[2]
    cuts = strips(width, kv_width)
    meta_at = cuts[-1][1] - cuts[-1][0]
    ends = [ref[unit:, :].astype(jnp.float32) for ref in got]
    metas = [end[-PIECE:, meta_at:] for end in ends]

    over = [meta[:, 2 * unit : 3 * unit] for meta in metas]
    dest = by_lane(over, 2).astype(jnp.int32)
    part = iota(dest.shape, 1) % PIECE
    to = jnp.where(dest < shards, ((dest - me_ref[0]) & (shards - 1)) * PIECE + part, -1)
    behind = jnp.where(dest < shards - 1, ((dest + 1 - me_ref[0]) & (shards - 1)) * PIECE + part, -1)
    to, behind = select_rows(to, 0, shards * PIECE), select_rows(behind, 0, shards * PIECE)
    over_kv = jnp.concatenate([end[0:PIECE] for end in ends], axis=0).astype(jnp.bfloat16)
    row = iota((PIECE, unit), 0)
    codes = jnp.where(row == 0, by_lane(over, 0), jnp.where(row == 1, by_lane(over, 1), 0.0)).astype(jnp.bfloat16)
    meta = jnp.concatenate([matmul_nt(codes, to), matmul_nt(codes, behind)], axis=1)
    meta = jnp.concatenate([meta, jnp.zeros((PIECE, width - 2 * kv_width - 2 * unit), jnp.float32)], axis=1)
    to_kv, behind_kv = matmul(to, over_kv), matmul(behind, over_kv)
    to_q = []
    for i, (start, stop) in enumerate(cuts):
        strip = [end[(i + 1) * PIECE : (i + 2) * PIECE, 0 : stop - start] for end in ends]
        to_q.append(matmul(to, jnp.concatenate(strip, axis=0).astype(jnp.bfloat16)))
    to_q = jnp.concatenate(to_q, axis=1)
    copies = []
    for r in range(shards):
        piece = slice(r * PIECE, (r + 1) * PIECE)
        lower = jnp.concatenate([to_kv[piece], behind_kv[piece], meta], axis=1)
        tails[r] = jnp.concatenate([to_q[piece], lower], axis=0).astype(jnp.bfloat16)
        copies.append(pltpu.make_async_copy(tails.at[r], blocks[r].at[pl.ds(unit, 2 * PIECE), :], sems.at[r]))
        copies[-1].start()

    code = jnp.concatenate([decode(meta[0:1, 0:unit], meta[1:2, 0:unit]) for meta in metas], axis=1)
    codes_ref[...] = code
    rows = jnp.concatenate([ref[0:unit, 0:half] for ref in got], axis=0)
    k_out[...] = matmul(select_rows(code, 1, count), rows).astype(jnp.bfloat16)
    code = [decode(meta[0:1, unit : 2 * unit], meta[1:2, unit : 2 * unit]) for meta in metas]
    rows = jnp.concatenate([ref[0:unit, half:] for ref in got], axis=0)
    v_out[...] = matmul(select_rows(jnp.concatenate(code, axis=1), 1, count), rows).astype(jnp.bfloat16)
    by_dest = jnp.zeros((1, unit), jnp.float32)
    most = jnp.zeros((1, 1), jnp.float32)
    for meta in metas:
        flags = meta[2:3, unit : 2 * unit]
        by_dest += flags
        most = jnp.maximum(most, jnp.sum(flags, axis=1, keepdims=True))
    most = jnp.maximum(most, jnp.max(by_dest, axis=1, keepdims=True))
    crowd_ref[...] = jnp.broadcast_to((most > 1.5).astype(jnp.int32), crowd_ref.shape)
    for c in copies:
        c.wait()


def relay(me, got, q_blocks, unit):
    shards = len(got)
    count = shards * unit
    shape = q_blocks[0].shape
    outs = pl.pallas_call(
        functools.partial(relay_kernel, shards, unit),
        out_shape=[
            jax.ShapeDtypeStruct((count, got[0].shape[1] // 2), jnp.bfloat16),
            jax.ShapeDtypeStruct((count, got[0].shape[1] // 2), jnp.bfloat16),
            jax.ShapeDtypeStruct((1, count), jnp.int32),
            jax.ShapeDtypeStruct((8, 128), jnp.int32),
        ]
        + [jax.ShapeDtypeStruct(shape, jnp.bfloat16)] * shards,
        in_specs=[SM] + [VM] * shards + [HB] * shards,
        out_specs=[VM] * 4 + [HB] * shards,
        scratch_shapes=[
            pltpu.VMEM((shards, 2 * PIECE, shape[1]), jnp.bfloat16),
            pltpu.SemaphoreType.DMA((shards,)),
        ],
        input_output_aliases={1 + shards + r: 4 + r for r in range(shards)},
        compiler_params=params(10),
        cost_estimate=light(),
        name="relay",
    )(me, *got, *q_blocks)
    return *outs[:4], outs[4:]


def attend_core(shard, anc_ref, q_pl, kv_all, out_ref, groups):
    count, width = out_ref.shape
    block_count = anc_ref.shape[0]
    size = count // block_count
    ratio = width // groups // HEAD_SIZE
    window = (block_count + 1) * size
    scale = math.log2(math.e) / math.sqrt(HEAD_SIZE)
    lane = iota((size, window), 1)
    causal = (lane >= block_count * size) & (lane - block_count * size <= iota((size, window), 0))

    def columns(g):
        return [(g * ratio + h) * HEAD_SIZE for h in range(ratio)]

    def scores_of(b, g):
        q = jnp.concatenate([q_pl[b * size : (b + 1) * size, c : c + HEAD_SIZE] for c in columns(g)], axis=0)
        return matmul_nt(q, kv_all[b * size : b * size + window, g * HEAD_SIZE : (g + 1) * HEAD_SIZE])

    def bias_of(b):
        key_block = lane // size + (shard - 1) * block_count + b
        seen = lane < 0
        for a in range(anc_ref.shape[1]):
            seen = seen | (key_block == anc_ref[b, a])
        return jnp.where((seen & (lane < block_count * size)) | causal, 0.0, NEG)

    def softmax(scores, bias):
        scores = (scores * scale).reshape(ratio, size, window) + bias[None]
        scores = scores.reshape(ratio * size, window)
        expo = jnp.exp2(scores - jnp.max(scores, axis=1, keepdims=True))
        return expo.astype(jnp.bfloat16), 1.0 / jnp.sum(expo, axis=1, keepdims=True)

    def finish(b, g, expo, inverse):
        column = (groups + g) * HEAD_SIZE
        v = kv_all[b * size : b * size + window, column : column + HEAD_SIZE]
        output = (matmul(expo, v) * inverse).astype(jnp.bfloat16)
        for h, c in enumerate(columns(g)):
            out_ref[b * size : (b + 1) * size, c : c + HEAD_SIZE] = output[h * size : (h + 1) * size]

    tiles = [(b, g) for b in range(block_count) for g in range(groups)]
    scores, held = scores_of(*tiles[0]), None
    for i, tile in enumerate(tiles):
        upcoming = scores_of(*tiles[i + 1]) if i + 1 < len(tiles) else None
        if held is not None:
            finish(*held)
        held = (*tile, *softmax(scores, bias_of(tile[0])))
        scores = upcoming
    finish(*held)


def attend_kernel(shards, unit, groups, me_ref, anc_ref, code_ref, *refs):
    got, (own_k, own_v, prior_k, beside_v, prior_v) = refs[:shards], refs[shards : shards + 5]
    out_ref, raw, tails, q_pl, kv_all, sems = refs[shards + 5 :]
    count, width = out_ref.shape
    half = own_k.shape[1]
    kv_width = 2 * half
    copies = []

    def fetch(source, target):
        copies.append(pltpu.make_async_copy(source, target, sems.at[len(copies)]))
        copies[-1].start()

    for r, ref in enumerate(got):
        fetch(ref.at[pl.ds(unit, 2 * PIECE), :], tails.at[r])
        fetch(ref.at[pl.ds(0, unit), :], raw.at[pl.ds(r * unit, unit), :])
    fetch(prior_k, kv_all.at[pl.ds(0, count), pl.ds(0, half)])
    fetch(own_k, kv_all.at[pl.ds(count, count), pl.ds(0, half)])
    fetch(own_v, kv_all.at[pl.ds(count, count), pl.ds(half, half)])
    odd = me_ref[0] & 1

    @pl.when(odd == 1)
    def _():
        kv_all[0:count, half:] = beside_v[...]

    @pl.when(odd == 0)
    def _():
        kv_all[0:count, half:] = prior_v[...]

    for c in copies:
        c.wait()
    ends = [tails[r].astype(jnp.float32) for r in range(shards)]
    metas = [end[PIECE:, 2 * kv_width :] for end in ends]
    own = [meta[:, 0:unit] for meta in metas]
    behind = [meta[:, unit : 2 * unit] for meta in metas]
    own = decode(by_lane(own, 0), by_lane(own, 1))
    behind = decode(by_lane(behind, 0), by_lane(behind, 1))
    raw[count:, :] = jnp.concatenate([end[0:PIECE] for end in ends], axis=0).astype(jnp.bfloat16)
    onehot = select_rows(jnp.concatenate([code_ref[...], own], axis=1), 1, count)
    q_pl[...] = matmul(onehot, raw[...]).astype(jnp.bfloat16)
    for j, (code, start) in enumerate(((behind, kv_width), (own, 0))):
        rows = jnp.concatenate([end[PIECE:, start : start + kv_width] for end in ends], axis=0)
        rows = matmul(select_rows(code, 1, count), rows.astype(jnp.bfloat16))
        kv_all[j * count : (j + 1) * count, :] += rows.astype(jnp.bfloat16)
    attend_core(me_ref[0], anc_ref, q_pl, kv_all, out_ref, groups)


def attend(me, ancestors, codes, got, own_k, own_v, prior_k, beside_v, prior_v, unit):
    shards = len(got)
    count, width = shards * unit, got[0].shape[1]
    groups = own_k.shape[1] // HEAD_SIZE
    return pl.pallas_call(
        functools.partial(attend_kernel, shards, unit, groups),
        out_shape=jax.ShapeDtypeStruct((count, width), jnp.bfloat16),
        in_specs=[SM, SM, VM] + [HB] * (shards + 3) + [VM, VM],
        out_specs=VM,
        scratch_shapes=[
            pltpu.VMEM((count + shards * PIECE, width), jnp.bfloat16),
            pltpu.VMEM((shards, 2 * PIECE, width), jnp.bfloat16),
            pltpu.VMEM((count, width), jnp.bfloat16),
            pltpu.VMEM((2 * count, 2 * own_k.shape[1]), jnp.bfloat16),
            pltpu.SemaphoreType.DMA((2 * shards + 3,)),
        ],
        compiler_params=params(28),
        cost_estimate=light(),
        name="attend",
    )(me, ancestors, codes, *got, own_k, own_v, prior_k, beside_v, prior_v)


def attend_padded_kernel(me_ref, anc_ref, code_ref, raw_ref, own_kv, prior_kv, out_ref, q_pl, kv_all):
    count = out_ref.shape[0]
    kv_all[0:count, :] = prior_kv[...]
    kv_all[count : 2 * count, :] = own_kv[...]
    q_pl[...] = matmul(select_rows(code_ref[...], 1, count), raw_ref[...]).astype(jnp.bfloat16)
    attend_core(me_ref[0], anc_ref, q_pl, kv_all, out_ref, kv_all.shape[1] // (2 * HEAD_SIZE))


def attend_padded(me, ancestors, codes, raw, own_kv, prior_kv):
    count, width = own_kv.shape[0], raw.shape[1]
    return pl.pallas_call(
        attend_padded_kernel,
        out_shape=jax.ShapeDtypeStruct((count, width), jnp.bfloat16),
        in_specs=[SM, SM] + [VM] * 4,
        out_specs=VM,
        scratch_shapes=[
            pltpu.VMEM((count, width), jnp.bfloat16),
            pltpu.VMEM((2 * count, own_kv.shape[1]), jnp.bfloat16),
        ],
        compiler_params=params(),
        name="attend_padded",
    )(me, ancestors, codes, raw, own_kv, prior_kv)


def positions(dest_shard, shards):
    onehot = (dest_shard[:, None] == jnp.arange(shards, dtype=jnp.int32)[None, :]).astype(jnp.int32)
    before = jnp.cumsum(onehot, axis=0) - onehot
    return jnp.sum(before * onehot, axis=1)


def exchange(source, index, total):
    buffer = jnp.zeros((total,) + source.shape[1:], source.dtype).at[index].set(source, mode="drop")
    return lax.all_to_all(buffer, "seq", split_axis=0, concat_axis=0, tiled=True)


def from_behind(block):
    n = lax.axis_size("seq")
    return lax.ppermute(block, "seq", [(i, i + 1) for i in range(n - 1)])


def rotate(block, r):
    n = lax.axis_size("seq")
    return lax.ppermute(block, "seq", [(i, (i + r) % n) for i in range(n)])


def padded_plan(me, queries, keys, values, dest_shard, dest_slot, ancestors):
    count = queries.shape[0]
    shards = lax.axis_size("seq")
    capacity = 2 * count // shards
    total = shards * capacity
    index = dest_shard * capacity + positions(dest_shard, shards)
    kv = exchange(jnp.concatenate([keys, values], axis=1), index, total)
    raw = exchange(queries, index, total)
    code = exchange(dest_slot + 1, index, total)
    slots = jnp.where(code > 0, code - 1, count)
    own_kv = jnp.zeros((count, kv.shape[1]), kv.dtype).at[slots].set(kv, mode="drop")
    prior_kv = from_behind(own_kv)
    return attend_padded(me, ancestors, code.reshape(1, total), raw, own_kv, prior_kv)


def after(block, *done):
    return lax.optimization_barrier((block, *done))[0]


def relay_plan(me, queries, keys, values, dest_shard, dest_slot, ancestors):
    count = queries.shape[0]
    shards = lax.axis_size("seq")
    unit = count // shards
    kv_blocks, index = pack_kv(me, dest_shard, dest_slot, keys, values, queries, shards, unit)
    got_kv = [kv_blocks[0]] + [rotate(kv_blocks[r], r) for r in range(1, shards)]
    q_blocks = pack_q(after(index, got_kv[1]), queries, shards, unit)
    own_k, beside_v, codes, crowd, q_blocks = relay(me, got_kv, q_blocks, unit)
    got_q = [q_blocks[0]] + [rotate(q_blocks[r], r) for r in range(1, shards)]
    prior_k = from_behind(after(own_k, got_q[1]))
    to_v = after(beside_v, got_q[7])
    prior_v = lax.ppermute(to_v, "seq", [(i, i + 2) for i in range(0, shards - 2, 2)])
    own_v = lax.ppermute(after(beside_v, got_q[4]), "seq", [(i, i ^ 1) for i in range(shards)])
    result = attend(me, ancestors, codes, got_q, own_k, own_v, prior_k, beside_v, prior_v, unit)
    args = (queries, keys, values, dest_shard, dest_slot, ancestors)
    return lax.cond(crowd[0, 0] > 0, lambda: padded_plan(me, *args), lambda: result)


def local(queries, keys, values, dest_shard, dest_slot, ancestors):
    shards = lax.axis_size("seq")
    me = lax.axis_index("seq").astype(jnp.int32).reshape(1)
    plan = relay_plan if queries.shape[0] == 8 * PIECE * shards and shards == 8 else padded_plan
    return plan(me, queries, keys, values, dest_shard, dest_slot, ancestors)


def solution(mesh):
    rows = P(("groups", "seq"))
    heads = P(("groups", "seq"), "head")
    return jax.shard_map(
        local,
        mesh=mesh,
        in_specs=(heads, heads, heads, rows, rows, P(("groups", "seq"), None)),
        out_specs=heads,
        check_vma=False,
    )
```

```python
import functools
import math

import jax
import jax.numpy as jnp
from jax import lax
from jax.experimental import pallas as pl
from jax.experimental.pallas import tpu as pltpu
from jax.sharding import PartitionSpec as P

HEAD_SIZE = 128
PIECE = 8
RADIX = 32
NO_DEST = 255.0
NEG = -1e30

VM = pl.BlockSpec(memory_space=pltpu.VMEM)
SM = pl.BlockSpec(memory_space=pltpu.SMEM)
HB = pl.BlockSpec(memory_space=pl.ANY)


def light():
    return pl.CostEstimate(flops=0, bytes_accessed=0, transcendentals=0)


def params(mebibytes=56):
    return pltpu.CompilerParams(vmem_limit_bytes=mebibytes * 1024 * 1024)


def iota(shape, axis):
    return lax.broadcasted_iota(jnp.int32, shape, axis)


def matmul(a, b):
    return jnp.dot(a, b, preferred_element_type=jnp.float32)


def matmul_nt(a, b):
    return lax.dot_general(a, b, (((1,), (1,)), ((), ())), preferred_element_type=jnp.float32)


def select_rows(index, start, rows, dtype=jnp.bfloat16):
    return (iota((rows, index.shape[1]), 0) + start == index).astype(dtype)


def strips(width, kv_width):
    return [(c, min(c + kv_width, width)) for c in range(0, width, kv_width)]


def pack_kv_kernel(shards, unit, me_ref, dest_ref, slot_ref, k_ref, v_ref, q_ref, *outs):
    blocks, index_ref = outs[:shards], outs[shards]
    count, kv = k_ref.shape
    dest = dest_ref[...].reshape(1, count)
    code = slot_ref[...].reshape(1, count) + 1
    onehot = (iota((shards, count), 0) == dest).astype(jnp.bfloat16)
    earlier = (iota((count, count), 0) < iota((count, count), 1)).astype(jnp.bfloat16)
    before = matmul(onehot, earlier)
    position = jnp.sum(before * onehot.astype(jnp.float32), axis=0, keepdims=True).astype(jnp.int32)
    base = position < unit
    index = jnp.where(base, ((dest - me_ref[0]) & (shards - 1)) * unit + position, -1)
    index_ref[...] = index
    v_index = jnp.where(base, (((dest ^ 1) - me_ref[0]) & (shards - 1)) * unit + position, -1)
    over_index = jnp.where(base, -1, position - unit)
    totals = matmul_nt(jnp.ones((PIECE, count), jnp.bfloat16), onehot)
    flags = jnp.where(iota((PIECE, shards), 0) == 2, (totals > unit + 0.5).astype(jnp.float32), 0.0)
    flags = jnp.concatenate([flags, jnp.zeros((PIECE, unit - shards), jnp.float32)], axis=1)
    over_dest = jnp.max(jnp.where(base, -1, dest))
    over_value = jnp.where(over_dest < 0, NO_DEST, over_dest.astype(jnp.float32))

    row = iota((PIECE, count), 0)
    codes = jnp.where(row == 0, code // RADIX, jnp.where(row == 1, code % RADIX, 0))
    codes = codes.astype(jnp.float32).astype(jnp.bfloat16)

    picked = select_rows(index, 0, count)
    k_rows = matmul(picked, k_ref[...]).astype(jnp.bfloat16)
    sent = matmul_nt(codes, picked)
    picked = select_rows(v_index, 0, count)
    v_rows = matmul(picked, v_ref[...]).astype(jnp.bfloat16)
    v_sent = matmul_nt(codes, picked)
    picked = select_rows(over_index, 0, unit)
    over_k = matmul(picked, k_ref[...])
    over_v = matmul(picked, v_ref[...])
    over_q = matmul(picked, q_ref[...])
    over_sent = matmul_nt(codes, picked)
    over_sent = jnp.where(iota((PIECE, unit), 0) == 2, over_value, over_sent)
    empty = jnp.zeros((PIECE, unit), jnp.float32)
    for r in range(shards):
        rows = slice(r * unit, (r + 1) * unit)
        blocks[r][0:unit, 0:kv] = k_rows[rows]
        blocks[r][0:unit, kv : 2 * kv] = v_rows[rows]
        piece = slice(r * PIECE, (r + 1) * PIECE)
        meta = jnp.concatenate([sent[:, rows], flags + v_sent[:, rows], over_sent, empty], axis=1)
        tail = [jnp.concatenate([over_k[piece], over_v[piece]], axis=1)]
        for start, stop in strips(over_q.shape[1], 2 * kv):
            tail.append(over_q[piece, start:stop])
        tail[-1] = jnp.concatenate([tail[-1], meta], axis=1)
        blocks[r][unit:, :] = jnp.concatenate(tail, axis=0).astype(jnp.bfloat16)


def pack_kv(me, dest, slot, keys, values, queries, shards, unit):
    kv_width = 2 * keys.shape[1]
    rows = unit + PIECE * (1 + len(strips(queries.shape[1], kv_width)))
    shapes = [jax.ShapeDtypeStruct((rows, kv_width), jnp.bfloat16)] * shards
    shapes += [jax.ShapeDtypeStruct((1, keys.shape[0]), jnp.int32)]
    outs = pl.pallas_call(
        functools.partial(pack_kv_kernel, shards, unit),
        out_shape=shapes,
        in_specs=[SM] + [VM] * 5,
        out_specs=[VM] * len(shapes),
        compiler_params=params(16),
        cost_estimate=light(),
        name="pack_kv",
    )(me, dest, slot, keys, values, queries)
    return outs[:shards], outs[shards]


def pack_q_kernel(unit, index_ref, q_ref, *blocks):
    for r, block in enumerate(blocks):
        picked = select_rows(index_ref[...], r * unit, unit)
        block[0:unit, :] = matmul(picked, q_ref[...]).astype(jnp.bfloat16)


def pack_q(index, queries, shards, unit):
    return pl.pallas_call(
        functools.partial(pack_q_kernel, unit),
        out_shape=[jax.ShapeDtypeStruct((unit + 2 * PIECE, queries.shape[1]), jnp.bfloat16)] * shards,
        in_specs=[VM, VM],
        out_specs=[VM] * shards,
        compiler_params=params(12),
        cost_estimate=light(),
        name="pack_q",
    )(index, queries)


def by_lane(parts, row):
    lane = iota((1, parts[0].shape[1]), 1) // PIECE
    total = jnp.zeros(lane.shape, jnp.float32)
    for r, part in enumerate(parts):
        total += jnp.where(lane == r, part[row : row + 1, :], 0.0)
    return total


def decode(high, low):
    return (high * RADIX + low).astype(jnp.int32)


def relay_kernel(shards, unit, me_ref, *refs):
    got = refs[:shards]
    k_out, v_out, codes_ref, crowd_ref = refs[2 * shards : 2 * shards + 4]
    blocks = refs[2 * shards + 4 : 3 * shards + 4]
    tails, sems = refs[3 * shards + 4 :]
    count, half = k_out.shape
    kv_width = 2 * half
    width = tails.shape[2]
    cuts = strips(width, kv_width)
    meta_at = cuts[-1][1] - cuts[-1][0]
    ends = [ref[unit:, :].astype(jnp.float32) for ref in got]
    metas = [end[-PIECE:, meta_at:] for end in ends]

    over = [meta[:, 2 * unit : 3 * unit] for meta in metas]
    dest = by_lane(over, 2).astype(jnp.int32)
    part = iota(dest.shape, 1) % PIECE
    to = jnp.where(dest < shards, ((dest - me_ref[0]) & (shards - 1)) * PIECE + part, -1)
    behind = jnp.where(dest < shards - 1, ((dest + 1 - me_ref[0]) & (shards - 1)) * PIECE + part, -1)
    to, behind = select_rows(to, 0, shards * PIECE), select_rows(behind, 0, shards * PIECE)
    over_kv = jnp.concatenate([end[0:PIECE] for end in ends], axis=0).astype(jnp.bfloat16)
    row = iota((PIECE, unit), 0)
    codes = jnp.where(row == 0, by_lane(over, 0), jnp.where(row == 1, by_lane(over, 1), 0.0)).astype(jnp.bfloat16)
    meta = jnp.concatenate([matmul_nt(codes, to), matmul_nt(codes, behind)], axis=1)
    meta = jnp.concatenate([meta, jnp.zeros((PIECE, width - 2 * kv_width - 2 * unit), jnp.float32)], axis=1)
    to_kv, behind_kv = matmul(to, over_kv), matmul(behind, over_kv)
    to_q = []
    for i, (start, stop) in enumerate(cuts):
        strip = [end[(i + 1) * PIECE : (i + 2) * PIECE, 0 : stop - start] for end in ends]
        to_q.append(matmul(to, jnp.concatenate(strip, axis=0).astype(jnp.bfloat16)))
    to_q = jnp.concatenate(to_q, axis=1)
    copies = []
    for r in range(shards):
        piece = slice(r * PIECE, (r + 1) * PIECE)
        lower = jnp.concatenate([to_kv[piece], behind_kv[piece], meta], axis=1)
        tails[r] = jnp.concatenate([to_q[piece], lower], axis=0).astype(jnp.bfloat16)
        copies.append(pltpu.make_async_copy(tails.at[r], blocks[r].at[pl.ds(unit, 2 * PIECE), :], sems.at[r]))
        copies[-1].start()

    code = jnp.concatenate([decode(meta[0:1, 0:unit], meta[1:2, 0:unit]) for meta in metas], axis=1)
    codes_ref[...] = code
    rows = jnp.concatenate([ref[0:unit, 0:half] for ref in got], axis=0)
    k_out[...] = matmul(select_rows(code, 1, count), rows).astype(jnp.bfloat16)
    code = [decode(meta[0:1, unit : 2 * unit], meta[1:2, unit : 2 * unit]) for meta in metas]
    rows = jnp.concatenate([ref[0:unit, half:] for ref in got], axis=0)
    v_out[...] = matmul(select_rows(jnp.concatenate(code, axis=1), 1, count), rows).astype(jnp.bfloat16)
    by_dest = jnp.zeros((1, unit), jnp.float32)
    most = jnp.zeros((1, 1), jnp.float32)
    for meta in metas:
        flags = meta[2:3, unit : 2 * unit]
        by_dest += flags
        most = jnp.maximum(most, jnp.sum(flags, axis=1, keepdims=True))
    most = jnp.maximum(most, jnp.max(by_dest, axis=1, keepdims=True))
    crowd_ref[...] = jnp.broadcast_to((most > 1.5).astype(jnp.int32), crowd_ref.shape)
    for c in copies:
        c.wait()


def relay(me, got, q_blocks, unit):
    shards = len(got)
    count = shards * unit
    shape = q_blocks[0].shape
    outs = pl.pallas_call(
        functools.partial(relay_kernel, shards, unit),
        out_shape=[
            jax.ShapeDtypeStruct((count, got[0].shape[1] // 2), jnp.bfloat16),
            jax.ShapeDtypeStruct((count, got[0].shape[1] // 2), jnp.bfloat16),
            jax.ShapeDtypeStruct((1, count), jnp.int32),
            jax.ShapeDtypeStruct((8, 128), jnp.int32),
        ]
        + [jax.ShapeDtypeStruct(shape, jnp.bfloat16)] * shards,
        in_specs=[SM] + [VM] * shards + [HB] * shards,
        out_specs=[VM] * 4 + [HB] * shards,
        scratch_shapes=[
            pltpu.VMEM((shards, 2 * PIECE, shape[1]), jnp.bfloat16),
            pltpu.SemaphoreType.DMA((shards,)),
        ],
        input_output_aliases={1 + shards + r: 4 + r for r in range(shards)},
        compiler_params=params(10),
        cost_estimate=light(),
        name="relay",
    )(me, *got, *q_blocks)
    return *outs[:4], outs[4:]


def attend_core(shard, anc_ref, q_pl, kv_all, out_ref, groups):
    count, width = out_ref.shape
    block_count = anc_ref.shape[0]
    size = count // block_count
    ratio = width // groups // HEAD_SIZE
    window = (block_count + 1) * size
    scale = math.log2(math.e) / math.sqrt(HEAD_SIZE)
    lane = iota((size, window), 1)
    causal = (lane >= block_count * size) & (lane - block_count * size <= iota((size, window), 0))

    def columns(g):
        return [(g * ratio + h) * HEAD_SIZE for h in range(ratio)]

    def scores_of(b, g):
        q = jnp.concatenate([q_pl[b * size : (b + 1) * size, c : c + HEAD_SIZE] for c in columns(g)], axis=0)
        return matmul_nt(q, kv_all[b * size : b * size + window, g * HEAD_SIZE : (g + 1) * HEAD_SIZE])

    def bias_of(b):
        key_block = lane // size + (shard - 1) * block_count + b
        seen = lane < 0
        for a in range(anc_ref.shape[1]):
            seen = seen | (key_block == anc_ref[b, a])
        return jnp.where((seen & (lane < block_count * size)) | causal, 0.0, NEG)

    def softmax(scores, bias):
        scores = (scores * scale).reshape(ratio, size, window) + bias[None]
        scores = scores.reshape(ratio * size, window)
        expo = jnp.exp2(scores - jnp.max(scores, axis=1, keepdims=True))
        return expo.astype(jnp.bfloat16), 1.0 / jnp.sum(expo, axis=1, keepdims=True)

    def finish(b, g, expo, inverse):
        column = (groups + g) * HEAD_SIZE
        v = kv_all[b * size : b * size + window, column : column + HEAD_SIZE]
        output = (matmul(expo, v) * inverse).astype(jnp.bfloat16)
        for h, c in enumerate(columns(g)):
            out_ref[b * size : (b + 1) * size, c : c + HEAD_SIZE] = output[h * size : (h + 1) * size]

    tiles = [(b, g) for b in range(block_count) for g in range(groups)]
    scores, held = scores_of(*tiles[0]), None
    for i, tile in enumerate(tiles):
        upcoming = scores_of(*tiles[i + 1]) if i + 1 < len(tiles) else None
        if held is not None:
            finish(*held)
        held = (*tile, *softmax(scores, bias_of(tile[0])))
        scores = upcoming
    finish(*held)


def attend_kernel(shards, unit, groups, me_ref, anc_ref, code_ref, *refs):
    got, (own_k, own_v, prior_k, beside_v, prior_v) = refs[:shards], refs[shards : shards + 5]
    out_ref, raw, q_pl, kv_all, sems = refs[shards + 5 :]
    count, width = out_ref.shape
    half = own_k.shape[1]
    kv_width = 2 * half
    copies = []

    def fetch(source, target):
        copies.append(pltpu.make_async_copy(source, target, sems.at[len(copies)]))
        copies[-1].start()

    fetch(prior_k, kv_all.at[pl.ds(0, count), pl.ds(0, half)])
    fetch(own_k, kv_all.at[pl.ds(count, count), pl.ds(0, half)])
    fetch(own_v, kv_all.at[pl.ds(count, count), pl.ds(half, half)])
    odd = me_ref[0] & 1

    @pl.when(odd == 1)
    def _():
        kv_all[0:count, half:] = beside_v[...]

    @pl.when(odd == 0)
    def _():
        kv_all[0:count, half:] = prior_v[...]

    for r, ref in enumerate(got):
        raw[r * unit : (r + 1) * unit, :] = ref[0:unit, :]
    for c in copies:
        c.wait()
    ends = [ref[unit:, :].astype(jnp.float32) for ref in got]
    metas = [end[PIECE:, 2 * kv_width :] for end in ends]
    own = [meta[:, 0:unit] for meta in metas]
    behind = [meta[:, unit : 2 * unit] for meta in metas]
    own = decode(by_lane(own, 0), by_lane(own, 1))
    behind = decode(by_lane(behind, 0), by_lane(behind, 1))
    raw[count:, :] = jnp.concatenate([end[0:PIECE] for end in ends], axis=0).astype(jnp.bfloat16)
    onehot = select_rows(jnp.concatenate([code_ref[...], own], axis=1), 1, count)
    q_pl[...] = matmul(onehot, raw[...]).astype(jnp.bfloat16)
    for j, (code, start) in enumerate(((behind, kv_width), (own, 0))):
        rows = jnp.concatenate([end[PIECE:, start : start + kv_width] for end in ends], axis=0)
        rows = matmul(select_rows(code, 1, count), rows.astype(jnp.bfloat16))
        kv_all[j * count : (j + 1) * count, :] += rows.astype(jnp.bfloat16)
    attend_core(me_ref[0], anc_ref, q_pl, kv_all, out_ref, groups)


def attend(me, ancestors, codes, got, own_k, own_v, prior_k, beside_v, prior_v, unit):
    shards = len(got)
    count, width = shards * unit, got[0].shape[1]
    groups = own_k.shape[1] // HEAD_SIZE
    return pl.pallas_call(
        functools.partial(attend_kernel, shards, unit, groups),
        out_shape=jax.ShapeDtypeStruct((count, width), jnp.bfloat16),
        in_specs=[SM, SM, VM] + [VM] * shards + [HB] * 3 + [VM, VM],
        out_specs=VM,
        scratch_shapes=[
            pltpu.VMEM((count + shards * PIECE, width), jnp.bfloat16),
            pltpu.VMEM((count, width), jnp.bfloat16),
            pltpu.VMEM((2 * count, 2 * own_k.shape[1]), jnp.bfloat16),
            pltpu.SemaphoreType.DMA((3,)),
        ],
        compiler_params=params(28),
        cost_estimate=light(),
        name="attend",
    )(me, ancestors, codes, *got, own_k, own_v, prior_k, beside_v, prior_v)


def attend_padded_kernel(me_ref, anc_ref, code_ref, raw_ref, own_kv, prior_kv, out_ref, q_pl, kv_all):
    count = out_ref.shape[0]
    kv_all[0:count, :] = prior_kv[...]
    kv_all[count : 2 * count, :] = own_kv[...]
    q_pl[...] = matmul(select_rows(code_ref[...], 1, count), raw_ref[...]).astype(jnp.bfloat16)
    attend_core(me_ref[0], anc_ref, q_pl, kv_all, out_ref, kv_all.shape[1] // (2 * HEAD_SIZE))


def attend_padded(me, ancestors, codes, raw, own_kv, prior_kv):
    count, width = own_kv.shape[0], raw.shape[1]
    return pl.pallas_call(
        attend_padded_kernel,
        out_shape=jax.ShapeDtypeStruct((count, width), jnp.bfloat16),
        in_specs=[SM, SM] + [VM] * 4,
        out_specs=VM,
        scratch_shapes=[
            pltpu.VMEM((count, width), jnp.bfloat16),
            pltpu.VMEM((2 * count, own_kv.shape[1]), jnp.bfloat16),
        ],
        compiler_params=params(),
        name="attend_padded",
    )(me, ancestors, codes, raw, own_kv, prior_kv)


def positions(dest_shard, shards):
    onehot = (dest_shard[:, None] == jnp.arange(shards, dtype=jnp.int32)[None, :]).astype(jnp.int32)
    before = jnp.cumsum(onehot, axis=0) - onehot
    return jnp.sum(before * onehot, axis=1)


def exchange(source, index, total):
    buffer = jnp.zeros((total,) + source.shape[1:], source.dtype).at[index].set(source, mode="drop")
    return lax.all_to_all(buffer, "seq", split_axis=0, concat_axis=0, tiled=True)


def from_behind(block):
    n = lax.axis_size("seq")
    return lax.ppermute(block, "seq", [(i, i + 1) for i in range(n - 1)])


def rotate(block, r):
    n = lax.axis_size("seq")
    return lax.ppermute(block, "seq", [(i, (i + r) % n) for i in range(n)])


def padded_plan(me, queries, keys, values, dest_shard, dest_slot, ancestors):
    count = queries.shape[0]
    shards = lax.axis_size("seq")
    capacity = 2 * count // shards
    total = shards * capacity
    index = dest_shard * capacity + positions(dest_shard, shards)
    kv = exchange(jnp.concatenate([keys, values], axis=1), index, total)
    raw = exchange(queries, index, total)
    code = exchange(dest_slot + 1, index, total)
    slots = jnp.where(code > 0, code - 1, count)
    own_kv = jnp.zeros((count, kv.shape[1]), kv.dtype).at[slots].set(kv, mode="drop")
    prior_kv = from_behind(own_kv)
    return attend_padded(me, ancestors, code.reshape(1, total), raw, own_kv, prior_kv)


def after(block, *done):
    return lax.optimization_barrier((block, *done))[0]


def relay_plan(me, queries, keys, values, dest_shard, dest_slot, ancestors):
    count = queries.shape[0]
    shards = lax.axis_size("seq")
    unit = count // shards
    kv_blocks, index = pack_kv(me, dest_shard, dest_slot, keys, values, queries, shards, unit)
    got_kv = [kv_blocks[0]] + [rotate(kv_blocks[r], r) for r in range(1, shards)]
    q_blocks = pack_q(after(index, got_kv[1]), queries, shards, unit)
    own_k, beside_v, codes, crowd, q_blocks = relay(me, got_kv, q_blocks, unit)
    got_q = [q_blocks[0]] + [rotate(q_blocks[r], r) for r in range(1, shards)]
    prior_k = from_behind(after(own_k, got_q[1]))
    to_v = after(beside_v, got_q[7])
    prior_v = lax.ppermute(to_v, "seq", [(i, i + 2) for i in range(0, shards - 2, 2)])
    own_v = lax.ppermute(after(beside_v, got_q[4]), "seq", [(i, i ^ 1) for i in range(shards)])
    result = attend(me, ancestors, codes, got_q, own_k, own_v, prior_k, beside_v, prior_v, unit)
    args = (queries, keys, values, dest_shard, dest_slot, ancestors)
    return lax.cond(crowd[0, 0] > 0, lambda: padded_plan(me, *args), lambda: result)


def local(queries, keys, values, dest_shard, dest_slot, ancestors):
    shards = lax.axis_size("seq")
    me = lax.axis_index("seq").astype(jnp.int32).reshape(1)
    plan = relay_plan if queries.shape[0] == 8 * PIECE * shards and shards == 8 else padded_plan
    return plan(me, queries, keys, values, dest_shard, dest_slot, ancestors)


def solution(mesh):
    rows = P(("groups", "seq"))
    heads = P(("groups", "seq"), "head")
    return jax.shard_map(
        local,
        mesh=mesh,
        in_specs=(heads, heads, heads, rows, rows, P(("groups", "seq"), None)),
        out_specs=heads,
        check_vma=False,
    )
```

```python
import functools
import math

import jax
import jax.numpy as jnp
from jax import lax
from jax.experimental import pallas as pl
from jax.experimental.pallas import tpu as pltpu
from jax.sharding import PartitionSpec as P

HEAD_SIZE = 128
PIECE = 8
RADIX = 32
NO_DEST = 255.0
NEG = -1e30

VM = pl.BlockSpec(memory_space=pltpu.VMEM)
SM = pl.BlockSpec(memory_space=pltpu.SMEM)
HB = pl.BlockSpec(memory_space=pl.ANY)


def light():
    return pl.CostEstimate(flops=0, bytes_accessed=0, transcendentals=0)


def params(mebibytes=56):
    return pltpu.CompilerParams(vmem_limit_bytes=mebibytes * 1024 * 1024)


def iota(shape, axis):
    return lax.broadcasted_iota(jnp.int32, shape, axis)


def matmul(a, b):
    return jnp.dot(a, b, preferred_element_type=jnp.float32)


def matmul_nt(a, b):
    return lax.dot_general(a, b, (((1,), (1,)), ((), ())), preferred_element_type=jnp.float32)


def select_rows(index, start, rows, dtype=jnp.bfloat16):
    return (iota((rows, index.shape[1]), 0) + start == index).astype(dtype)


def strips(width, kv_width):
    return [(c, min(c + kv_width, width)) for c in range(0, width, kv_width)]


def pack_kv_kernel(shards, unit, me_ref, dest_ref, slot_ref, k_ref, v_ref, q_ref, *outs):
    blocks, index_ref = outs[:shards], outs[shards]
    count, kv = k_ref.shape
    dest = dest_ref[...].reshape(1, count)
    code = slot_ref[...].reshape(1, count) + 1
    onehot = (iota((shards, count), 0) == dest).astype(jnp.bfloat16)
    earlier = (iota((count, count), 0) < iota((count, count), 1)).astype(jnp.bfloat16)
    before = matmul(onehot, earlier)
    position = jnp.sum(before * onehot.astype(jnp.float32), axis=0, keepdims=True).astype(jnp.int32)
    base = position < unit
    index = jnp.where(base, ((dest - me_ref[0]) & (shards - 1)) * unit + position, -1)
    index_ref[...] = index
    v_index = jnp.where(base, (((dest ^ 1) - me_ref[0]) & (shards - 1)) * unit + position, -1)
    over_index = jnp.where(base, -1, position - unit)
    totals = matmul_nt(jnp.ones((PIECE, count), jnp.bfloat16), onehot)
    flags = jnp.where(iota((PIECE, shards), 0) == 2, (totals > unit + 0.5).astype(jnp.float32), 0.0)
    flags = jnp.concatenate([flags, jnp.zeros((PIECE, unit - shards), jnp.float32)], axis=1)
    over_dest = jnp.max(jnp.where(base, -1, dest))
    over_value = jnp.where(over_dest < 0, NO_DEST, over_dest.astype(jnp.float32))

    row = iota((PIECE, count), 0)
    codes = jnp.where(row == 0, code // RADIX, jnp.where(row == 1, code % RADIX, 0))
    codes = codes.astype(jnp.float32).astype(jnp.bfloat16)

    picked = select_rows(index, 0, count)
    k_rows = matmul(picked, k_ref[...]).astype(jnp.bfloat16)
    sent = matmul_nt(codes, picked)
    picked = select_rows(v_index, 0, count)
    v_rows = matmul(picked, v_ref[...]).astype(jnp.bfloat16)
    v_sent = matmul_nt(codes, picked)
    picked = select_rows(over_index, 0, unit)
    over_k = matmul(picked, k_ref[...])
    over_v = matmul(picked, v_ref[...])
    over_q = matmul(picked, q_ref[...])
    over_sent = matmul_nt(codes, picked)
    over_sent = jnp.where(iota((PIECE, unit), 0) == 2, over_value, over_sent)
    empty = jnp.zeros((PIECE, unit), jnp.float32)
    for r in range(shards):
        rows = slice(r * unit, (r + 1) * unit)
        blocks[r][0:unit, 0:kv] = k_rows[rows]
        blocks[r][0:unit, kv : 2 * kv] = v_rows[rows]
        piece = slice(r * PIECE, (r + 1) * PIECE)
        meta = jnp.concatenate([sent[:, rows], flags + v_sent[:, rows], over_sent, empty], axis=1)
        tail = [jnp.concatenate([over_k[piece], over_v[piece]], axis=1)]
        for start, stop in strips(over_q.shape[1], 2 * kv):
            tail.append(over_q[piece, start:stop])
        tail[-1] = jnp.concatenate([tail[-1], meta], axis=1)
        blocks[r][unit:, :] = jnp.concatenate(tail, axis=0).astype(jnp.bfloat16)


def pack_kv(me, dest, slot, keys, values, queries, shards, unit):
    kv_width = 2 * keys.shape[1]
    rows = unit + PIECE * (1 + len(strips(queries.shape[1], kv_width)))
    shapes = [jax.ShapeDtypeStruct((rows, kv_width), jnp.bfloat16)] * shards
    shapes += [jax.ShapeDtypeStruct((1, keys.shape[0]), jnp.int32)]
    outs = pl.pallas_call(
        functools.partial(pack_kv_kernel, shards, unit),
        out_shape=shapes,
        in_specs=[SM] + [VM] * 5,
        out_specs=[VM] * len(shapes),
        compiler_params=params(16),
        cost_estimate=light(),
        name="pack_kv",
    )(me, dest, slot, keys, values, queries)
    return outs[:shards], outs[shards]


def pack_q_kernel(unit, index_ref, q_ref, *blocks):
    for r, block in enumerate(blocks):
        picked = select_rows(index_ref[...], r * unit, unit)
        block[0:unit, :] = matmul(picked, q_ref[...]).astype(jnp.bfloat16)


def pack_q(index, queries, shards, unit):
    return pl.pallas_call(
        functools.partial(pack_q_kernel, unit),
        out_shape=[jax.ShapeDtypeStruct((unit + 2 * PIECE, queries.shape[1]), jnp.bfloat16)] * shards,
        in_specs=[VM, VM],
        out_specs=[VM] * shards,
        compiler_params=params(12),
        cost_estimate=light(),
        name="pack_q",
    )(index, queries)


def by_lane(parts, row):
    lane = iota((1, parts[0].shape[1]), 1) // PIECE
    total = jnp.zeros(lane.shape, jnp.float32)
    for r, part in enumerate(parts):
        total += jnp.where(lane == r, part[row : row + 1, :], 0.0)
    return total


def decode(high, low):
    return (high * RADIX + low).astype(jnp.int32)


def relay_kernel(shards, unit, me_ref, *refs):
    got = refs[:shards]
    blocks = refs[2 * shards : 3 * shards]
    tails, sems = refs[3 * shards :]
    kv_width = got[0].shape[1]
    width = tails.shape[2]
    cuts = strips(width, kv_width)
    meta_at = cuts[-1][1] - cuts[-1][0]
    ends = [ref[unit:, :].astype(jnp.float32) for ref in got]
    metas = [end[-PIECE:, meta_at:] for end in ends]

    over = [meta[:, 2 * unit : 3 * unit] for meta in metas]
    dest = by_lane(over, 2).astype(jnp.int32)
    part = iota(dest.shape, 1) % PIECE
    to = jnp.where(dest < shards, ((dest - me_ref[0]) & (shards - 1)) * PIECE + part, -1)
    behind = jnp.where(dest < shards - 1, ((dest + 1 - me_ref[0]) & (shards - 1)) * PIECE + part, -1)
    to, behind = select_rows(to, 0, shards * PIECE), select_rows(behind, 0, shards * PIECE)
    over_kv = jnp.concatenate([end[0:PIECE] for end in ends], axis=0).astype(jnp.bfloat16)
    row = iota((PIECE, unit), 0)
    codes = jnp.where(row == 0, by_lane(over, 0), jnp.where(row == 1, by_lane(over, 1), 0.0)).astype(jnp.bfloat16)
    meta = jnp.concatenate([matmul_nt(codes, to), matmul_nt(codes, behind)], axis=1)
    meta = jnp.concatenate([meta, jnp.zeros((PIECE, width - 2 * kv_width - 2 * unit), jnp.float32)], axis=1)
    to_kv, behind_kv = matmul(to, over_kv), matmul(behind, over_kv)
    to_q = []
    for i, (start, stop) in enumerate(cuts):
        strip = [end[(i + 1) * PIECE : (i + 2) * PIECE, 0 : stop - start] for end in ends]
        to_q.append(matmul(to, jnp.concatenate(strip, axis=0).astype(jnp.bfloat16)))
    to_q = jnp.concatenate(to_q, axis=1)
    copies = []
    for r in range(shards):
        piece = slice(r * PIECE, (r + 1) * PIECE)
        lower = jnp.concatenate([to_kv[piece], behind_kv[piece], meta], axis=1)
        tails[r] = jnp.concatenate([to_q[piece], lower], axis=0).astype(jnp.bfloat16)
        copies.append(pltpu.make_async_copy(tails.at[r], blocks[r].at[pl.ds(unit, 2 * PIECE), :], sems.at[r]))
        copies[-1].start()

    for c in copies:
        c.wait()


def place_kernel(shards, unit, *refs):
    got, (k_out, v_out, codes_ref, crowd_ref) = refs[:shards], refs[shards:]
    count, half = k_out.shape
    meta_at = got[0].shape[1] - 4 * unit
    metas = [ref[got[0].shape[0] - PIECE :, meta_at:].astype(jnp.float32) for ref in got]
    code = jnp.concatenate([decode(meta[0:1, 0:unit], meta[1:2, 0:unit]) for meta in metas], axis=1)
    codes_ref[...] = code
    rows = jnp.concatenate([ref[0:unit, 0:half] for ref in got], axis=0)
    k_out[...] = matmul(select_rows(code, 1, count), rows).astype(jnp.bfloat16)
    code = [decode(meta[0:1, unit : 2 * unit], meta[1:2, unit : 2 * unit]) for meta in metas]
    rows = jnp.concatenate([ref[0:unit, half:] for ref in got], axis=0)
    v_out[...] = matmul(select_rows(jnp.concatenate(code, axis=1), 1, count), rows).astype(jnp.bfloat16)
    by_dest = jnp.zeros((1, unit), jnp.float32)
    most = jnp.zeros((1, 1), jnp.float32)
    for meta in metas:
        flags = meta[2:3, unit : 2 * unit]
        by_dest += flags
        most = jnp.maximum(most, jnp.sum(flags, axis=1, keepdims=True))
    most = jnp.maximum(most, jnp.max(by_dest, axis=1, keepdims=True))
    crowd_ref[...] = jnp.broadcast_to((most > 1.5).astype(jnp.int32), crowd_ref.shape)


def place(got, unit):
    shards = len(got)
    count, half = shards * unit, got[0].shape[1] // 2
    shapes = [((count, half), jnp.bfloat16)] * 2 + [((1, count), jnp.int32), ((8, 128), jnp.int32)]
    return pl.pallas_call(
        functools.partial(place_kernel, shards, unit),
        out_shape=[jax.ShapeDtypeStruct(*shape) for shape in shapes],
        in_specs=[VM] * shards,
        out_specs=[VM] * 4,
        compiler_params=params(10),
        cost_estimate=light(),
        name="place",
    )(*got)


def relay(me, got, q_blocks, unit):
    shards = len(got)
    shape = q_blocks[0].shape
    return pl.pallas_call(
        functools.partial(relay_kernel, shards, unit),
        out_shape=[jax.ShapeDtypeStruct(shape, jnp.bfloat16)] * shards,
        in_specs=[SM] + [VM] * shards + [HB] * shards,
        out_specs=[HB] * shards,
        scratch_shapes=[
            pltpu.VMEM((shards, 2 * PIECE, shape[1]), jnp.bfloat16),
            pltpu.SemaphoreType.DMA((shards,)),
        ],
        input_output_aliases={1 + shards + r: r for r in range(shards)},
        compiler_params=params(10),
        cost_estimate=light(),
        name="relay",
    )(me, *got, *q_blocks)


def attend_core(shard, anc_ref, q_pl, kv_all, out_ref, groups, flush=None):
    count, width = out_ref.shape
    block_count = anc_ref.shape[0]
    size = count // block_count
    ratio = width // groups // HEAD_SIZE
    window = (block_count + 1) * size
    scale = math.log2(math.e) / math.sqrt(HEAD_SIZE)
    lane = iota((size, window), 1)
    causal = (lane >= block_count * size) & (lane - block_count * size <= iota((size, window), 0))

    def columns(g):
        return [(g * ratio + h) * HEAD_SIZE for h in range(ratio)]

    def scores_of(b, g):
        q = jnp.concatenate([q_pl[b * size : (b + 1) * size, c : c + HEAD_SIZE] for c in columns(g)], axis=0)
        return matmul_nt(q, kv_all[b * size : b * size + window, g * HEAD_SIZE : (g + 1) * HEAD_SIZE])

    def bias_of(b):
        key_block = lane // size + (shard - 1) * block_count + b
        seen = lane < 0
        for a in range(anc_ref.shape[1]):
            seen = seen | (key_block == anc_ref[b, a])
        return jnp.where((seen & (lane < block_count * size)) | causal, 0.0, NEG)

    def softmax(scores, bias):
        scores = (scores * scale).reshape(ratio, size, window) + bias[None]
        scores = scores.reshape(ratio * size, window)
        expo = jnp.exp2(scores - jnp.max(scores, axis=1, keepdims=True))
        return expo.astype(jnp.bfloat16), 1.0 / jnp.sum(expo, axis=1, keepdims=True)

    def finish(b, g, expo, inverse):
        column = (groups + g) * HEAD_SIZE
        v = kv_all[b * size : b * size + window, column : column + HEAD_SIZE]
        output = (matmul(expo, v) * inverse).astype(jnp.bfloat16)
        for h, c in enumerate(columns(g)):
            out_ref[b * size : (b + 1) * size, c : c + HEAD_SIZE] = output[h * size : (h + 1) * size]
        if flush is not None and g == groups - 1:
            flush(b)

    tiles = [(b, g) for b in range(block_count) for g in range(groups)]
    scores, held = scores_of(*tiles[0]), None
    for i, tile in enumerate(tiles):
        upcoming = scores_of(*tiles[i + 1]) if i + 1 < len(tiles) else None
        if held is not None:
            finish(*held)
        held = (*tile, *softmax(scores, bias_of(tile[0])))
        scores = upcoming
    finish(*held)


def attend_kernel(shards, unit, groups, me_ref, anc_ref, code_ref, *refs):
    got, (own_k, own_v, prior_k, beside_v, prior_v) = refs[:shards], refs[shards : shards + 5]
    out_hbm, raw, q_pl, kv_all, out_ref, sems, out_sems = refs[shards + 5 :]
    count, width = out_ref.shape
    half = own_k.shape[1]
    kv_width = 2 * half
    copies = []

    def fetch(source, target):
        copies.append(pltpu.make_async_copy(source, target, sems.at[len(copies)]))
        copies[-1].start()

    fetch(prior_k, kv_all.at[pl.ds(0, count), pl.ds(0, half)])
    fetch(own_k, kv_all.at[pl.ds(count, count), pl.ds(0, half)])
    fetch(own_v, kv_all.at[pl.ds(count, count), pl.ds(half, half)])
    odd = me_ref[0] & 1

    @pl.when(odd == 1)
    def _():
        kv_all[0:count, half:] = beside_v[...]

    @pl.when(odd == 0)
    def _():
        kv_all[0:count, half:] = prior_v[...]

    for r, ref in enumerate(got):
        raw[r * unit : (r + 1) * unit, :] = ref[0:unit, :]
    for c in copies:
        c.wait()
    ends = [ref[unit:, :].astype(jnp.float32) for ref in got]
    metas = [end[PIECE:, 2 * kv_width :] for end in ends]
    own = [meta[:, 0:unit] for meta in metas]
    behind = [meta[:, unit : 2 * unit] for meta in metas]
    own = decode(by_lane(own, 0), by_lane(own, 1))
    behind = decode(by_lane(behind, 0), by_lane(behind, 1))
    raw[count:, :] = jnp.concatenate([end[0:PIECE] for end in ends], axis=0).astype(jnp.bfloat16)
    onehot = select_rows(jnp.concatenate([code_ref[...], own], axis=1), 1, count)
    q_pl[...] = matmul(onehot, raw[...]).astype(jnp.bfloat16)
    for j, (code, start) in enumerate(((behind, kv_width), (own, 0))):
        rows = jnp.concatenate([end[PIECE:, start : start + kv_width] for end in ends], axis=0)
        rows = matmul(select_rows(code, 1, count), rows.astype(jnp.bfloat16))
        kv_all[j * count : (j + 1) * count, :] += rows.astype(jnp.bfloat16)
    written = []

    def flush(b):
        rows = pl.ds(b * (count // anc_ref.shape[0]), count // anc_ref.shape[0])
        written.append(pltpu.make_async_copy(out_ref.at[rows, :], out_hbm.at[rows, :], out_sems.at[b]))
        written[-1].start()

    attend_core(me_ref[0], anc_ref, q_pl, kv_all, out_ref, groups, flush)
    for c in written:
        c.wait()


def attend(me, ancestors, codes, got, own_k, own_v, prior_k, beside_v, prior_v, unit):
    shards = len(got)
    count, width = shards * unit, got[0].shape[1]
    groups = own_k.shape[1] // HEAD_SIZE
    return pl.pallas_call(
        functools.partial(attend_kernel, shards, unit, groups),
        out_shape=jax.ShapeDtypeStruct((count, width), jnp.bfloat16),
        in_specs=[SM, SM, VM] + [VM] * shards + [HB] * 3 + [VM, VM],
        out_specs=HB,
        scratch_shapes=[
            pltpu.VMEM((count + shards * PIECE, width), jnp.bfloat16),
            pltpu.VMEM((count, width), jnp.bfloat16),
            pltpu.VMEM((2 * count, 2 * own_k.shape[1]), jnp.bfloat16),
            pltpu.VMEM((count, width), jnp.bfloat16),
            pltpu.SemaphoreType.DMA((3,)),
            pltpu.SemaphoreType.DMA((ancestors.shape[0],)),
        ],
        compiler_params=params(28),
        cost_estimate=light(),
        name="attend",
    )(me, ancestors, codes, *got, own_k, own_v, prior_k, beside_v, prior_v)


def attend_padded_kernel(me_ref, anc_ref, code_ref, raw_ref, own_kv, prior_kv, out_ref, q_pl, kv_all):
    count = out_ref.shape[0]
    kv_all[0:count, :] = prior_kv[...]
    kv_all[count : 2 * count, :] = own_kv[...]
    q_pl[...] = matmul(select_rows(code_ref[...], 1, count), raw_ref[...]).astype(jnp.bfloat16)
    attend_core(me_ref[0], anc_ref, q_pl, kv_all, out_ref, kv_all.shape[1] // (2 * HEAD_SIZE))


def attend_padded(me, ancestors, codes, raw, own_kv, prior_kv):
    count, width = own_kv.shape[0], raw.shape[1]
    return pl.pallas_call(
        attend_padded_kernel,
        out_shape=jax.ShapeDtypeStruct((count, width), jnp.bfloat16),
        in_specs=[SM, SM] + [VM] * 4,
        out_specs=VM,
        scratch_shapes=[
            pltpu.VMEM((count, width), jnp.bfloat16),
            pltpu.VMEM((2 * count, own_kv.shape[1]), jnp.bfloat16),
        ],
        compiler_params=params(),
        name="attend_padded",
    )(me, ancestors, codes, raw, own_kv, prior_kv)


def positions(dest_shard, shards):
    onehot = (dest_shard[:, None] == jnp.arange(shards, dtype=jnp.int32)[None, :]).astype(jnp.int32)
    before = jnp.cumsum(onehot, axis=0) - onehot
    return jnp.sum(before * onehot, axis=1)


def exchange(source, index, total):
    buffer = jnp.zeros((total,) + source.shape[1:], source.dtype).at[index].set(source, mode="drop")
    return lax.all_to_all(buffer, "seq", split_axis=0, concat_axis=0, tiled=True)


def from_behind(block):
    n = lax.axis_size("seq")
    return lax.ppermute(block, "seq", [(i, i + 1) for i in range(n - 1)])


def rotate(block, r):
    n = lax.axis_size("seq")
    return lax.ppermute(block, "seq", [(i, (i + r) % n) for i in range(n)])


def padded_plan(me, queries, keys, values, dest_shard, dest_slot, ancestors):
    count = queries.shape[0]
    shards = lax.axis_size("seq")
    capacity = 2 * count // shards
    total = shards * capacity
    index = dest_shard * capacity + positions(dest_shard, shards)
    kv = exchange(jnp.concatenate([keys, values], axis=1), index, total)
    raw = exchange(queries, index, total)
    code = exchange(dest_slot + 1, index, total)
    slots = jnp.where(code > 0, code - 1, count)
    own_kv = jnp.zeros((count, kv.shape[1]), kv.dtype).at[slots].set(kv, mode="drop")
    prior_kv = from_behind(own_kv)
    return attend_padded(me, ancestors, code.reshape(1, total), raw, own_kv, prior_kv)


def after(block, *done):
    return lax.optimization_barrier((block, *done))[0]


def relay_plan(me, queries, keys, values, dest_shard, dest_slot, ancestors):
    count = queries.shape[0]
    shards = lax.axis_size("seq")
    unit = count // shards
    kv_blocks, index = pack_kv(me, dest_shard, dest_slot, keys, values, queries, shards, unit)
    got_kv = [kv_blocks[0]] + [rotate(kv_blocks[r], r) for r in range(1, shards)]
    q_blocks = pack_q(after(index, got_kv[1]), queries, shards, unit)
    q_blocks = relay(me, got_kv, q_blocks, unit)
    got_q = [q_blocks[0]] + [rotate(q_blocks[r], r) for r in range(1, shards)]
    own_k, beside_v, codes, crowd = place([after(got_kv[0], got_q[4]), *got_kv[1:]], unit)
    prior_k = from_behind(after(own_k, got_q[1]))
    to_v = after(beside_v, got_q[7])
    prior_v = lax.ppermute(to_v, "seq", [(i, i + 2) for i in range(0, shards - 2, 2)])
    own_v = lax.ppermute(after(beside_v, got_q[4]), "seq", [(i, i ^ 1) for i in range(shards)])
    result = attend(me, ancestors, codes, got_q, own_k, own_v, prior_k, beside_v, prior_v, unit)
    args = (queries, keys, values, dest_shard, dest_slot, ancestors)
    return lax.cond(crowd[0, 0] > 0, lambda: padded_plan(me, *args), lambda: result)


def local(queries, keys, values, dest_shard, dest_slot, ancestors):
    shards = lax.axis_size("seq")
    me = lax.axis_index("seq").astype(jnp.int32).reshape(1)
    plan = relay_plan if queries.shape[0] == 8 * PIECE * shards and shards == 8 else padded_plan
    return plan(me, queries, keys, values, dest_shard, dest_slot, ancestors)


def solution(mesh):
    rows = P(("groups", "seq"))
    heads = P(("groups", "seq"), "head")
    return jax.shard_map(
        local,
        mesh=mesh,
        in_specs=(heads, heads, heads, rows, rows, P(("groups", "seq"), None)),
        out_specs=heads,
        check_vma=False,
    )
```
